32 devices in a mesh: dp: 16 (over z, y, x), seq: 2 (over core).
Axes of the slice: x: 2, y: 2, z: 4, core: 2. Of those that a mesh axis runs over, the one named last changes fastest.
Arguments:
- tokens: bfloat16 [64, 256, 384], P('dp', 'seq'), may hold values from -6 to 6
- cotangent: bfloat16 [64, 256, 384], P('dp', 'seq'), may hold values from -6 to 6
- cond: bfloat16 [32, 384], P('dp'), may hold values from -6 to 6
- group_ids: int32 [64], P('dp'), may hold values from 0 to 31
- image_counts: int32 [16], P('dp'), may hold values from 1 to 4, as said below
- patch_mask: int32 [64, 256], P('dp'), may hold values 0 or 1
- qkv_weight: bfloat16 [384, 1152], replicated, may hold values from -0.3125 to 0.3125
- qv_bias: bfloat16 [2, 384], replicated, may hold values from -1.796875 to 1.796875
- out_weight: bfloat16 [384, 384], replicated, may hold values from -1.75 to 1.75
- out_bias: bfloat16 [384], replicated, may hold values from -1.796875 to 1.796875
- up_weight: bfloat16 [384, 1536], replicated, may hold values from -0.3125 to 0.3125
- up_bias: bfloat16 [1536], replicated, may hold values from -1.796875 to 1.796875
- down_weight: bfloat16 [1536, 384], replicated, may hold values from -0.15625 to 0.15625
- down_bias: bfloat16 [384], replicated, may hold values from -1.796875 to 1.796875
- ada_weight: bfloat16 [384, 2304], replicated, may hold values from -0.3125 to 0.3125
- ada_bias: bfloat16 [2304], replicated, may hold values from -1.796875 to 1.796875
Outputs:
- output: bfloat16 [64, 256, 384], P('dp', 'seq')
- grad_tokens: bfloat16 [64, 256, 384], P('dp', 'seq')
- grad_cond: float32 [32, 384], P('dp', 'seq')
- grad_qkv_weight: float32 [384, 1152], P('dp', 'seq')
- grad_qv_bias: float32 [2, 384], replicated
- grad_out_weight: float32 [384, 384], P('dp', 'seq')
- grad_out_bias: float32 [384], replicated
- grad_up_weight: float32 [384, 1536], P('dp', 'seq')
- grad_up_bias: float32 [1536], replicated
- grad_down_weight: float32 [1536, 384], P('dp', 'seq')
- grad_down_bias: float32 [384], replicated
- grad_ada_weight: float32 [384, 2304], P('dp', 'seq')
- grad_ada_bias: float32 [2304], replicated
The draws below stay inside these ranges and needn't reach their ends.
Inputs may be any that keep to these rules, and one draw needn't show every extreme that they name: `image_counts`: some index of dp holds 4 images and another holds one.
All inputs are finite; a program needn't handle non-finite values. No bound on the sum of `patch_mask` on one device may be relied on, other than what follows from the above.
Results may differ from the reference program's by a relative error of at most 0.012.
The reference program's roundings to bfloat16 on the way count: a program that leaves them out, or rounds other values in their place, can miss the bound.
Values may be sent and summed in bfloat16 or wider, within the bound.
No kernel may reach another device: no remote copies, remote signals or barrier semaphores. Data moves between devices by JAX's collectives and lax.ppermute only.
A program may use at most 320 MiB of HBM per device.

```python
import math
import jax
import jax.numpy as jnp
from jax import lax

D = 384
HEADS = 6
HEAD_DIM = 64
FF = 1536
L = 256
SLOTS = 4
IMAGES = 64
GROUPS = 32
MOD = 2304


def draw_image_counts(key, part):
    rank_count = IMAGES // SLOTS
    counts = jax.random.randint(key, (rank_count,), 1, SLOTS + 1)
    full_at = jax.random.randint(jax.random.fold_in(key, 11), (), 0, rank_count)
    offset = jax.random.randint(jax.random.fold_in(key, 12), (), 1, rank_count)
    single_at = (full_at + offset) % rank_count
    counts = counts.at[full_at].set(SLOTS)
    counts = counts.at[single_at].set(1)
    return counts.astype(jnp.int32)


def plant(drawn, own_key, least, top_value):
    longest = drawn.shape.index(max(drawn.shape))
    spots = []
    for shift in (0, 1):
        where = [jax.random.randint(jax.random.fold_in(own_key, axis), (), 0, length) for axis, length in enumerate(drawn.shape)]
        where[longest] = (where[longest] + shift) % drawn.shape[longest]
        spots.append(tuple(where))
    return drawn.at[spots[0]].set(least).at[spots[1]].set(top_value)


def shard_levels(stream_key, dims, shards, least, top_value):
    factor_of = 1.0
    for position, blocks in shards:
        heights = jax.random.uniform(jax.random.fold_in(jax.random.fold_in(stream_key, 6), position), (blocks,), jnp.float32, least / len(shards), top_value / len(shards))
        factor_of = factor_of * jnp.repeat(jnp.exp(heights), dims[position] // blocks).reshape((-1,) + (1,) * (len(dims) - 1 - position))
    return factor_of


def normal_values(rng, extent, deviation, bound, cuts=(), kind=jnp.bfloat16):
    level = shard_levels(rng, extent, cuts, -0.22, 0.18) if cuts else 1.0
    array = jax.random.normal(rng, extent, jnp.float32) * deviation * level
    return jnp.minimum(jnp.maximum(array, -bound), bound).astype(kind)


def setup_inputs(seed: int = 0) -> dict:
    streams_of = jax.random.split(jax.random.key(seed), 17)
    tokens = normal_values(streams_of[0], (IMAGES, L, D), 1.0, 6.0, ((0, 16), (1, 2)))
    cotangent = normal_values(streams_of[1], (IMAGES, L, D), 1.0, 6.0, ((0, 16), (1, 2)))
    cond = normal_values(streams_of[2], (GROUPS, D), 1.0, 6.0, ((0, 16),))
    group_ids = plant(jax.random.randint(streams_of[3], (IMAGES,), 0, GROUPS), jax.random.fold_in(streams_of[3], 1), 0, GROUPS - 1).astype(jnp.int32)
    image_counts = draw_image_counts(jax.random.fold_in(streams_of[16], 71), 0)
    patch_mask = plant((jax.random.randint(streams_of[5], (IMAGES, L), 0, 8) < 7).astype(jnp.int32), jax.random.fold_in(streams_of[5], 1), 0, 1)
    qkv_weight = normal_values(streams_of[6], (D, 3 * D), D ** -0.5, 0.3125)
    qv_bias = normal_values(streams_of[7], (2, D), 0.3, 1.796875)
    out_weight = normal_values(streams_of[8], (D, D), (D // 32) ** -0.5, 1.75)
    out_bias = normal_values(streams_of[9], (D,), 0.3, 1.796875)
    up_weight = normal_values(streams_of[10], (D, FF), D ** -0.5, 0.3125)
    up_bias = normal_values(streams_of[11], (FF,), 0.3, 1.796875)
    down_weight = normal_values(streams_of[12], (FF, D), FF ** -0.5, 0.15625)
    down_bias = normal_values(streams_of[13], (D,), 0.3, 1.796875)
    ada_weight = normal_values(streams_of[14], (D, MOD), D ** -0.5, 0.3125)
    ada_bias = normal_values(streams_of[15], (MOD,), 0.3, 1.796875)
    return dict(tokens=tokens, cotangent=cotangent, cond=cond, group_ids=group_ids, image_counts=image_counts, patch_mask=patch_mask, qkv_weight=qkv_weight, qv_bias=qv_bias, out_weight=out_weight, out_bias=out_bias, up_weight=up_weight, up_bias=up_bias, down_weight=down_weight, down_bias=down_bias, ada_weight=ada_weight, ada_bias=ada_bias)


@jax.custom_vjp
def low(v):
    return lax.optimization_barrier(v.astype(jnp.bfloat16)).astype(jnp.float32)

@jax.custom_vjp
def low_back(v):
    return v

def low_keep(v):
    return (low(v), None)

def low_pass(kept, grad):
    return (grad,)

def back_keep(v):
    return (v, None)

def back_low(kept, grad):
    return (low(grad),)
low.defvjp(low_keep, low_pass)
low_back.defvjp(back_keep, back_low)

def layer_norm(values):
    center = values - lax.optimization_barrier(jnp.mean(values, axis=-1, keepdims=True))
    spread = lax.optimization_barrier(jnp.mean(center * center, axis=-1, keepdims=True))
    return center * lax.rsqrt(spread + 1e-06)

def forward(inputs, cond, qkv_weight, qv_bias, out_weight, out_bias, up_weight, up_bias, down_weight, down_bias, ada_weight, ada_bias, group_ids, valid):
    highest = lax.Precision.HIGHEST
    batch_size = inputs.shape[0]
    silu_cond = low(jax.nn.silu(cond))
    modulation = low(jnp.dot(silu_cond, ada_weight, precision=highest) + ada_bias)
    rows_mod = modulation[group_ids]
    pieces = [rows_mod[:, None, index * D:(index + 1) * D] for index in range(6)]
    shift_one, scale_one, gate_one, shift_two, scale_two, gate_two = pieces
    normed_one = low(layer_norm(inputs) * (1.0 + scale_one) + shift_one)
    proj_bias = jnp.concatenate([qv_bias[0], jnp.zeros((D,), jnp.float32), qv_bias[1]])
    projected = jnp.einsum('bld,de->ble', normed_one, qkv_weight, precision=highest) + proj_bias
    projected = low_back(low(projected)).reshape(batch_size, L, 3, HEADS, HEAD_DIM)
    queries = projected[:, :, 0]
    keys_all = projected[:, :, 1]
    values_all = projected[:, :, 2]
    raw_scores = low_back(jnp.einsum('bqhd,bkhd->bhqk', queries, keys_all, precision=highest) * HEAD_DIM ** (-0.5))
    scores = raw_scores + ((valid - 1.0) * 30000.0)[:, None, None, :]
    probs = jax.nn.softmax(scores, axis=-1)
    attended = jnp.einsum('bhqk,bkhd->bqhd', low(probs), values_all, precision=highest)
    attended = low_back(low(attended)).reshape(batch_size, L, D)
    attn_out = low_back(jnp.einsum('bld,de->ble', attended, out_weight, precision=highest) + out_bias)
    valid_col = valid[:, :, None]
    middle = inputs + valid_col * gate_one * attn_out
    normed_two = low(layer_norm(middle) * (1.0 + scale_two) + shift_two)
    pre_act = low_back(jnp.einsum('bld,df->blf', normed_two, up_weight, precision=highest) + up_bias)
    hidden = low(jax.nn.gelu(pre_act, approximate=True))
    ffn_out = low_back(jnp.einsum('blf,fd->bld', hidden, down_weight, precision=highest) + down_bias)
    return middle + valid_col * gate_two * ffn_out

def reference(tokens, cotangent, cond, group_ids, image_counts, patch_mask, qkv_weight, qv_bias, out_weight, out_bias, up_weight, up_bias, down_weight, down_bias, ada_weight, ada_bias):
    params = tuple((item.astype(jnp.float32) for item in (cond, qkv_weight, qv_bias, out_weight, out_bias, up_weight, up_bias, down_weight, down_bias, ada_weight, ada_bias)))
    image_index = jnp.arange(IMAGES, dtype=jnp.int32)
    live_slots = (image_index % SLOTS < image_counts[image_index // SLOTS]).astype(jnp.float32)
    valid = patch_mask.astype(jnp.float32) * live_slots[:, None]
    block_size = math.gcd(IMAGES, 16)
    block_count = IMAGES // block_size
    blocks_in = (tokens.reshape(block_count, block_size, L, D), cotangent.reshape(block_count, block_size, L, D), group_ids.reshape(block_count, block_size), valid.reshape(block_count, block_size, L))

    def one_block(running, block_data):
        block_tokens, block_cot, block_groups, block_valid = block_data

        def apply_layer(inputs, *weights):
            return forward(inputs, *weights, block_groups, block_valid)
        result, pullback = jax.vjp(apply_layer, block_tokens.astype(jnp.float32), *params)
        gradients = pullback(block_cot.astype(jnp.float32))
        running = tuple((total + part for total, part in zip(running, gradients[1:])))
        return (running, (result.astype(jnp.bfloat16), gradients[0].astype(jnp.bfloat16)))
    start = tuple((jnp.zeros(item.shape, jnp.float32) for item in params))
    sums, (results, input_grads) = lax.scan(one_block, start, blocks_in)
    return (results.reshape(IMAGES, L, D), input_grads.reshape(IMAGES, L, D), sums[0], sums[1], sums[2], sums[3], sums[4], sums[5], sums[6], sums[7], sums[8], sums[9], sums[10])
```

```python
from functools import partial

import jax
import jax.numpy as jnp
from jax import lax
from jax.experimental import pallas as pl
from jax.experimental.pallas import tpu as pltpu
from jax.sharding import PartitionSpec as P

HEADS = 6
HEAD_DIM = 64
PAIR = 2 * HEAD_DIM
CORE_SWAP = ((0, 1), (1, 0))
CHUNK = 256
LANES = 128
GROUPS_PER_RANK = 2
GENERAL = False
F32 = jnp.float32
LOW = jnp.bfloat16


def nn(left, right):
    return lax.dot_general(left, right, (((1,), (0,)), ((), ())), preferred_element_type=F32)


def nt(left, right):
    return lax.dot_general(left, right, (((1,), (1,)), ((), ())), preferred_element_type=F32)


def tn(left, right):
    return lax.dot_general(left, right, (((0,), (0,)), ((), ())), preferred_element_type=F32)


def normalize(values):
    center = values - jnp.mean(values, axis=-1, keepdims=True)
    spread = jnp.mean(center * center, axis=-1, keepdims=True)
    inverse = lax.rsqrt(spread + 1e-06)
    return center * inverse, inverse


def norm_back(grad, normed, inverse):
    return inverse * (
        grad
        - jnp.mean(grad, axis=-1, keepdims=True)
        - normed * jnp.mean(grad * normed, axis=-1, keepdims=True)
    )


def column_sum(values):
    return jnp.sum(values, axis=0, keepdims=True)


def head_masks(rows):
    lane = lax.broadcasted_iota(jnp.int32, (rows, PAIR), 1)
    return lane < HEAD_DIM, lane >= HEAD_DIM


def masked(values, mask):
    return jnp.where(mask, values, jnp.zeros_like(values))


def softmax_rows(queries, keys, penalty):
    scores = nt(queries, keys) + penalty
    exps = jnp.exp(scores - jnp.max(scores, axis=-1, keepdims=True))
    return exps / jnp.sum(exps, axis=-1, keepdims=True)


def fetch(pairs, sems):
    copies = []
    for index, (source, target) in enumerate(pairs):
        copy = pltpu.make_async_copy(source, target, sems.at[index])
        copy.start()
        copies.append(copy)
    return copies


def own_images(near_ref, far_ref, target_ref, first_image):
    half_len = near_ref.shape[1]
    pairs = []
    for image in range(target_ref.shape[0]):
        slot = first_image + image
        pairs.append((near_ref.at[slot], target_ref.at[image, pl.ds(0, half_len)]))
        pairs.append((far_ref.at[slot], target_ref.at[image, pl.ds(half_len, half_len)]))
    return pairs


def own_marks(mask_ref, counts_ref, core, image, image_count, half_len):
    slot = core * image_count + image
    live = jnp.where(slot < counts_ref[0], 1.0, 0.0)
    marks = mask_ref[pl.ds(slot, 1), :].astype(F32) * live
    low_marks, high_marks = marks[:, :half_len], marks[:, half_len:]
    return jnp.concatenate(
        [
            jnp.where(core == 0, low_marks, high_marks),
            jnp.where(core == 0, high_marks, low_marks),
        ],
        axis=1,
    )


def as_row(ref):
    return ref[...].astype(F32).reshape(1, ref.shape[0])


def forward_kernel(
    lead_rows,
    tokens_hbm,
    tokens_far_hbm,
    cot_hbm,
    cot_far_hbm,
    cond_hbm,
    ids_hbm,
    counts_hbm,
    mask_hbm,
    qkv_w_hbm,
    qv_b_hbm,
    out_w_hbm,
    out_b_hbm,
    up_w_hbm,
    up_b_hbm,
    down_w_hbm,
    down_b_hbm,
    ada_w_hbm,
    ada_b_hbm,
    output_hbm,
    qkv_hbm,
    grad_att_hbm,
    grad_mid_hbm,
    mod_hbm,
    images_hbm,
    penalty_hbm,
    lead_hbm,
    keep_ref,
    send_ref,
    small_ref,
    tokens_ref,
    cot_ref,
    cond_ref,
    mask_ref,
    qkv_w_ref,
    qv_b_ref,
    out_w_ref,
    out_b_ref,
    up_w_ref,
    up_b_ref,
    down_w_ref,
    down_b_ref,
    ada_w_ref,
    ada_b_ref,
    ids_ref,
    counts_ref,
    output_ref,
    qkv_ref,
    grad_att_ref,
    grad_mid_ref,
    mod_ref,
    penalty_ref,
    valid_ref,
    att_ref,
    mid_ref,
    attn_ref,
    h2_ref,
    gffn_ref,
    act_ref,
    gpre_ref,
    ffn_ref,
    gh2_ref,
    turned_ref,
    lead_ref,
    in_sems,
    out_sems,
):
    core = lax.axis_index("seq")
    image_count, length, width = tokens_ref.shape
    half_len = length // 2
    half = width // 2
    ff_width = up_w_ref.shape[1]
    first_image = core * image_count
    copies = fetch(
        [
            (ids_hbm, ids_ref),
            (counts_hbm, counts_ref),
            (cond_hbm, cond_ref),
            (ada_w_hbm, ada_w_ref),
            (ada_b_hbm, ada_b_ref),
            (mask_hbm, mask_ref),
        ]
        + own_images(tokens_hbm, tokens_far_hbm, tokens_ref, first_image)
        + [
            (qkv_w_hbm, qkv_w_ref),
            (qv_b_hbm, qv_b_ref),
            (out_w_hbm, out_w_ref),
            (out_b_hbm, out_b_ref),
        ]
        + own_images(cot_hbm, cot_far_hbm, cot_ref, first_image)
        + [
            (up_w_hbm, up_w_ref),
            (up_b_hbm, up_b_ref),
            (down_w_hbm, down_w_ref),
            (down_b_hbm, down_b_ref),
        ],
        in_sems,
    )
    token_copies = 6 + 2 * image_count
    for copy in copies[:5]:
        copy.wait()
    block_count, block_rows = cond_ref.shape[:2]
    cond = cond_ref[...].reshape(block_count * block_rows, width).astype(F32)
    silu = (cond / (1.0 + jnp.exp(-cond))).astype(LOW)
    row = lax.broadcasted_iota(jnp.int32, (8, block_count * block_rows), 0)
    column = lax.broadcasted_iota(jnp.int32, (8, block_count * block_rows), 1)
    hot = jnp.zeros((8, block_count * block_rows), F32)
    for image in range(image_count):
        group = ids_ref[first_image + image]
        place = block_rows * (group // GROUPS_PER_RANK) + group % GROUPS_PER_RANK
        hot = jnp.where((row == image) & (column == place), 1.0, hot)
    image_silu = nn(hot.astype(LOW), silu).astype(LOW)
    mod_ref[...] = (nn(image_silu, ada_w_ref[...]) + as_row(ada_b_ref)).astype(LOW)
    if lead_rows:
        turned_ref[...] = silu.astype(F32).T
        start = pl.multiple_of(lax.axis_index("dp") * lead_rows, 8)
        lead_ref[...] = turned_ref[pl.ds(start, lead_rows), :].astype(LOW)
    else:
        lead_ref[...] = jnp.zeros_like(lead_ref)
    results = fetch([(mod_ref, mod_hbm), (lead_ref, lead_hbm)], out_sems)
    for copy in copies[5 : token_copies + 2]:
        copy.wait()

    def part(image, which):
        return mod_ref[image : image + 1, which * width : (which + 1) * width].astype(F32)

    def rows_of(image):
        return slice(image * length, (image + 1) * length)

    small_ref[...] = jnp.zeros_like(small_ref)
    qkv_bias = jnp.concatenate(
        [qv_b_ref[0:1, :], jnp.zeros((1, width), LOW), qv_b_ref[1:2, :]], axis=1
    ).astype(F32)
    for image in range(image_count):
        rows = rows_of(image)
        marks = own_marks(mask_ref, counts_ref, core, image, image_count, half_len)
        penalty_ref[image : image + 1, :] = (marks - 1.0) * 30000.0
        valid_ref[rows, :] = jnp.broadcast_to(marks, (LANES, length)).T
        normed, _ = normalize(tokens_ref[image].astype(F32))
        h1 = (normed * (1.0 + part(image, 1)) + part(image, 0)).astype(LOW)
        qkv_ref[rows, :] = (nn(h1, qkv_w_ref[...]) + qkv_bias).astype(LOW)

    results += fetch(
        [(qkv_ref, qkv_hbm), (tokens_ref, images_hbm), (penalty_ref, penalty_hbm)],
        out_sems.at[pl.ds(2, 3)],
    )

    def valid_of(image):
        column = valid_ref[rows_of(image), :]
        return jnp.concatenate([column] * (width // LANES), axis=1)

    first, second = head_masks(length)

    def pair_step(step, carry):
        image = step // (HEADS // 2)
        pair = step % (HEADS // 2)
        rows = pl.ds(pl.multiple_of(image * length, length), length)

        def lanes(which):
            return pl.ds(pl.multiple_of(which * width + pair * PAIR, PAIR), PAIR)

        queries = qkv_ref[rows, lanes(0)] * jnp.asarray(HEAD_DIM**-0.5, LOW)
        keys = qkv_ref[rows, lanes(1)]
        values = qkv_ref[rows, lanes(2)]
        penalty = penalty_ref[pl.ds(image, 1), :]
        total = jnp.zeros((length, PAIR), F32)
        for mask in (first, second):
            probs = softmax_rows(masked(queries, mask), keys, penalty).astype(LOW)
            total = total + nn(probs, masked(values, mask))
        att_ref[rows, lanes(0)] = total.astype(LOW)
        return carry

    lax.fori_loop(0, image_count * (HEADS // 2), pair_step, 0)

    for copy in copies[token_copies + 2 :]:
        copy.wait()
    down_bias_grad = jnp.zeros((1, width), F32)
    for image in range(image_count):
        rows = rows_of(image)
        valid = valid_of(image)
        attn = nn(att_ref[rows, :], out_w_ref[...]) + as_row(out_b_ref)
        attn_ref[rows, :] = attn
        middle = tokens_ref[image].astype(F32) + valid * part(image, 2) * attn
        mid_ref[rows, :] = middle
        normed, _ = normalize(middle)
        h2_ref[rows, :] = (normed * (1.0 + part(image, 4)) + part(image, 3)).astype(LOW)
        grad_ffn = (valid * part(image, 5) * cot_ref[image].astype(F32)).astype(LOW)
        gffn_ref[rows, :] = grad_ffn
        down_bias_grad = down_bias_grad + column_sum(grad_ffn.astype(F32))
        ffn_ref[rows, :] = jnp.zeros((length, width), F32)
        gh2_ref[rows, :] = jnp.zeros((length, width), F32)
    small_ref[13:14, :] = down_bias_grad
    for image in range(image_count):
        group = ids_ref[first_image + image].astype(F32)
        small_ref[14 + image : 15 + image, :] = jnp.full((1, width), group, F32)

    first_half = gffn_ref[:, :half]
    second_half = gffn_ref[:, half:]
    gffn_keep = jnp.where(core == 0, first_half, second_half)
    gffn_send = jnp.where(core == 0, second_half, first_half)
    side_chunks = ff_width // CHUNK // 2
    up_bias = as_row(up_b_ref)

    def ffn_chunk(chunk):
        columns = slice(chunk * CHUNK, (chunk + 1) * CHUNK)
        up_w = up_w_ref[:, columns]
        down_w = down_w_ref[columns, :]
        up_b = up_bias[:, columns]
        for image in range(image_count):
            rows = rows_of(image)
            pre = nn(h2_ref[rows, :], up_w) + up_b
            square = pre * pre
            inner = jnp.tanh(0.7978845608028654 * (pre + 0.044715 * (square * pre)))
            cdf = 0.5 * (1.0 + inner)
            act = (pre * cdf).astype(LOW)
            slope = cdf + 0.5 * pre * (1.0 - inner * inner) * (
                0.7978845608028654 * (1.0 + 3.0 * 0.044715 * square)
            )
            grad_pre = (nt(gffn_ref[rows, :], down_w) * slope).astype(LOW)
            act_ref[rows, :] = act
            gpre_ref[rows, :] = grad_pre
            ffn_ref[rows, :] += nn(act, down_w)
            gh2_ref[rows, :] += nt(grad_pre, up_w)
        bias = column_sum(gpre_ref[...].astype(F32))
        for tile in range(CHUNK // LANES):
            start = chunk * CHUNK + tile * LANES
            small_ref[9 + start // width : 10 + start // width, start % width : start % width + LANES] = (
                bias[:, tile * LANES : (tile + 1) * LANES]
            )
        return (
            tn(h2_ref[...], gpre_ref[...]),
            tn(act_ref[...], gffn_keep),
            tn(act_ref[...], gffn_send),
        )

    for step in range(side_chunks):
        up_low, keep_low, send_low = ffn_chunk(step)
        up_high, keep_high, send_high = ffn_chunk(step + side_chunks)
        up_keep = jnp.where(core == 0, up_low, up_high)
        up_send = jnp.where(core == 0, up_high, up_low).astype(LOW)
        for tile in range(CHUNK // LANES):
            start = step * CHUNK + tile * LANES
            rows = slice(start // width * width, (start // width + 1) * width)
            columns = slice(start % width, start % width + LANES)
            keep_ref[rows, columns] = up_keep[:, tile * LANES : (tile + 1) * LANES]
            send_ref[rows, columns] = up_send[:, tile * LANES : (tile + 1) * LANES]
        rows = slice(2 * width + step * CHUNK, 2 * width + (step + 1) * CHUNK)
        keep_ref[rows, :] = jnp.concatenate([keep_low, keep_high], axis=1)
        send_ref[rows, :] = jnp.concatenate([send_low, send_high], axis=1).astype(LOW)

    out_bias_grad = jnp.zeros((1, width), F32)
    for image in range(image_count):
        rows = rows_of(image)
        valid = valid_of(image)
        upstream = cot_ref[image].astype(F32)
        middle = mid_ref[rows, :]
        ffn = ffn_ref[rows, :] + as_row(down_b_ref)
        result = (middle + valid * part(image, 5) * ffn).astype(LOW)
        output_ref[image] = result
        start = keep_ref.shape[0] + 16 + image * half_len
        send_ref[start : start + half_len, :] = result[half_len:]
        small_ref[6 + image : 7 + image, :] = column_sum(valid * ffn * upstream)
        normed, inverse = normalize(middle)
        grad_h2 = gh2_ref[rows, :]
        small_ref[2 + image : 3 + image, :] = column_sum(grad_h2)
        small_ref[4 + image : 5 + image, :] = column_sum(grad_h2 * normed)
        grad_mid = upstream + norm_back(grad_h2 * (1.0 + part(image, 4)), normed, inverse)
        grad_mid_ref[rows, :] = grad_mid
        small_ref[image : image + 1, :] = column_sum(valid * attn_ref[rows, :] * grad_mid)
        grad_attn = (valid * part(image, 2) * grad_mid).astype(LOW)
        h2_ref[rows, :] = grad_attn
        out_bias_grad = out_bias_grad + column_sum(grad_attn.astype(F32))
        grad_att_ref[rows, :] = nt(grad_attn, out_w_ref[...]).astype(LOW)
    small_ref[8:9, :] = out_bias_grad
    results += fetch(
        [
            (grad_att_ref, grad_att_hbm),
            (grad_mid_ref, grad_mid_hbm),
            (
                output_ref.at[:, pl.ds(0, half_len)],
                output_hbm.at[pl.ds(first_image, image_count)],
            ),
        ],
        out_sems.at[pl.ds(5, 3)],
    )
    out_term = tn(att_ref[...], h2_ref[...])
    out_first = jnp.concatenate([out_term[:half, :half], out_term[half:, :half]], axis=1)
    out_second = jnp.concatenate([out_term[:half, half:], out_term[half:, half:]], axis=1)
    rows = slice(2 * width + ff_width // 2, 2 * width + ff_width // 2 + half)
    keep_ref[rows, :] = jnp.where(core == 0, out_first, out_second)
    send_ref[rows, :] = jnp.where(core == 0, out_second, out_first).astype(LOW)
    send_ref[keep_ref.shape[0] : keep_ref.shape[0] + 16, :] = small_ref[...].astype(LOW)
    for copy in results:
        copy.wait()


def backward_kernel(
    images_hbm,
    penalty_hbm,
    qkv_w_hbm,
    qkv_hbm,
    grad_att_hbm,
    grad_mid_hbm,
    mod_hbm,
    after_ref,
    grad_tokens_hbm,
    far_ref,
    h1_ref,
    gqkv_ref,
    small_ref,
    tokens_ref,
    penalty_ref,
    qkv_w_ref,
    qkv_ref,
    grad_att_ref,
    grad_mid_ref,
    mod_ref,
    grad_tokens_ref,
    in_sems,
    out_sems,
):
    image_count, length, width = tokens_ref.shape
    half_len = length // 2
    copies = fetch(
        [
            (penalty_hbm, penalty_ref),
            (qkv_hbm, qkv_ref),
            (grad_att_hbm, grad_att_ref),
            (mod_hbm, mod_ref),
            (images_hbm, tokens_ref),
            (qkv_w_hbm, qkv_w_ref),
            (grad_mid_hbm, grad_mid_ref),
        ],
        in_sems,
    )
    for copy in copies[:3]:
        copy.wait()
    first, second = head_masks(length)

    def pair_step(step, carry):
        image = step // (HEADS // 2)
        pair = step % (HEADS // 2)
        rows = pl.ds(pl.multiple_of(image * length, length), length)

        def lanes(which):
            return pl.ds(pl.multiple_of(which * width + pair * PAIR, PAIR), PAIR)

        queries = qkv_ref[rows, lanes(0)] * jnp.asarray(HEAD_DIM**-0.5, LOW)
        keys = qkv_ref[rows, lanes(1)]
        values = qkv_ref[rows, lanes(2)]
        grad_att = grad_att_ref[rows, lanes(0)]
        penalty = penalty_ref[pl.ds(image, 1), :]
        grad_q = jnp.zeros((length, PAIR), F32)
        grad_k = jnp.zeros((length, PAIR), F32)
        grad_v = jnp.zeros((length, PAIR), F32)
        for mask in (first, second):
            own_queries = masked(queries, mask)
            own_grad = masked(grad_att, mask)
            probs = softmax_rows(own_queries, keys, penalty)
            grad_probs = nt(own_grad, values)
            dots = jnp.sum(probs * grad_probs, axis=-1, keepdims=True)
            grad_scores = (probs * (grad_probs - dots)).astype(LOW)
            grad_v = grad_v + tn(probs.astype(LOW), own_grad)
            grad_q = grad_q + nn(grad_scores, masked(keys, mask))
            grad_k = grad_k + tn(grad_scores, own_queries)
        gqkv_ref[rows, lanes(0)] = (grad_q * HEAD_DIM**-0.5).astype(LOW)
        gqkv_ref[rows, lanes(1)] = grad_k.astype(LOW)
        gqkv_ref[rows, lanes(2)] = grad_v.astype(LOW)
        return carry

    lax.fori_loop(0, image_count * (HEADS // 2), pair_step, 0)

    def part(image, which):
        return mod_ref[image : image + 1, which * width : (which + 1) * width].astype(F32)

    for copy in copies[3:]:
        copy.wait()
    small_ref[...] = jnp.zeros_like(small_ref)
    small_ref[4:5, :] = column_sum(gqkv_ref[:, :width].astype(F32))
    small_ref[5:6, :] = column_sum(gqkv_ref[:, 2 * width :].astype(F32))
    for image in range(image_count):
        rows = slice(image * length, (image + 1) * length)
        normed, inverse = normalize(tokens_ref[image].astype(F32))
        h1_ref[rows, :] = (normed * (1.0 + part(image, 1)) + part(image, 0)).astype(LOW)
        grad_h1 = nt(gqkv_ref[rows, :], qkv_w_ref[...])
        small_ref[image : image + 1, :] = column_sum(grad_h1)
        small_ref[2 + image : 3 + image, :] = column_sum(grad_h1 * normed)
        grad_in = norm_back(grad_h1 * (1.0 + part(image, 1)), normed, inverse)
        result = (grad_mid_ref[rows, :] + grad_in).astype(LOW)
        grad_tokens_ref[image] = result
        far_ref[image] = result[half_len:]
    results = fetch(
        [
            (
                grad_tokens_ref.at[:, pl.ds(0, half_len)],
                grad_tokens_hbm.at[pl.ds(lax.axis_index("seq") * image_count, image_count)],
            ),
        ],
        out_sems,
    )
    for copy in results:
        copy.wait()


def qkv_kernel(h1_ref, gqkv_ref, small_ref, keep_ref, send_ref, other_ref):
    core = lax.axis_index("seq")
    width = keep_ref.shape[1]
    half = width // 2
    low_term = tn(h1_ref[...], gqkv_ref[:, :width])
    high_term = tn(h1_ref[...], gqkv_ref[:, 2 * width :])
    keep_ref[:width, :] = jnp.where(core == 0, low_term, high_term)
    pair = jnp.where(core == 0, high_term, low_term).astype(LOW)
    send_ref[...] = pair[: width // 4 * 3]
    other_ref[: width // 4, :] = pair[width // 4 * 3 :]
    term = tn(h1_ref[...], gqkv_ref[:, width : 2 * width])
    low_unit = jnp.concatenate([term[:half, :half], term[half:, :half]], axis=1)
    high_unit = jnp.concatenate([term[:half, half:], term[half:, half:]], axis=1)
    keep_ref[width:, :] = jnp.where(core == 0, low_unit, high_unit)
    start = width // 4
    other_ref[start : start + half, :] = jnp.where(core == 0, high_unit, low_unit).astype(LOW)
    other_ref[start + half : start + half + 8, :] = small_ref[...].astype(LOW)


def by_core(core, near, far):
    return [jnp.where(core == 0, near, far), jnp.where(core == 0, far, near)]


def split_kernel(keep_ref, recv_ref, small_ref, own_ref, one_ref, two_ref, three_ref):
    core = lax.axis_index("seq")
    width = keep_ref.shape[1]
    piece = width // 16
    long = 4 * piece
    near = small_ref[...].astype(LOW).astype(F32)
    far = recv_ref[keep_ref.shape[0] : keep_ref.shape[0] + 16, :].astype(F32)
    first, second = by_core(core, near, far)
    mods = []
    for row in range(0, 6, 2):
        low_kind = [first[:2], second[:2]] if row == 0 else [jnp.zeros((4, width), F32)]
        high_kind = [first[row + 2 : row + 4], second[row + 2 : row + 4]]
        mods.append(
            jnp.where(
                core == 0, jnp.concatenate(low_kind, axis=0), jnp.concatenate(high_kind, axis=0)
            )
        )
    mods += [first[14:16], second[14:16], first[8:14] + second[8:14], jnp.zeros((2, width), F32)]
    small = jnp.concatenate(mods, axis=0)
    for step, target in enumerate((own_ref, one_ref, two_ref, three_ref)):
        who = (lax.axis_index("dp") & 3) ^ step

        def move(start, size, to):
            rows = pl.ds(pl.multiple_of(start, 8), size)
            target[to : to + size, :] = (
                keep_ref[rows, :] + recv_ref[rows, :].astype(F32)
            ).astype(target.dtype)

        for z in range(4):
            for side in range(2):
                move(side * width + piece * (4 * z + who), piece, (2 * z + side) * piece)
        for z in range(2):
            move(2 * width + long * (4 * z + who), long, 8 * piece + z * long)
            move(2 * width + 8 * long + piece * (4 * z + who), piece, 16 * piece + z * piece)
        target[18 * piece :, :] = small.astype(LOW).astype(target.dtype)


def split_qkv_kernel(keep_ref, recv_ref, other_ref, small_ref, *refs):
    core = lax.axis_index("seq")
    width = keep_ref.shape[1]
    piece = width // 16
    quarter = recv_ref.shape[0]
    near = small_ref[...].astype(LOW).astype(F32)
    start = keep_ref.shape[0] - quarter
    far = other_ref[start : start + 8, :].astype(F32)
    first, second = by_core(core, near, far)
    mods = jnp.concatenate([first[0:2], second[0:2], first[2:4], second[2:4]], axis=0)
    small = jnp.concatenate(
        [mods, first[4:6] + second[4:6], jnp.zeros((6, width), F32)], axis=0
    ).astype(LOW)
    total_ref = refs[-1]
    total_ref[:quarter, :] = keep_ref[:quarter, :] + recv_ref[...].astype(F32)
    total_ref[quarter:, :] = keep_ref[quarter:, :] + other_ref[:start, :].astype(F32)
    for step, target in enumerate(refs[-5:-1]):
        who = (lax.axis_index("dp") & 3) ^ step
        for z in range(6):
            start = width + piece * (4 * (z - 4) + who) if z >= 4 else piece * (4 * z + who)
            rows = pl.ds(pl.multiple_of(start, 8), piece)
            target[piece * z : piece * (z + 1), :] = total_ref[rows, :].astype(target.dtype)
        target[6 * piece :, :] = small.astype(target.dtype)


def fold_kernel(*refs):
    ones, twos = refs[:4], refs[4:8]
    rest_ref, rest_small_ref = refs[8:10]
    sends = refs[10:13]
    one_ref, two_ref, group_ref, late_ref = refs[13:]
    core = lax.axis_index("seq")
    width = one_ref.shape[1]
    piece = width // 16
    long = 4 * piece
    half = width // 2
    plane = lax.axis_index("dp") & 3

    def summed(sources, rows):
        return sum((source[rows, :].astype(F32) for source in sources[1:]), sources[0][rows, :])

    one_ref[...] = summed(ones, slice(0, 18 * piece))
    two_ref[...] = summed(twos, slice(0, 6 * piece))
    for step in range(4):
        group_ref[plane ^ step] = ones[step][18 * piece :, :].astype(F32)
        late_ref[plane ^ step] = twos[step][6 * piece :, :].astype(F32)
    rows = []
    for q in range(4):
        early, late = group_ref[q], late_ref[q]
        rows.append(
            jnp.where(
                core == 0, jnp.concatenate([late[:8], early[:4]], axis=0), early[:12]
            )
        )
        rows.append(early[12:16])
    early = group_ref[0] + group_ref[1] + group_ref[2] + group_ref[3]
    late = late_ref[0] + late_ref[1] + late_ref[2] + late_ref[3]
    rows += [early[16:22], late[8:10]]
    small = jnp.concatenate(rows, axis=0).astype(LOW)
    rest_small_ref[...] = small
    for step, target in enumerate((rest_ref,) + tuple(sends)):
        who = (lax.axis_index("dp") >> 2) ^ step
        dtype = target.dtype

        def block(ref, start, size):
            return ref[pl.ds(pl.multiple_of(start, 8), size), :]

        def side(value):
            return jnp.where(who < 2, value[:, :half], value[:, half:])

        target[: 2 * piece, :] = block(one_ref, 2 * piece * who, 2 * piece).astype(dtype)
        down = side(block(one_ref, 8 * piece + long * (who % 2), long))
        down = jnp.concatenate([down[: 2 * piece], down[2 * piece :]], axis=1)
        target[2 * piece : 4 * piece, :] = down.astype(dtype)
        out = side(block(one_ref, 16 * piece + piece * (who % 2), piece))
        unit = side(block(two_ref, 4 * piece + piece * (who % 2), piece))
        target[4 * piece : 5 * piece, :] = jnp.concatenate([out, unit], axis=1).astype(dtype)
        target[5 * piece : 6 * piece, :] = block(two_ref, piece * who, piece).astype(dtype)
        if step:
            target[6 * piece :, :] = small


def group_parts(lead, own_groups, hot, kinds, kind_of, extra):
    silu_rows = nn(lead, hot).astype(LOW)
    zeros = jnp.zeros_like(kind_of, F32)
    blocks = [masked(silu_rows, kind_of == kind) for kind in kinds]
    rows = []
    for kind in kinds:
        for one in own_groups:
            rows.append(jnp.where((kind_of == kind) & one, 1.0, zeros))
    for kind in kinds:
        rows.append(jnp.where(kind_of == kind, 1.0, zeros))
    for mark in extra:
        rows.append(jnp.where(mark, 1.0, zeros))
    while len(rows) % 8:
        rows.append(zeros)
    return blocks, jnp.concatenate(rows, axis=0).astype(LOW)


def split_dot(values, weight):
    high = values.astype(LOW)
    low = (values - high.astype(F32)).astype(LOW)
    return nt(high, weight) + nt(low, weight)


def spread_ids(marks, count, row_of):
    column = lax.broadcasted_iota(jnp.int32, (marks.shape[1], count), 1)
    row = lax.broadcasted_iota(jnp.int32, (marks.shape[1], count), 0)
    chosen = jnp.where(row == row_of(column), 1.0, 0.0).astype(LOW)
    return nn(marks, chosen)[:1].astype(jnp.int32)


def one_hot(ids, lead):
    place = lax.broadcasted_iota(jnp.int32, (lead.shape[1], ids.shape[1]), 0)
    wanted = (ids // GROUPS_PER_RANK) * 8 + ids % GROUPS_PER_RANK
    return jnp.where(place == wanted, 1.0, 0.0).astype(LOW)


def late_kernel(
    own_ref,
    own_small_ref,
    one_ref,
    two_ref,
    three_ref,
    lead_ref,
    ada_hbm,
    recv_ref,
    far_ref,
    output_hbm,
    grad_tokens_hbm,
    output_to,
    grad_tokens_to,
    up_ref,
    out_ref,
    down_ref,
    qkv_ref,
    ada_out_ref,
    own_sums_ref,
    send_ref,
    out_bias_ref,
    up_bias_ref,
    down_bias_ref,
    qv_ref,
    stack_ref,
    bias_ref,
    ada_ref,
    sems,
):
    core = lax.axis_index("seq")
    width = own_ref.shape[1]
    piece = width // 16
    half = width // 2
    count, half_len = far_ref.shape[:2]
    start = recv_ref.shape[0] - count * half_len
    pairs = [
        (ada_hbm.at[:, pl.ds(pl.multiple_of(core * 3 * width, LANES), 3 * width)], ada_ref),
        (far_ref, grad_tokens_to.at[pl.ds((1 - core) * count, count)]),
    ]
    for image in range(count):
        pairs.append(
            (
                recv_ref.at[pl.ds(start + image * half_len, half_len)],
                output_to.at[(1 - core) * count + image],
            )
        )
    copies = fetch(pairs, sems)
    parts = (own_ref, one_ref, two_ref, three_ref)
    weights = slice(0, 6 * piece)
    total = sum((part[weights, :].astype(F32) for part in parts[1:]), own_ref[weights, :])
    up_ref[...] = jnp.concatenate([total[:piece], total[piece : 2 * piece]], axis=1)
    down = total[2 * piece : 4 * piece]
    down_ref[...] = jnp.concatenate([down[:, :half], down[:, half:]], axis=0)
    out_ref[...] = total[4 * piece : 5 * piece, :half]
    unit = total[4 * piece : 5 * piece, half:]
    pair = total[5 * piece :]
    qkv_ref[...] = jnp.where(
        core == 0,
        jnp.concatenate([pair, unit], axis=1),
        jnp.concatenate([unit, pair], axis=1),
    )
    line = lax.axis_index("dp") >> 2
    smalls = (own_small_ref[...],) + tuple(part[6 * piece :, :] for part in parts[1:])
    for step, small in enumerate(smalls):
        stack_ref[line ^ step] = small[:64]
        bias_ref[line ^ step] = small[64:].astype(F32)
    bias = bias_ref[0] + bias_ref[1] + bias_ref[2] + bias_ref[3]
    out_bias_ref[...] = bias[0:1].reshape(width)
    up_bias_ref[...] = jnp.concatenate([bias[1 + row : 2 + row] for row in range(4)], axis=1).reshape(
        4 * width
    )
    down_bias_ref[...] = bias[5:6].reshape(width)
    qv_ref[...] = bias[6:8]
    stack = stack_ref[...].reshape(256, width)
    lead = lead_ref[...]
    corner = (lax.broadcasted_iota(jnp.int32, (8, LANES), 1) == 0).astype(F32).astype(LOW)
    marks = nt(corner, stack[:, :LANES]).astype(LOW)
    ids = spread_ids(marks, 256, lambda index: index - index % 16 + 12 + index % 4)
    hot = one_hot(ids, lead)
    item = lax.broadcasted_iota(jnp.int32, (1, 256), 1) % 16
    base = GROUPS_PER_RANK * lax.axis_index("dp")
    own = [ids == base + index for index in range(GROUPS_PER_RANK)]
    blocks, rows = group_parts(lead, own, hot, range(3), item // 4, [])
    for kind in range(3):
        ada_out_ref[:, kind * width : (kind + 1) * width] = nn(blocks[kind], stack)
    sums = nn(rows, stack)
    copies[0].wait()
    cond = jnp.zeros((8, width), F32)
    for kind in range(3):
        own_sum = jnp.concatenate(
            [sums[2 * kind : 2 * kind + 2], jnp.zeros((6, width), F32)], axis=0
        )
        cond = cond + split_dot(own_sum, ada_ref[:, kind * width : (kind + 1) * width])
    low_cond, high_cond = cond[:2, :half], cond[:2, half:]
    kept = jnp.where(core == 0, low_cond, high_cond)
    sent = jnp.where(core == 0, high_cond, low_cond)
    zeros = jnp.zeros((2, half), F32)
    pad = jnp.zeros((3, width), F32)
    own_sums_ref[...] = jnp.concatenate(
        [jnp.concatenate([kept, zeros], axis=1), sums[6:9], pad], axis=0
    )
    send_ref[...] = jnp.concatenate(
        [jnp.concatenate([sent, zeros], axis=1), sums[6:9], pad], axis=0
    )
    for copy in copies[1:]:
        copy.wait()


def final_kernel(own_ref, recv_ref, own_cond_ref, cond_ref, bias_ref):
    core = lax.axis_index("seq")
    width = own_ref.shape[1]
    half = width // 2
    near, far = own_ref[...], recv_ref[...]
    values = own_cond_ref[...].astype(F32)
    values = jnp.where(core == 0, values[:, :half], values[:, half:])
    gate = 1.0 / (1.0 + jnp.exp(-values))
    cond_ref[...] = (near[:2, :half] + far[:2, :half]) * (gate * (1.0 + values * (1.0 - gate)))
    rows = [block[row : row + 1] for block in by_core(core, near, far) for row in range(2, 5)]
    bias_ref[...] = jnp.concatenate(rows, axis=1).reshape(6 * width)


def silu_slope(values):
    sigmoid_val = jax.nn.sigmoid(values)
    return sigmoid_val * (1.0 + values * (1.0 - sigmoid_val))


def swap_cores(values):
    return lax.ppermute(values, "seq", CORE_SWAP)


def pick(core, first, second):
    return jnp.where(core == 0, first, second)


def to_patches(placed, far, core):
    return lax.dynamic_update_slice_in_dim(
        placed, swap_cores(far), (1 - core) * far.shape[0], 0
    )


def call(kernel, name, shapes, scratch, limit, spaces, *operands, aliases=None):
    chosen = {
        "s": pl.BlockSpec(memory_space=pltpu.SMEM),
        "v": pl.BlockSpec(memory_space=pltpu.VMEM),
        "V": pl.BlockSpec(memory_space=pltpu.VMEM),
        "a": pl.BlockSpec(memory_space=pl.ANY),
        "h": pl.BlockSpec(memory_space=pltpu.HBM),
    }
    pinned = {"h": pltpu.HBM, "V": pltpu.VMEM}
    into, out_of = spaces
    operands = [
        pltpu.with_memory_space_constraint(item, pinned[kind]) if kind in pinned else item
        for kind, item in zip(into, operands)
    ]
    return pl.pallas_call(
        kernel,
        out_shape=tuple(
            pinned.get(kind, jax.ShapeDtypeStruct)(shape, dtype)
            for kind, (shape, dtype) in zip(out_of, shapes)
        ),
        in_specs=[chosen[kind] for kind in into],
        out_specs=[chosen[kind] for kind in out_of],
        scratch_shapes=scratch,
        compiler_params=pltpu.CompilerParams(vmem_limit_bytes=limit << 20),
        cost_estimate=pl.CostEstimate(flops=1, bytes_accessed=1, transcendentals=0),
        input_output_aliases=aliases or {},
        name=name,
    )(*operands)


def rank_swap(values, step, count):
    return lax.ppermute(values, "dp", [(rank, rank ^ step) for rank in range(count)])


def owner_total(term, dp_count):
    blocks = term.astype(LOW).reshape(dp_count, term.shape[0] // dp_count, term.shape[1])
    return jnp.sum(lax.all_to_all(blocks, "dp", 0, 0, tiled=True).astype(F32), axis=0)


def general_tail(
    core, dp_count, dp_rank, sides, smalls, heads, cond_rows, cond, own_ids, ada_weight
):
    highest = lax.Precision.HIGHEST
    width, mod_width = ada_weight.shape
    half = width // 2
    (keep_one, send_one), (keep_two, send_two) = sides
    far_rows = send_one[keep_one.shape[0] + 16 :]
    small_one, small_two = smalls
    first_sum = keep_one + swap_cores(send_one[: keep_one.shape[0]]).astype(F32)
    second_sum = keep_two + swap_cores(send_two)[: keep_two.shape[0]].astype(F32)
    ff_half = first_sum.shape[0] - 2 * width - half
    up = jnp.concatenate([first_sum[:width], first_sum[width : 2 * width]], axis=1)
    down = first_sum[2 * width : 2 * width + ff_half]
    down = jnp.concatenate([down[:, :half], down[:, half:]], axis=0)
    out = first_sum[2 * width + ff_half :]
    out = jnp.concatenate([out[:, :half], out[:, half:]], axis=0)
    pair, unit = second_sum[:width], second_sum[width:]
    unit = jnp.concatenate([unit[:, :half], unit[:, half:]], axis=0)
    qkv = pick(
        core, jnp.concatenate([pair, unit], axis=1), jnp.concatenate([unit, pair], axis=1)
    )
    sums = [owner_total(term, dp_count) for term in (qkv, out, up, down)]
    image_grad = jnp.concatenate(
        [small_two[0:2], small_two[2:4], small_one[0:2], small_one[2:4], small_one[4:6], small_one[6:8]],
        axis=1,
    )
    biases = jnp.concatenate([small_two[4:6], small_one[8:14]], axis=0)
    marks = jnp.broadcast_to(own_ids.astype(F32)[:, None], (own_ids.shape[0], width))
    packed = jnp.concatenate([image_grad.reshape(-1, width), biases, marks], axis=0)
    gathered = lax.all_to_all(
        jnp.broadcast_to(packed[None], (2 * dp_count,) + packed.shape),
        ("dp", "seq"),
        0,
        0,
        tiled=True,
    )
    grad_rows = gathered[:, :12].reshape(-1, mod_width)
    bias_sums = jnp.sum(gathered[:, 12:20], axis=0)
    all_ids = gathered[:, 20:, 0].reshape(-1).astype(jnp.int32)
    group_count = cond_rows.shape[0]
    all_hot = (all_ids[:, None] == jnp.arange(group_count, dtype=jnp.int32)[None, :]).astype(F32)
    group_grad = jnp.dot(all_hot.T, grad_rows, precision=highest)
    own_rows = width // dp_count
    silu_rows = lax.reduce_precision(jax.nn.silu(cond_rows.astype(F32)), 8, 7)
    silu_part = lax.dynamic_slice_in_dim(silu_rows, dp_rank * own_rows, own_rows, 1)
    grad_half = pick(core, group_grad[:, : mod_width // 2], group_grad[:, mod_width // 2 :])
    ada_sum = jnp.dot(silu_part.T, grad_half, precision=highest)
    own_grad = lax.dynamic_slice_in_dim(
        group_grad, dp_rank * GROUPS_PER_RANK, GROUPS_PER_RANK, 0
    )
    ada_half = lax.dynamic_slice_in_dim(ada_weight, core * half, half, 0).astype(F32)
    cond_half = pick(core, cond[:, :half], cond[:, half:]).astype(F32)
    grad_cond = silu_slope(cond_half) * jnp.dot(own_grad, ada_half.T, precision=highest)
    return (
        to_patches(heads[0], far_rows.reshape(heads[2].shape), core),
        to_patches(heads[1], heads[2], core),
        grad_cond,
        sums[0],
        bias_sums[:2],
        sums[1],
        bias_sums[2],
        sums[2],
        bias_sums[3:7].reshape(-1),
        sums[3],
        bias_sums[7],
        ada_sum,
        jnp.sum(grad_rows, axis=0),
    )


def body(
    tokens,
    cotangent,
    cond,
    group_ids,
    image_counts,
    patch_mask,
    qkv_weight,
    qv_bias,
    out_weight,
    out_bias,
    up_weight,
    up_bias,
    down_weight,
    down_bias,
    ada_weight,
    ada_bias,
):
    slot_count, half_len, width = tokens.shape
    ff_width = up_weight.shape[1]
    mod_width = ada_weight.shape[1]
    dp_count = lax.axis_size("dp")
    core = lax.axis_index("seq").astype(jnp.int32)
    dp_rank = lax.axis_index("dp").astype(jnp.int32)
    image_count = slot_count // 2
    length = 2 * half_len
    row_count = image_count * length
    half = width // 2
    piece = width // dp_count
    fast = dp_count == 16 and not GENERAL
    block_shape = (dp_count, 8, width)
    block_rows = lax.broadcasted_iota(jnp.int32, block_shape, 1)
    block = jnp.zeros(block_shape, LOW)
    for row in range(GROUPS_PER_RANK):
        block = jnp.where(block_rows == row, cond[row][None, None], block)
    cond_blocks = lax.all_to_all(block, "dp", 0, 0, tiled=True)
    tokens_far = swap_cores(tokens)
    cot_far = swap_cores(cotangent)
    half_shape = (image_count, half_len, width)
    image_shape = (image_count, length, width)
    packed_rows = 2 * width + ff_width // 2 + half
    vmem = pltpu.VMEM
    (
        output,
        qkv,
        grad_att,
        grad_mid,
        image_mod,
        images,
        penalty,
        lead,
        keep_one,
        send_one,
        small_one,
    ) = call(
        partial(forward_kernel, piece if fast else 0),
        "forward_and_ffn_back",
        (
            (tokens.shape, LOW),
            ((row_count, 3 * width), LOW),
            ((row_count, width), LOW),
            ((row_count, width), F32),
            ((8, mod_width), LOW),
            (image_shape, LOW),
            ((8, length), F32),
            ((24, 8 * dp_count), LOW),
            ((packed_rows, width), F32),
            ((packed_rows + 16 + image_count * half_len, width), LOW),
            ((16, width), F32),
        ),
        [
            vmem(image_shape, LOW),
            vmem(image_shape, LOW),
            vmem(block_shape, LOW),
            vmem(patch_mask.shape, jnp.int32),
            vmem(qkv_weight.shape, LOW),
            vmem(qv_bias.shape, LOW),
            vmem(out_weight.shape, LOW),
            vmem(out_bias.shape, LOW),
            vmem(up_weight.shape, LOW),
            vmem(up_bias.shape, LOW),
            vmem(down_weight.shape, LOW),
            vmem(down_bias.shape, LOW),
            vmem(ada_weight.shape, LOW),
            vmem(ada_bias.shape, LOW),
            pltpu.SMEM(group_ids.shape, jnp.int32),
            pltpu.SMEM(image_counts.shape, jnp.int32),
            vmem(image_shape, LOW),
            vmem((row_count, 3 * width), LOW),
            vmem((row_count, width), LOW),
            vmem((row_count, width), F32),
            vmem((8, mod_width), LOW),
            vmem((8, length), F32),
            vmem((row_count, LANES), F32),
            vmem((row_count, width), LOW),
            vmem((row_count, width), F32),
            vmem((row_count, width), F32),
            vmem((row_count, width), LOW),
            vmem((row_count, width), LOW),
            vmem((row_count, CHUNK), LOW),
            vmem((row_count, CHUNK), LOW),
            vmem((row_count, width), F32),
            vmem((row_count, width), F32),
            vmem((width, 8 * dp_count), F32),
            vmem((24, 8 * dp_count), LOW),
            pltpu.SemaphoreType.DMA((14 + 4 * image_count,)),
            pltpu.SemaphoreType.DMA((8,)),
        ],
        40,
        ("hahaaaa" + "h" * 11, "h" * 8 + "VVV"),
        tokens,
        tokens_far,
        cotangent,
        cot_far,
        cond_blocks,
        group_ids,
        image_counts,
        patch_mask,
        qkv_weight,
        qv_bias,
        out_weight,
        out_bias,
        up_weight,
        up_bias,
        down_weight,
        down_bias,
        ada_weight,
        ada_bias,
    )

    def attention_back(after):
        return call(
            backward_kernel,
            "attention_back",
            (
                (tokens.shape, LOW),
                (half_shape, LOW),
                ((row_count, width), LOW),
                ((row_count, 3 * width), LOW),
                ((8, width), F32),
            ),
            [
                vmem(image_shape, LOW),
                vmem((8, length), F32),
                vmem(qkv_weight.shape, LOW),
                vmem((row_count, 3 * width), LOW),
                vmem((row_count, width), LOW),
                vmem((row_count, width), F32),
                vmem((8, mod_width), LOW),
                vmem(image_shape, LOW),
                pltpu.SemaphoreType.DMA((7,)),
                pltpu.SemaphoreType.DMA((1,)),
            ],
            24,
            ("h" * 7 + "a", "hVVVV"),
            images,
            penalty,
            qkv_weight,
            qkv,
            grad_att,
            grad_mid,
            image_mod,
            after,
        )

    def qkv_back(h1, grad_qkv, small_two):
        return call(
            qkv_kernel,
            "qkv_back",
            (
                ((width + half, width), F32),
                ((width // 4 * 3, width), LOW),
                ((width // 4 + half + 8, width), LOW),
            ),
            [],
            16,
            ("VVV", "VVV"),
            h1,
            grad_qkv,
            small_two,
        )

    if not fast:
        grad_tokens, grad_far, h1, grad_qkv, small_two = attention_back(small_one)
        keep_two, *sent_two = qkv_back(h1, grad_qkv, small_two)
        own_ids = lax.dynamic_slice_in_dim(group_ids, core * image_count, image_count, 0)
        return general_tail(
            core,
            dp_count,
            dp_rank,
            ((keep_one, send_one), (keep_two, jnp.concatenate(sent_two, axis=0))),
            (small_one, small_two),
            (output, grad_tokens, grad_far),
            cond_blocks[:, :GROUPS_PER_RANK].reshape(-1, width),
            cond,
            own_ids,
            ada_weight,
        )

    recv_one = swap_cores(send_one)
    split_rows = 18 * piece + 24
    own_part, *sent_parts = call(
        split_kernel,
        "split_plane",
        (((split_rows, width), F32),) + (((split_rows, width), LOW),) * 3,
        [],
        16,
        ("VVV", "VVVV"),
        keep_one,
        recv_one,
        small_one,
    )
    near_parts = [rank_swap(item, step + 1, 16) for step, item in enumerate(sent_parts)]
    grad_tokens, grad_far, h1, grad_qkv, small_two = attention_back(sent_parts[2])
    keep_two, send_two, send_other = qkv_back(h1, grad_qkv, small_two)
    recv_far = swap_cores(grad_far)
    split_rows = 6 * piece + 16
    own_qkv, *sent_qkv = call(
        split_qkv_kernel,
        "split_qkv_plane",
        (((split_rows, width), F32),) + (((split_rows, width), LOW),) * 3,
        [vmem((width + half, width), F32)],
        16,
        ("VVVVaaa", "VVVV"),
        keep_two,
        swap_cores(send_two),
        swap_cores(send_other),
        small_two,
        *near_parts,
    )
    near_qkv = [rank_swap(item, step + 1, 16) for step, item in enumerate(sent_qkv)]
    line_rows = 6 * piece + 72
    rest, rest_small, *lines = call(
        fold_kernel,
        "fold_plane",
        (((6 * piece, width), F32), ((72, width), LOW)) + (((line_rows, width), LOW),) * 3,
        [
            vmem((18 * piece, width), F32),
            vmem((6 * piece, width), F32),
            vmem((4, 24, width), F32),
            vmem((4, 16, width), F32),
        ],
        16,
        ("V" * 8, "VVVVV"),
        own_part,
        *near_parts,
        own_qkv,
        *near_qkv,
    )
    lines = [rank_swap(item, 4 * (step + 1), 16) for step, item in enumerate(lines)]
    (
        output,
        grad_tokens,
        up_sum,
        out_sum,
        down_sum,
        qkv_sum,
        ada_sum,
        own_sums,
        send_sums,
        out_bias_sum,
        up_bias_sum,
        down_bias_sum,
        qv_sum,
    ) = call(
        late_kernel,
        "late_groups",
        (
            (tokens.shape, LOW),
            (tokens.shape, LOW),
            ((piece, ff_width // 2), F32),
            ((piece, half), F32),
            ((4 * piece, half), F32),
            ((piece, 3 * half), F32),
            ((piece, mod_width // 2), F32),
            ((8, width), F32),
            ((8, width), F32),
            ((width,), F32),
            ((ff_width,), F32),
            ((width,), F32),
            ((2, width), F32),
        ),
        [
            vmem((4, 64, width), LOW),
            vmem((4, 8, width), F32),
            vmem((width, mod_width // 2), LOW),
            pltpu.SemaphoreType.DMA((2 + image_count,)),
        ],
        16,
        ("VVVVVVhVVhh", "hhvvvvvVVvvvv"),
        rest,
        rest_small,
        *lines,
        lead,
        ada_weight,
        recv_one,
        recv_far,
        output,
        grad_tokens,
        aliases={9: 0, 10: 1},
    )
    grad_cond, ada_bias_sum = call(
        final_kernel,
        "final_groups",
        (((GROUPS_PER_RANK, half), F32), ((mod_width,), F32)),
        [],
        16,
        ("VVv", "vv"),
        own_sums,
        swap_cores(send_sums),
        cond,
    )
    return (
        output,
        grad_tokens,
        grad_cond,
        qkv_sum,
        qv_sum,
        out_sum,
        out_bias_sum,
        up_sum,
        up_bias_sum,
        down_sum,
        down_bias_sum,
        ada_sum,
        ada_bias_sum,
    )


def solution(mesh):
    placed = (
        P("dp", "seq", None),
        P("dp", "seq", None),
        P("dp", None),
        P("dp"),
        P("dp"),
        P("dp", None),
        P(),
        P(),
        P(),
        P(),
        P(),
        P(),
        P(),
        P(),
        P(),
        P(),
    )
    return jax.shard_map(
        body,
        mesh=mesh,
        in_specs=placed,
        out_specs=(
            P("dp", "seq", None),
            P("dp", "seq", None),
            P("dp", "seq"),
            P("dp", "seq"),
            P(),
            P("dp", "seq"),
            P(),
            P("dp", "seq"),
            P(),
            P("dp", "seq"),
            P(),
            P("dp", "seq"),
            P(),
        ),
        check_vma=False,
    )
```

```python
from functools import partial

import jax
import jax.numpy as jnp
from jax import lax
from jax.experimental import pallas as pl
from jax.experimental.pallas import tpu as pltpu
from jax.sharding import PartitionSpec as P

HEADS = 6
HEAD_DIM = 64
PAIR = 2 * HEAD_DIM
CORE_SWAP = ((0, 1), (1, 0))
CHUNK = 256
LANES = 128
GROUPS_PER_RANK = 2
GENERAL = False
F32 = jnp.float32
LOW = jnp.bfloat16


def nn(left, right):
    return lax.dot_general(left, right, (((1,), (0,)), ((), ())), preferred_element_type=F32)


def nt(left, right):
    return lax.dot_general(left, right, (((1,), (1,)), ((), ())), preferred_element_type=F32)


def tn(left, right):
    return lax.dot_general(left, right, (((0,), (0,)), ((), ())), preferred_element_type=F32)


def normalize(values):
    center = values - jnp.mean(values, axis=-1, keepdims=True)
    spread = jnp.mean(center * center, axis=-1, keepdims=True)
    inverse = lax.rsqrt(spread + 1e-06)
    return center * inverse, inverse


def norm_back(grad, normed, inverse):
    return inverse * (
        grad
        - jnp.mean(grad, axis=-1, keepdims=True)
        - normed * jnp.mean(grad * normed, axis=-1, keepdims=True)
    )


def column_sum(values):
    return jnp.sum(values, axis=0, keepdims=True)


def head_masks(rows):
    lane = lax.broadcasted_iota(jnp.int32, (rows, PAIR), 1)
    return lane < HEAD_DIM, lane >= HEAD_DIM


def masked(values, mask):
    return jnp.where(mask, values, jnp.zeros_like(values))


def softmax_rows(queries, keys, penalty):
    scores = nt(queries, keys) + penalty
    exps = jnp.exp(scores - jnp.max(scores, axis=-1, keepdims=True))
    return exps / jnp.sum(exps, axis=-1, keepdims=True)


def fetch(pairs, sems):
    copies = []
    for index, (source, target) in enumerate(pairs):
        copy = pltpu.make_async_copy(source, target, sems.at[index])
        copy.start()
        copies.append(copy)
    return copies


def own_images(near_ref, far_ref, target_ref, first_image):
    half_len = near_ref.shape[1]
    pairs = []
    for image in range(target_ref.shape[0]):
        slot = first_image + image
        pairs.append((near_ref.at[slot], target_ref.at[image, pl.ds(0, half_len)]))
        pairs.append((far_ref.at[slot], target_ref.at[image, pl.ds(half_len, half_len)]))
    return pairs


def own_marks(mask_ref, counts_ref, core, image, image_count, half_len):
    slot = core * image_count + image
    live = jnp.where(slot < counts_ref[0], 1.0, 0.0)
    marks = mask_ref[pl.ds(slot, 1), :].astype(F32) * live
    low_marks, high_marks = marks[:, :half_len], marks[:, half_len:]
    return jnp.concatenate(
        [
            jnp.where(core == 0, low_marks, high_marks),
            jnp.where(core == 0, high_marks, low_marks),
        ],
        axis=1,
    )


def as_row(ref):
    return ref[...].astype(F32).reshape(1, ref.shape[0])


def load_kernel(
    tokens_hbm,
    tokens_far_ref,
    cot_hbm,
    cot_far_ref,
    ids_hbm,
    counts_hbm,
    mask_hbm,
    qv_b_hbm,
    out_b_hbm,
    up_b_hbm,
    down_b_hbm,
    ada_w_hbm,
    ada_b_hbm,
    images_ref,
    normed_ref,
    penalty_ref,
    hot_ref,
    marks_ref,
    qkv_b_ref,
    out_b_ref,
    up_b_ref,
    down_b_ref,
    ada_w_ref,
    ada_b_ref,
    cot_images_hbm,
    inverse_hbm,
    cot_ref,
    inverse_ref,
    ids_ref,
    counts_ref,
    mask_ref,
    qv_b_ref,
    out_b_raw,
    up_b_raw,
    down_b_raw,
    ada_b_raw,
    sems,
):
    core = lax.axis_index("seq")
    image_count, length, width = images_ref.shape
    half_len = length // 2
    first_image = core * image_count
    copies = fetch(
        own_images(tokens_hbm, tokens_far_ref, images_ref, first_image)
        + [
            (ids_hbm, ids_ref),
            (counts_hbm, counts_ref),
            (mask_hbm, mask_ref),
            (qv_b_hbm, qv_b_ref),
            (out_b_hbm, out_b_raw),
            (up_b_hbm, up_b_raw),
            (down_b_hbm, down_b_raw),
            (ada_b_hbm, ada_b_raw),
        ]
        + own_images(cot_hbm, cot_far_ref, cot_ref, first_image)
        + [(ada_w_hbm, ada_w_ref)],
        sems,
    )
    token_copies = 2 * image_count
    for copy in copies[: token_copies + 8]:
        copy.wait()
    row = lax.broadcasted_iota(jnp.int32, hot_ref.shape, 0)
    column = lax.broadcasted_iota(jnp.int32, hot_ref.shape, 1)
    hot = jnp.zeros(hot_ref.shape, F32)
    marks_ref[...] = jnp.zeros_like(marks_ref)
    penalty_ref[...] = jnp.zeros_like(penalty_ref)
    for image in range(image_count):
        group = ids_ref[first_image + image]
        place = 8 * (group // GROUPS_PER_RANK) + group % GROUPS_PER_RANK
        hot = jnp.where((row == image) & (column == place), 1.0, hot)
        marks_ref[image : image + 1, :] = jnp.full((1, width), group.astype(F32), F32)
        marks = own_marks(mask_ref, counts_ref, core, image, image_count, half_len)
        penalty_ref[image : image + 1, :] = (marks - 1.0) * 30000.0
        rows = slice(image * length, (image + 1) * length)
        normed, inverse = normalize(images_ref[image].astype(F32))
        normed_ref[rows, :] = normed
        inverse_ref[rows, :] = jnp.broadcast_to(inverse, (length, LANES))
    hot_ref[...] = hot.astype(LOW)
    qkv_b_ref[...] = jnp.concatenate(
        [qv_b_ref[0:1, :], jnp.zeros((1, width), LOW), qv_b_ref[1:2, :]], axis=1
    ).astype(F32)
    for raw, target in (
        (out_b_raw, out_b_ref),
        (up_b_raw, up_b_ref),
        (down_b_raw, down_b_ref),
        (ada_b_raw, ada_b_ref),
    ):
        target[...] = as_row(raw)
    for copy in copies[token_copies + 8 :]:
        copy.wait()
    for copy in fetch([(cot_ref, cot_images_hbm), (inverse_ref, inverse_hbm)], sems):
        copy.wait()


def attention_pair(step, qkv_ref, penalty_ref, length, width):
    image, pair = divmod(step, HEADS // 2)
    rows = slice(image * length, (image + 1) * length)

    def lanes(which):
        start = which * width + pair * PAIR
        return slice(start, start + PAIR)

    queries = qkv_ref[rows, lanes(0)] * jnp.asarray(HEAD_DIM**-0.5, LOW)
    return rows, lanes, queries, qkv_ref[rows, lanes(1)], qkv_ref[rows, lanes(2)]


def forward_kernel(
    lead_rows,
    cond_ref,
    images_ref,
    normed_ref,
    penalty_ref,
    hot_ref,
    marks_ref,
    qkv_b_ref,
    out_b_ref,
    up_b_ref,
    down_b_ref,
    ada_w_ref,
    ada_b_ref,
    cot_hbm,
    qkv_w_hbm,
    out_w_hbm,
    up_w_hbm,
    down_w_hbm,
    output_ref,
    qkv_ref,
    h1_ref,
    grad_att_ref,
    grad_mid_ref,
    mod_ref,
    lead_ref,
    qkv_w_ref,
    keep_ref,
    send_ref,
    small_ref,
    cond_rows_ref,
    turned_ref,
    att_ref,
    mid_ref,
    attn_ref,
    h2_ref,
    gffn_ref,
    act_ref,
    gpre_ref,
    valid_ref,
    cot_ref,
    out_w_ref,
    up_w_ref,
    down_w_ref,
    sems,
):
    core = lax.axis_index("seq")
    image_count, length, width = images_ref.shape
    half_len = length // 2
    half = width // 2
    ff_width = up_w_ref.shape[1]
    copies = fetch(
        [
            (qkv_w_hbm, qkv_w_ref),
            (out_w_hbm, out_w_ref),
            (cot_hbm, cot_ref),
            (up_w_hbm, up_w_ref),
            (down_w_hbm, down_w_ref),
        ],
        sems,
    )
    block_count, block_rows = cond_ref.shape[:2]
    cond_rows_ref[...] = jnp.zeros_like(cond_rows_ref)
    for block in range(block_count):
        cond_rows_ref[8 * block : 8 * block + block_rows, :] = cond_ref[block].astype(F32)
    cond = cond_rows_ref[...]
    silu = cond / (1.0 + jnp.exp(-cond))
    image_silu = nn(hot_ref[...], silu.astype(LOW)).astype(LOW)
    mod_ref[...] = (nn(image_silu, ada_w_ref[...]) + ada_b_ref[...]).astype(LOW)

    def part(image, which):
        return mod_ref[image : image + 1, which * width : (which + 1) * width].astype(F32)

    def rows_of(image):
        return slice(image * length, (image + 1) * length)

    def valid_of(image):
        column = valid_ref[rows_of(image), :]
        return jnp.concatenate([column] * (width // LANES), axis=1)

    copies[0].wait()
    for image in range(image_count):
        rows = rows_of(image)
        marks = jnp.where(penalty_ref[image : image + 1, :] < 0.0, 0.0, 1.0)
        valid_ref[rows, :] = jnp.broadcast_to(marks, (LANES, length)).T
        h1 = (normed_ref[rows, :] * (1.0 + part(image, 1)) + part(image, 0)).astype(LOW)
        h1_ref[rows, :] = h1
        qkv_ref[rows, :] = (nn(h1, qkv_w_ref[...]) + qkv_b_ref[...]).astype(LOW)

    first, second = head_masks(length)
    for step in range(image_count * (HEADS // 2)):
        rows, lanes, queries, keys, values = attention_pair(
            step, qkv_ref, penalty_ref, length, width
        )
        image = step // (HEADS // 2)
        penalty = penalty_ref[image : image + 1, :]
        total = jnp.zeros((length, PAIR), F32)
        for mask in (first, second):
            probs = softmax_rows(masked(queries, mask), keys, penalty).astype(LOW)
            total = total + nn(probs, masked(values, mask))
        att_ref[rows, lanes(0)] = total.astype(LOW)

    for copy in copies[1:]:
        copy.wait()
    if lead_rows:
        turned_ref[...] = silu.T
        start = pl.multiple_of(lax.axis_index("dp") * lead_rows, 8)
        lead_ref[...] = turned_ref[pl.ds(start, lead_rows), :].astype(LOW)
    else:
        lead_ref[...] = jnp.zeros_like(lead_ref)
    small_ref[...] = jnp.zeros_like(small_ref)
    small_ref[14:16, :] = marks_ref[:2, :]
    down_bias_grad = jnp.zeros((1, width), F32)
    for image in range(image_count):
        rows = rows_of(image)
        valid = valid_of(image)
        attn = nn(att_ref[rows, :], out_w_ref[...]) + out_b_ref[...]
        attn_ref[rows, :] = attn
        middle = images_ref[image].astype(F32) + valid * part(image, 2) * attn
        mid_ref[rows, :] = middle
        normed, _ = normalize(middle)
        h2_ref[rows, :] = (normed * (1.0 + part(image, 4)) + part(image, 3)).astype(LOW)
        grad_ffn = (valid * part(image, 5) * cot_ref[image].astype(F32)).astype(LOW)
        gffn_ref[rows, :] = grad_ffn
        down_bias_grad = down_bias_grad + column_sum(grad_ffn.astype(F32))
    small_ref[13:14, :] = down_bias_grad

    for chunk in range(ff_width // CHUNK):
        columns = slice(chunk * CHUNK, (chunk + 1) * CHUNK)
        up_w = up_w_ref[:, columns]
        down_w = down_w_ref[columns, :]
        bias = jnp.zeros((1, CHUNK), F32)
        for image in range(image_count):
            rows = rows_of(image)
            pre = nn(h2_ref[rows, :], up_w) + up_b_ref[:, columns]
            square = pre * pre
            inner = jnp.tanh(pre * (0.7978845608028654 + 0.035677408136300125 * square))
            cdf = 0.5 * inner + 0.5
            act_ref[rows, columns] = (pre * cdf).astype(LOW)
            slope = 0.5 * (pre * (0.7978845608028654 + 0.10703222440890037 * square)) * (
                1.0 - inner * inner
            ) + cdf
            grad_pre = (nt(gffn_ref[rows, :], down_w) * slope).astype(LOW)
            gpre_ref[rows, columns] = grad_pre
            bias = bias + column_sum(grad_pre.astype(F32))
        for tile in range(CHUNK // LANES):
            start = chunk * CHUNK + tile * LANES
            small_ref[9 + start // width : 10 + start // width, start % width : start % width + LANES] = (
                bias[:, tile * LANES : (tile + 1) * LANES]
            )

    first_half = gffn_ref[:, :half]
    second_half = gffn_ref[:, half:]
    gffn_keep = jnp.where(core == 0, first_half, second_half)
    gffn_send = jnp.where(core == 0, second_half, first_half)
    side_chunks = ff_width // CHUNK // 2
    for step in range(side_chunks):
        low = slice(step * CHUNK, (step + 1) * CHUNK)
        high = slice((step + side_chunks) * CHUNK, (step + side_chunks + 1) * CHUNK)
        up_low = tn(h2_ref[...], gpre_ref[:, low])
        up_high = tn(h2_ref[...], gpre_ref[:, high])
        up_keep = jnp.where(core == 0, up_low, up_high)
        up_send = jnp.where(core == 0, up_high, up_low).astype(LOW)
        for tile in range(CHUNK // LANES):
            start = step * CHUNK + tile * LANES
            rows = slice(start // width * width, (start // width + 1) * width)
            columns = slice(start % width, start % width + LANES)
            keep_ref[rows, columns] = up_keep[:, tile * LANES : (tile + 1) * LANES]
            send_ref[rows, columns] = up_send[:, tile * LANES : (tile + 1) * LANES]
        rows = slice(2 * width + step * CHUNK, 2 * width + (step + 1) * CHUNK)
        for target, side in ((keep_ref, gffn_keep), (send_ref, gffn_send)):
            target[rows, :] = jnp.concatenate(
                [tn(act_ref[:, low], side), tn(act_ref[:, high], side)], axis=1
            ).astype(target.dtype)

    out_bias_grad = jnp.zeros((1, width), F32)
    for image in range(image_count):
        rows = rows_of(image)
        valid = valid_of(image)
        upstream = cot_ref[image].astype(F32)
        middle = mid_ref[rows, :]
        ffn = nn(act_ref[rows, :], down_w_ref[...]) + down_b_ref[...]
        output_ref[image] = (middle + valid * part(image, 5) * ffn).astype(LOW)
        small_ref[6 + image : 7 + image, :] = column_sum(valid * ffn * upstream)
        normed, inverse = normalize(middle)
        grad_h2 = nt(gpre_ref[rows, :], up_w_ref[...])
        small_ref[2 + image : 3 + image, :] = column_sum(grad_h2)
        small_ref[4 + image : 5 + image, :] = column_sum(grad_h2 * normed)
        grad_mid = upstream + norm_back(grad_h2 * (1.0 + part(image, 4)), normed, inverse)
        grad_mid_ref[rows, :] = grad_mid
        small_ref[image : image + 1, :] = column_sum(valid * attn_ref[rows, :] * grad_mid)
        grad_attn = (valid * part(image, 2) * grad_mid).astype(LOW)
        h2_ref[rows, :] = grad_attn
        out_bias_grad = out_bias_grad + column_sum(grad_attn.astype(F32))
        grad_att_ref[rows, :] = nt(grad_attn, out_w_ref[...]).astype(LOW)
    small_ref[8:9, :] = out_bias_grad
    out_term = tn(att_ref[...], h2_ref[...])
    out_first = jnp.concatenate([out_term[:half, :half], out_term[half:, :half]], axis=1)
    out_second = jnp.concatenate([out_term[:half, half:], out_term[half:, half:]], axis=1)
    rows = slice(2 * width + ff_width // 2, 2 * width + ff_width // 2 + half)
    keep_ref[rows, :] = jnp.where(core == 0, out_first, out_second)
    send_ref[rows, :] = jnp.where(core == 0, out_second, out_first).astype(LOW)
    start = keep_ref.shape[0] + 16
    send_ref[start - 16 : start, :] = small_ref[...].astype(LOW)
    for image in range(image_count):
        rows = slice(start + image * half_len, start + (image + 1) * half_len)
        send_ref[rows, :] = output_ref[image, half_len:, :]


def backward_kernel(
    normed_ref,
    inverse_hbm,
    penalty_ref,
    qkv_w_ref,
    qkv_ref,
    h1_ref,
    grad_att_ref,
    grad_mid_ref,
    mod_ref,
    after_ref,
    grad_tokens_ref,
    keep_ref,
    send_ref,
    other_ref,
    small_ref,
    gqkv_ref,
    inverse_ref,
    sems,
):
    core = lax.axis_index("seq")
    copies = fetch([(inverse_hbm, inverse_ref)], sems)
    image_count, length, width = grad_tokens_ref.shape
    half_len = length // 2
    half = width // 2
    first, second = head_masks(length)
    for step in range(image_count * (HEADS // 2)):
        rows, lanes, queries, keys, values = attention_pair(
            step, qkv_ref, penalty_ref, length, width
        )
        image = step // (HEADS // 2)
        penalty = penalty_ref[image : image + 1, :]
        grad_att = grad_att_ref[rows, lanes(0)]
        grad_q = jnp.zeros((length, PAIR), F32)
        grad_k = jnp.zeros((length, PAIR), F32)
        grad_v = jnp.zeros((length, PAIR), F32)
        for mask in (first, second):
            own_queries = masked(queries, mask)
            own_grad = masked(grad_att, mask)
            probs = softmax_rows(own_queries, keys, penalty)
            grad_probs = nt(own_grad, values)
            dots = jnp.sum(probs * grad_probs, axis=-1, keepdims=True)
            grad_scores = (probs * (grad_probs - dots)).astype(LOW)
            grad_v = grad_v + tn(probs.astype(LOW), own_grad)
            grad_q = grad_q + nn(grad_scores, masked(keys, mask))
            grad_k = grad_k + tn(grad_scores, own_queries)
        gqkv_ref[rows, lanes(0)] = (grad_q * HEAD_DIM**-0.5).astype(LOW)
        gqkv_ref[rows, lanes(1)] = grad_k.astype(LOW)
        gqkv_ref[rows, lanes(2)] = grad_v.astype(LOW)

    def part(image, which):
        return mod_ref[image : image + 1, which * width : (which + 1) * width].astype(F32)

    small_ref[...] = jnp.zeros_like(small_ref)
    copies[0].wait()
    small_ref[4:5, :] = column_sum(gqkv_ref[:, :width].astype(F32))
    small_ref[5:6, :] = column_sum(gqkv_ref[:, 2 * width :].astype(F32))
    for image in range(image_count):
        rows = slice(image * length, (image + 1) * length)
        normed = normed_ref[rows, :]
        inverse = jnp.concatenate([inverse_ref[rows, :]] * (width // LANES), axis=1)
        grad_h1 = nt(gqkv_ref[rows, :], qkv_w_ref[...])
        small_ref[image : image + 1, :] = column_sum(grad_h1)
        small_ref[2 + image : 3 + image, :] = column_sum(grad_h1 * normed)
        grad_in = norm_back(grad_h1 * (1.0 + part(image, 1)), normed, inverse)
        grad_tokens_ref[image] = (grad_mid_ref[rows, :] + grad_in).astype(LOW)
    low_term = tn(h1_ref[...], gqkv_ref[:, :width])
    high_term = tn(h1_ref[...], gqkv_ref[:, 2 * width :])
    keep_ref[:width, :] = jnp.where(core == 0, low_term, high_term)
    pair = jnp.where(core == 0, high_term, low_term).astype(LOW)
    term = tn(h1_ref[...], gqkv_ref[:, width : 2 * width])
    low_unit = jnp.concatenate([term[:half, :half], term[half:, :half]], axis=1)
    high_unit = jnp.concatenate([term[:half, half:], term[half:, half:]], axis=1)
    keep_ref[width:, :] = jnp.where(core == 0, low_unit, high_unit)
    cut = width // 4 * 3
    send_ref[:cut, :] = pair[:cut]
    start = width - cut
    other_ref[:start, :] = pair[cut:]
    other_ref[start : start + half, :] = jnp.where(core == 0, high_unit, low_unit).astype(LOW)
    start += half
    other_ref[start : start + 8, :] = small_ref[...].astype(LOW)
    for index, (target, start) in enumerate(((send_ref, cut), (other_ref, start + 8))):
        target[start:, :] = grad_tokens_ref[index, half_len:, :]


def by_core(core, near, far):
    return [jnp.where(core == 0, near, far), jnp.where(core == 0, far, near)]


def split_kernel(
    keep_ref, recv_ref, small_ref, own_ref, one_ref, two_ref, three_ref, early_ref
):
    core = lax.axis_index("seq")
    width = keep_ref.shape[1]
    piece = width // 16
    long = 4 * piece
    start = keep_ref.shape[0]
    near = small_ref[...].astype(LOW).astype(F32)
    far = recv_ref[start : start + 16, :].astype(F32)
    first, second = by_core(core, near, far)
    mods = []
    for row in range(0, 6, 2):
        low_kind = [first[:2], second[:2]] if row == 0 else [jnp.zeros((4, width), F32)]
        high_kind = [first[row + 2 : row + 4], second[row + 2 : row + 4]]
        mods.append(
            jnp.where(
                core == 0, jnp.concatenate(low_kind, axis=0), jnp.concatenate(high_kind, axis=0)
            )
        )
    early_ref[...] = jnp.concatenate(
        mods + [first[8:14] + second[8:14], jnp.zeros((6, width), F32)], axis=0
    )
    lane = lax.broadcasted_iota(jnp.int32, (8, width), 1)
    ids = jnp.zeros((8, width), F32)
    for slot, block in enumerate((first[14:15], first[15:16], second[14:15], second[15:16])):
        ids = jnp.where(lane == slot, block, ids)
    for step, target in enumerate((own_ref, one_ref, two_ref, three_ref)):
        who = (lax.axis_index("dp") & 3) ^ step

        def move(start, size, to):
            rows = pl.ds(pl.multiple_of(start, 8), size)
            target[to : to + size, :] = (
                keep_ref[rows, :] + recv_ref[rows, :].astype(F32)
            ).astype(target.dtype)

        for z in range(4):
            for side in range(2):
                move(side * width + piece * (4 * z + who), piece, (2 * z + side) * piece)
        for z in range(2):
            move(2 * width + long * (4 * z + who), long, 8 * piece + z * long)
            move(2 * width + 8 * long + piece * (4 * z + who), piece, 16 * piece + z * piece)
        target[18 * piece :, :] = ids.astype(target.dtype)


def split_qkv_kernel(keep_ref, recv_ref, other_ref, small_ref, early_ref, *refs):
    core = lax.axis_index("seq")
    width = keep_ref.shape[1]
    piece = width // 16
    cut = width // 4 * 3
    near = small_ref[...].astype(LOW).astype(F32)
    start = keep_ref.shape[0] - cut
    far = other_ref[start : start + 8, :].astype(F32)
    first, second = by_core(core, near, far)
    early = early_ref[...]
    late = jnp.concatenate([first[0:2], second[0:2], first[2:4], second[2:4], early[:4]], axis=0)
    small = jnp.concatenate(
        [
            jnp.where(core == 0, late, early[:12]),
            early[12:18],
            first[4:6] + second[4:6],
            jnp.zeros((4, width), F32),
        ],
        axis=0,
    ).astype(LOW)
    total_ref = refs[-1]
    total_ref[:cut, :] = keep_ref[:cut, :] + recv_ref[:cut, :].astype(F32)
    total_ref[cut:, :] = keep_ref[cut:, :] + other_ref[:start, :].astype(F32)
    for step, target in enumerate(refs[-5:-1]):
        who = (lax.axis_index("dp") & 3) ^ step
        for z in range(6):
            start = width + piece * (4 * (z - 4) + who) if z >= 4 else piece * (4 * z + who)
            rows = pl.ds(pl.multiple_of(start, 8), piece)
            target[piece * z : piece * (z + 1), :] = total_ref[rows, :].astype(target.dtype)
        target[6 * piece :, :] = small.astype(target.dtype)


def summed(sources, rows):
    return sum((source[rows, :].astype(F32) for source in sources[1:]), sources[0][rows, :])


def fold_kernel(*refs):
    parts, after = refs[:4], refs[4]
    kept_ref, rest_ref, rest_small_ref = refs[5:8]
    sends = refs[8:11]
    total_ref, group_ref = refs[11:]
    width = total_ref.shape[1]
    piece = width // 16
    long = 4 * piece
    half = width // 2
    total_ref[...] = summed(parts, slice(0, 16 * piece))
    for step, part in enumerate(parts):
        group_ref[(lax.axis_index("dp") & 3) ^ step] = part[18 * piece :, :].astype(F32)
    kept_ref[...] = summed(parts, slice(16 * piece, 18 * piece))
    ids = [group_ref[q, 0:1] for q in range(4)] + [jnp.zeros((4, width), F32)]
    small = jnp.concatenate(ids, axis=0).astype(LOW)
    rest_small_ref[...] = small
    for step, target in enumerate((rest_ref,) + tuple(sends)):
        who = (lax.axis_index("dp") >> 2) ^ step
        rows = pl.ds(pl.multiple_of(2 * piece * who, 8), 2 * piece)
        target[: 2 * piece, :] = total_ref[rows, :].astype(target.dtype)
        rows = pl.ds(pl.multiple_of(8 * piece + long * (who % 2), 8), long)
        down = total_ref[rows, :]
        down = jnp.where(who < 2, down[:, :half], down[:, half:])
        down = jnp.concatenate([down[: 2 * piece], down[2 * piece :]], axis=1)
        target[2 * piece : 4 * piece, :] = down.astype(target.dtype)
        if step:
            target[4 * piece :, :] = small


def fold_qkv_kernel(*refs):
    parts, kept_ref = refs[:4], refs[4]
    rest_ref, rest_small_ref = refs[5:7]
    sends = refs[7:10]
    total_ref, late_ref = refs[10:]
    width = total_ref.shape[1]
    piece = width // 16
    half = width // 2
    total_ref[: 6 * piece, :] = summed(parts, slice(0, 6 * piece))
    total_ref[6 * piece :, :] = kept_ref[...]
    for step, part in enumerate(parts):
        late_ref[(lax.axis_index("dp") & 3) ^ step] = part[6 * piece :, :].astype(F32)
    rows = [late_ref[q, :12] for q in range(4)]
    rows.append(late_ref[0, 12:20] + late_ref[1, 12:20] + late_ref[2, 12:20] + late_ref[3, 12:20])
    small = jnp.concatenate(rows, axis=0).astype(LOW)
    rest_small_ref[...] = small
    for step, target in enumerate((rest_ref,) + tuple(sends)):
        who = (lax.axis_index("dp") >> 2) ^ step

        def side(start):
            value = total_ref[pl.ds(pl.multiple_of(piece * (start + who % 2), 8), piece), :]
            return jnp.where(who < 2, value[:, :half], value[:, half:])

        target[:piece, :] = jnp.concatenate([side(6), side(4)], axis=1).astype(target.dtype)
        pair = total_ref[pl.ds(pl.multiple_of(piece * who, 8), piece), :]
        target[piece : 2 * piece, :] = pair.astype(target.dtype)
        if step:
            target[2 * piece :, :] = small


def one_hot(ids, lead):
    place = lax.broadcasted_iota(jnp.int32, (lead.shape[1], ids.shape[1]), 0)
    wanted = (ids // GROUPS_PER_RANK) * 8 + ids % GROUPS_PER_RANK
    return jnp.where(place == wanted, 1.0, 0.0).astype(LOW)


def group_parts(silu_rows, own_groups, kinds, kind_of):
    zeros = jnp.zeros_like(kind_of, F32)
    blocks = [masked(silu_rows, kind_of == kind) for kind in kinds]
    rows = []
    for kind in kinds:
        for one in own_groups:
            rows.append(jnp.where((kind_of == kind) & one, 1.0, zeros))
    for kind in kinds:
        rows.append(jnp.where(kind_of == kind, 1.0, zeros))
    while len(rows) % 8:
        rows.append(zeros)
    return blocks, jnp.concatenate(rows, axis=0).astype(LOW)


def split_dot(values, weight):
    high = values.astype(LOW)
    low = (values - high.astype(F32)).astype(LOW)
    return nt(high, weight) + nt(low, weight)


def finish_kernel(
    own_ref,
    own_small_ref,
    one_ref,
    two_ref,
    three_ref,
    lead_ref,
    recv_one_ref,
    recv_two_ref,
    recv_other_ref,
    output_ref,
    grad_tokens_ref,
    output_to,
    grad_tokens_to,
    up_ref,
    down_ref,
    silu_ref,
    ids_ref,
    stack_ref,
    sems,
):
    core = lax.axis_index("seq")
    width = own_ref.shape[1]
    piece = width // 16
    half = width // 2
    slots, half_len = output_to.shape[:2]
    count = slots // 2
    pairs = []
    for index, source in enumerate((recv_two_ref, recv_other_ref)):
        slot = (1 - core) * count + index
        start = recv_one_ref.shape[0] - (count - index) * half_len
        pairs.append((recv_one_ref.at[pl.ds(start, half_len)], output_to.at[slot]))
        start = source.shape[0] - half_len
        pairs.append((source.at[pl.ds(start, half_len)], grad_tokens_to.at[slot]))
        slot = core * count + index
        pairs.append((output_ref.at[index, pl.ds(0, half_len)], output_to.at[slot]))
        pairs.append((grad_tokens_ref.at[index, pl.ds(0, half_len)], grad_tokens_to.at[slot]))
    copies = fetch(pairs, sems)
    parts = (own_ref, one_ref, two_ref, three_ref)
    total = summed(parts, slice(0, 4 * piece))
    up_ref[...] = jnp.concatenate([total[:piece], total[piece : 2 * piece]], axis=1)
    down = total[2 * piece :]
    down_ref[...] = jnp.concatenate([down[:, :half], down[:, half:]], axis=0)
    line = lax.axis_index("dp") >> 2
    smalls = (own_small_ref[...],) + tuple(part[4 * piece :, :] for part in parts[1:])
    for step, small in enumerate(smalls):
        stack_ref[line ^ step] = small[:, :LANES].astype(F32)
    stack = stack_ref[...].reshape(32, LANES).astype(LOW)
    count = 192
    row = lax.broadcasted_iota(jnp.int32, (32, count), 0)
    chip = lax.broadcasted_iota(jnp.int32, (32, count), 1) // 12
    spread = tn(stack, jnp.where(row == chip + 4 * (chip // 4), 1.0, 0.0).astype(LOW))[:8]
    slot = lax.broadcasted_iota(jnp.int32, (8, count), 0)
    wanted = lax.broadcasted_iota(jnp.int32, (8, count), 1) % 4
    ids = column_sum(jnp.where(slot == wanted, spread, 0.0)).astype(jnp.int32)
    ids_ref[...] = ids
    lead = lead_ref[...]
    silu_ref[...] = nn(lead, one_hot(ids, lead)).astype(LOW)
    for copy in copies:
        copy.wait()


def late_kernel(
    own_ref,
    own_small_ref,
    one_ref,
    two_ref,
    three_ref,
    silu_ref,
    ids_ref,
    ada_ref,
    out_ref,
    qkv_ref,
    ada_out_ref,
    own_sums_ref,
    send_ref,
    out_bias_ref,
    up_bias_ref,
    down_bias_ref,
    qv_ref,
    stack_ref,
    bias_ref,
):
    core = lax.axis_index("seq")
    width = own_ref.shape[1]
    piece = width // 16
    half = width // 2
    parts = (own_ref, one_ref, two_ref, three_ref)
    line = lax.axis_index("dp") >> 2
    smalls = (own_small_ref[...],) + tuple(part[2 * piece :, :] for part in parts[1:])
    for step, small in enumerate(smalls):
        stack_ref[line ^ step] = small[:48]
        bias_ref[line ^ step] = small[48:].astype(F32)
    stack = stack_ref[...].reshape(192, width)
    ids = ids_ref[...]
    item = lax.broadcasted_iota(jnp.int32, (1, 192), 1) % 12
    base = GROUPS_PER_RANK * lax.axis_index("dp")
    own = [ids == base + index for index in range(GROUPS_PER_RANK)]
    blocks, rows = group_parts(silu_ref[...], own, range(3), item // 4)
    sums = nn(rows, stack)
    for kind in range(3):
        ada_out_ref[:, kind * width : (kind + 1) * width] = nn(blocks[kind], stack)
    weight = ada_ref[:, pl.ds(pl.multiple_of(core * 3 * width, LANES), 3 * width)]
    own_sum = jnp.concatenate(
        [
            jnp.concatenate([sums[2 * kind : 2 * kind + 2] for kind in range(3)], axis=1),
            jnp.zeros((6, 3 * width), F32),
        ],
        axis=0,
    )
    cond = split_dot(own_sum, weight)
    low_cond, high_cond = cond[:2, :half], cond[:2, half:]
    kept = jnp.where(core == 0, low_cond, high_cond)
    sent = jnp.where(core == 0, high_cond, low_cond)
    zeros = jnp.zeros((2, half), F32)
    pad = jnp.zeros((3, width), F32)
    own_sums_ref[...] = jnp.concatenate(
        [jnp.concatenate([kept, zeros], axis=1), sums[6:9], pad], axis=0
    )
    send_ref[...] = jnp.concatenate(
        [jnp.concatenate([sent, zeros], axis=1), sums[6:9], pad], axis=0
    )
    bias = bias_ref[0] + bias_ref[1] + bias_ref[2] + bias_ref[3]
    out_bias_ref[...] = bias[0:1].reshape(width)
    up_bias_ref[...] = jnp.concatenate([bias[1 + row : 2 + row] for row in range(4)], axis=1).reshape(
        4 * width
    )
    down_bias_ref[...] = bias[5:6].reshape(width)
    qv_ref[...] = bias[6:8]
    total = summed(parts, slice(0, 2 * piece))
    out_ref[...] = total[:piece, :half]
    unit, pair = total[:piece, half:], total[piece:]
    qkv_ref[...] = jnp.where(
        core == 0,
        jnp.concatenate([pair, unit], axis=1),
        jnp.concatenate([unit, pair], axis=1),
    )


def final_kernel(own_ref, recv_ref, own_cond_ref, cond_ref, bias_ref):
    core = lax.axis_index("seq")
    width = own_ref.shape[1]
    half = width // 2
    near, far = own_ref[...], recv_ref[...]
    values = own_cond_ref[...].astype(F32)
    values = jnp.where(core == 0, values[:, :half], values[:, half:])
    gate = 1.0 / (1.0 + jnp.exp(-values))
    cond_ref[...] = (near[:2, :half] + far[:2, :half]) * (gate * (1.0 + values * (1.0 - gate)))
    rows = [block[row : row + 1] for block in by_core(core, near, far) for row in range(2, 5)]
    bias_ref[...] = jnp.concatenate(rows, axis=1).reshape(6 * width)


def silu_slope(values):
    sigmoid_val = jax.nn.sigmoid(values)
    return sigmoid_val * (1.0 + values * (1.0 - sigmoid_val))


def swap_cores(values):
    return lax.ppermute(values, "seq", CORE_SWAP)


def pick(core, first, second):
    return jnp.where(core == 0, first, second)


def to_patches(images, far, core):
    half_len = images.shape[1] // 2
    return pick(
        core,
        jnp.concatenate([images[:, :half_len], far], axis=0),
        jnp.concatenate([far, images[:, :half_len]], axis=0),
    )


def call(kernel, name, shapes, scratch, limit, spaces, *operands, aliases=None):
    chosen = {
        "s": pl.BlockSpec(memory_space=pltpu.SMEM),
        "v": pl.BlockSpec(memory_space=pltpu.VMEM),
        "V": pl.BlockSpec(memory_space=pltpu.VMEM),
        "a": pl.BlockSpec(memory_space=pl.ANY),
        "h": pl.BlockSpec(memory_space=pltpu.HBM),
    }
    pinned = {"h": pltpu.HBM, "V": pltpu.VMEM}
    into, out_of = spaces
    operands = [
        pltpu.with_memory_space_constraint(item, pinned[kind]) if kind in pinned else item
        for kind, item in zip(into, operands)
    ]
    return pl.pallas_call(
        kernel,
        out_shape=tuple(
            pinned.get(kind, jax.ShapeDtypeStruct)(shape, dtype)
            for kind, (shape, dtype) in zip(out_of, shapes)
        ),
        in_specs=[chosen[kind] for kind in into],
        out_specs=[chosen[kind] for kind in out_of],
        scratch_shapes=scratch,
        compiler_params=pltpu.CompilerParams(vmem_limit_bytes=limit << 20),
        cost_estimate=pl.CostEstimate(flops=1, bytes_accessed=1, transcendentals=0),
        input_output_aliases=aliases or {},
        name=name,
    )(*operands)


def rank_swap(values, step, count):
    return lax.ppermute(values, "dp", [(rank, rank ^ step) for rank in range(count)])


def owner_total(term, dp_count):
    blocks = term.astype(LOW).reshape(dp_count, term.shape[0] // dp_count, term.shape[1])
    return jnp.sum(lax.all_to_all(blocks, "dp", 0, 0, tiled=True).astype(F32), axis=0)


def general_tail(
    core, dp_count, dp_rank, sides, smalls, heads, cond_rows, cond, own_ids, ada_weight
):
    highest = lax.Precision.HIGHEST
    width, mod_width = ada_weight.shape
    half = width // 2
    (keep_one, send_one), (keep_two, send_two, send_other) = sides
    output, grad_tokens = heads
    small_one, small_two = smalls
    half_len = output.shape[1] // 2
    recv_one = swap_cores(send_one)
    first_sum = keep_one + recv_one[: keep_one.shape[0]].astype(F32)
    recv_two, recv_other = swap_cores(send_two), swap_cores(send_other)
    cut = width // 4 * 3
    second_sum = keep_two + jnp.concatenate(
        [recv_two[:cut], recv_other[: keep_two.shape[0] - cut]], axis=0
    ).astype(F32)
    output_far = recv_one[keep_one.shape[0] + 16 :].reshape(-1, half_len, width)
    grad_far = jnp.stack([item[-half_len:] for item in (recv_two, recv_other)])
    ff_half = first_sum.shape[0] - 2 * width - half
    up = jnp.concatenate([first_sum[:width], first_sum[width : 2 * width]], axis=1)
    down = first_sum[2 * width : 2 * width + ff_half]
    down = jnp.concatenate([down[:, :half], down[:, half:]], axis=0)
    out = first_sum[2 * width + ff_half :]
    out = jnp.concatenate([out[:, :half], out[:, half:]], axis=0)
    pair, unit = second_sum[:width], second_sum[width:]
    unit = jnp.concatenate([unit[:, :half], unit[:, half:]], axis=0)
    qkv = pick(
        core, jnp.concatenate([pair, unit], axis=1), jnp.concatenate([unit, pair], axis=1)
    )
    sums = [owner_total(term, dp_count) for term in (qkv, out, up, down)]
    image_grad = jnp.concatenate(
        [small_two[0:2], small_two[2:4], small_one[0:2], small_one[2:4], small_one[4:6], small_one[6:8]],
        axis=1,
    )
    biases = jnp.concatenate([small_two[4:6], small_one[8:14]], axis=0)
    marks = jnp.broadcast_to(own_ids.astype(F32)[:, None], (own_ids.shape[0], width))
    packed = jnp.concatenate([image_grad.reshape(-1, width), biases, marks], axis=0)
    gathered = lax.all_to_all(
        jnp.broadcast_to(packed[None], (2 * dp_count,) + packed.shape),
        ("dp", "seq"),
        0,
        0,
        tiled=True,
    )
    grad_rows = gathered[:, :12].reshape(-1, mod_width)
    bias_sums = jnp.sum(gathered[:, 12:20], axis=0)
    all_ids = gathered[:, 20:, 0].reshape(-1).astype(jnp.int32)
    group_count = cond_rows.shape[0]
    all_hot = (all_ids[:, None] == jnp.arange(group_count, dtype=jnp.int32)[None, :]).astype(F32)
    group_grad = jnp.dot(all_hot.T, grad_rows, precision=highest)
    own_rows = width // dp_count
    silu_rows = lax.reduce_precision(jax.nn.silu(cond_rows.astype(F32)), 8, 7)
    silu_part = lax.dynamic_slice_in_dim(silu_rows, dp_rank * own_rows, own_rows, 1)
    grad_half = pick(core, group_grad[:, : mod_width // 2], group_grad[:, mod_width // 2 :])
    ada_sum = jnp.dot(silu_part.T, grad_half, precision=highest)
    own_grad = lax.dynamic_slice_in_dim(
        group_grad, dp_rank * GROUPS_PER_RANK, GROUPS_PER_RANK, 0
    )
    ada_half = lax.dynamic_slice_in_dim(ada_weight, core * half, half, 0).astype(F32)
    cond_half = pick(core, cond[:, :half], cond[:, half:]).astype(F32)
    grad_cond = silu_slope(cond_half) * jnp.dot(own_grad, ada_half.T, precision=highest)
    return (
        to_patches(output, output_far, core),
        to_patches(grad_tokens, grad_far, core),
        grad_cond,
        sums[0],
        bias_sums[:2],
        sums[1],
        bias_sums[2],
        sums[2],
        bias_sums[3:7].reshape(-1),
        sums[3],
        bias_sums[7],
        ada_sum,
        jnp.sum(grad_rows, axis=0),
    )


def body(
    tokens,
    cotangent,
    cond,
    group_ids,
    image_counts,
    patch_mask,
    qkv_weight,
    qv_bias,
    out_weight,
    out_bias,
    up_weight,
    up_bias,
    down_weight,
    down_bias,
    ada_weight,
    ada_bias,
):
    slot_count, half_len, width = tokens.shape
    ff_width = up_weight.shape[1]
    mod_width = ada_weight.shape[1]
    dp_count = lax.axis_size("dp")
    core = lax.axis_index("seq").astype(jnp.int32)
    dp_rank = lax.axis_index("dp").astype(jnp.int32)
    image_count = slot_count // 2
    length = 2 * half_len
    row_count = image_count * length
    half = width // 2
    piece = width // dp_count
    fast = dp_count == 16 and not GENERAL
    cond_blocks = lax.all_to_all(
        jnp.broadcast_to(cond[None], (dp_count,) + cond.shape), "dp", 0, 0, tiled=True
    )
    tokens_far = swap_cores(tokens)
    cot_far = swap_cores(cotangent)
    image_shape = (image_count, length, width)
    packed_rows = 2 * width + ff_width // 2 + half
    vmem = pltpu.VMEM
    (
        images,
        normed,
        penalty,
        hot,
        marks,
        qkv_b_row,
        out_b_row,
        up_b_row,
        down_b_row,
        ada_weight_near,
        ada_b_row,
        cot_images,
        inverse,
    ) = call(
        load_kernel,
        "load",
        (
            (image_shape, LOW),
            ((row_count, width), F32),
            ((8, length), F32),
            ((8, 8 * dp_count), LOW),
            ((8, width), F32),
            ((1, 3 * width), F32),
            ((1, width), F32),
            ((1, ff_width), F32),
            ((1, width), F32),
            (ada_weight.shape, LOW),
            ((1, mod_width), F32),
            (image_shape, LOW),
            ((row_count, LANES), F32),
        ),
        [
            vmem(image_shape, LOW),
            vmem((row_count, LANES), F32),
            pltpu.SMEM(group_ids.shape, jnp.int32),
            pltpu.SMEM(image_counts.shape, jnp.int32),
            vmem(patch_mask.shape, jnp.int32),
            vmem(qv_bias.shape, LOW),
            vmem(out_bias.shape, LOW),
            vmem(up_bias.shape, LOW),
            vmem(down_bias.shape, LOW),
            vmem(ada_bias.shape, LOW),
            pltpu.SemaphoreType.DMA((9 + 4 * image_count,)),
        ],
        12,
        ("hVhaha" + "h" * 7, "VV" + "V" * 9 + "hh"),
        tokens,
        tokens_far,
        cotangent,
        cot_far,
        group_ids,
        image_counts,
        patch_mask,
        qv_bias,
        out_bias,
        up_bias,
        down_bias,
        ada_weight,
        ada_bias,
    )
    (
        output,
        qkv,
        h1,
        grad_att,
        grad_mid,
        image_mod,
        lead,
        qkv_weight_near,
        keep_one,
        send_one,
        small_one,
    ) = call(
        partial(forward_kernel, piece if fast else 0),
        "forward_and_ffn_back",
        (
            (image_shape, LOW),
            ((row_count, 3 * width), LOW),
            ((row_count, width), LOW),
            ((row_count, width), LOW),
            ((row_count, width), F32),
            ((8, mod_width), LOW),
            ((24, 8 * dp_count), LOW),
            (qkv_weight.shape, LOW),
            ((packed_rows, width), F32),
            ((packed_rows + 16 + row_count // 2, width), LOW),
            ((16, width), F32),
        ),
        [
            vmem((8 * dp_count, width), F32),
            vmem((width, 8 * dp_count), F32),
            vmem((row_count, width), LOW),
            vmem((row_count, width), F32),
            vmem((row_count, width), F32),
            vmem((row_count, width), LOW),
            vmem((row_count, width), LOW),
            vmem((row_count, ff_width), LOW),
            vmem((row_count, ff_width), LOW),
            vmem((row_count, LANES), F32),
            vmem(image_shape, LOW),
            vmem(out_weight.shape, LOW),
            vmem(up_weight.shape, LOW),
            vmem(down_weight.shape, LOW),
            pltpu.SemaphoreType.DMA((5,)),
        ],
        30,
        ("V" * 12 + "h" * 5, "V" * 11),
        cond_blocks,
        images,
        normed,
        penalty,
        hot,
        marks,
        qkv_b_row,
        out_b_row,
        up_b_row,
        down_b_row,
        ada_weight_near,
        ada_b_row,
        cot_images,
        qkv_weight,
        out_weight,
        up_weight,
        down_weight,
    )

    def attention_back(after):
        return call(
            backward_kernel,
            "attention_back",
            (
                (image_shape, LOW),
                ((width + half, width), F32),
                ((width // 4 * 3 + half_len, width), LOW),
                ((width // 4 + half + 8 + half_len, width), LOW),
                ((8, width), F32),
            ),
            [
                vmem((row_count, 3 * width), LOW),
                vmem((row_count, LANES), F32),
                pltpu.SemaphoreType.DMA((1,)),
            ],
            24,
            ("VhVVVVVVVa", "VVVVV"),
            normed,
            inverse,
            penalty,
            qkv_weight_near,
            qkv,
            h1,
            grad_att,
            grad_mid,
            image_mod,
            after,
        )

    if not fast:
        grad_tokens, keep_two, send_two, send_other, small_two = attention_back(small_one)
        own_ids = lax.dynamic_slice_in_dim(group_ids, core * image_count, image_count, 0)
        return general_tail(
            core,
            dp_count,
            dp_rank,
            ((keep_one, send_one), (keep_two, send_two, send_other)),
            (small_one, small_two),
            (output, grad_tokens),
            cond_blocks.reshape(-1, width),
            cond,
            own_ids,
            ada_weight,
        )

    recv_one = swap_cores(send_one)
    split_rows = 18 * piece + 8
    own_part, *sent_parts, early = call(
        split_kernel,
        "split_plane",
        (((split_rows, width), F32),)
        + (((split_rows, width), LOW),) * 3
        + (((24, width), F32),),
        [],
        16,
        ("VVV", "VVVVV"),
        keep_one,
        recv_one,
        small_one,
    )
    near_parts = [rank_swap(item, step + 1, 16) for step, item in enumerate(sent_parts)]
    grad_tokens, keep_two, send_two, send_other, small_two = attention_back(sent_parts[2])
    recv_two, recv_other = swap_cores(send_two), swap_cores(send_other)
    split_rows = 6 * piece + 24
    own_qkv, *sent_qkv = call(
        split_qkv_kernel,
        "split_qkv_plane",
        (((split_rows, width), F32),) + (((split_rows, width), LOW),) * 3,
        [vmem((width + half, width), F32)],
        16,
        ("VVVVVaaa", "VVVV"),
        keep_two,
        recv_two,
        recv_other,
        small_two,
        early,
        *near_parts,
    )
    near_qkv = [rank_swap(item, step + 1, 16) for step, item in enumerate(sent_qkv)]
    line_rows = 4 * piece + 8
    kept_rows, rest, rest_ids, *lines = call(
        fold_kernel,
        "fold_plane",
        (((2 * piece, width), F32), ((4 * piece, width), F32), ((8, width), LOW))
        + (((line_rows, width), LOW),) * 3,
        [vmem((16 * piece, width), F32), vmem((4, 8, width), F32)],
        16,
        ("VVVVa", "VVVVVV"),
        own_part,
        *near_parts,
        sent_qkv[2],
    )
    lines = [rank_swap(item, 4 * (step + 1), 16) for step, item in enumerate(lines)]
    line_rows = 2 * piece + 56
    rest_qkv, rest_small, *lines_qkv = call(
        fold_qkv_kernel,
        "fold_qkv_plane",
        (((2 * piece, width), F32), ((56, width), LOW)) + (((line_rows, width), LOW),) * 3,
        [vmem((8 * piece, width), F32), vmem((4, 24, width), F32)],
        16,
        ("VVVVV", "VVVVV"),
        own_qkv,
        *near_qkv,
        kept_rows,
    )
    lines_qkv = [rank_swap(item, 4 * (step + 1), 16) for step, item in enumerate(lines_qkv)]
    output, grad_tokens, up_sum, down_sum, silu_rows, all_ids = call(
        finish_kernel,
        "finish_line",
        (
            (tokens.shape, LOW),
            (tokens.shape, LOW),
            ((piece, ff_width // 2), F32),
            ((4 * piece, half), F32),
            ((piece, 192), LOW),
            ((1, 192), jnp.int32),
        ),
        [vmem((4, 8, LANES), F32), pltpu.SemaphoreType.DMA((4 * image_count,))],
        16,
        ("V" * 11, "hhvvVV"),
        rest,
        rest_ids,
        *lines,
        lead,
        recv_one,
        recv_two,
        recv_other,
        output,
        grad_tokens,
    )
    (
        out_sum,
        qkv_sum,
        ada_sum,
        own_sums,
        send_sums,
        out_bias_sum,
        up_bias_sum,
        down_bias_sum,
        qv_sum,
    ) = call(
        late_kernel,
        "late_groups",
        (
            ((piece, half), F32),
            ((piece, 3 * half), F32),
            ((piece, mod_width // 2), F32),
            ((8, width), F32),
            ((8, width), F32),
            ((width,), F32),
            ((ff_width,), F32),
            ((width,), F32),
            ((2, width), F32),
        ),
        [vmem((4, 48, width), LOW), vmem((4, 8, width), F32)],
        16,
        ("V" * 8, "vvvVVvvvv"),
        rest_qkv,
        rest_small,
        *lines_qkv,
        silu_rows,
        all_ids,
        ada_weight_near,
    )
    grad_cond, ada_bias_sum = call(
        final_kernel,
        "final_groups",
        (((GROUPS_PER_RANK, half), F32), ((mod_width,), F32)),
        [],
        16,
        ("VVv", "vv"),
        own_sums,
        swap_cores(send_sums),
        cond,
    )
    return (
        output,
        grad_tokens,
        grad_cond,
        qkv_sum,
        qv_sum,
        out_sum,
        out_bias_sum,
        up_sum,
        up_bias_sum,
        down_sum,
        down_bias_sum,
        ada_sum,
        ada_bias_sum,
    )


def solution(mesh):
    placed = (
        P("dp", "seq", None),
        P("dp", "seq", None),
        P("dp", None),
        P("dp"),
        P("dp"),
        P("dp", None),
        P(),
        P(),
        P(),
        P(),
        P(),
        P(),
        P(),
        P(),
        P(),
        P(),
    )
    return jax.shard_map(
        body,
        mesh=mesh,
        in_specs=placed,
        out_specs=(
            P("dp", "seq", None),
            P("dp", "seq", None),
            P("dp", "seq"),
            P("dp", "seq"),
            P(),
            P("dp", "seq"),
            P(),
            P("dp", "seq"),
            P(),
            P("dp", "seq"),
            P(),
            P("dp", "seq"),
            P(),
        ),
        check_vma=False,
    )
```

```python
from functools import partial

import jax
import jax.numpy as jnp
from jax import lax
from jax.experimental import pallas as pl
from jax.experimental.pallas import tpu as pltpu
from jax.sharding import PartitionSpec as P

HEADS = 6
HEAD_DIM = 64
PAIR = 2 * HEAD_DIM
CORE_SWAP = ((0, 1), (1, 0))
CHUNK = 256
LANES = 128
GROUPS_PER_RANK = 2
GENERAL = False
PIECE_ROWS = 288
F32 = jnp.float32
LOW = jnp.bfloat16


def nn(left, right):
    return lax.dot_general(left, right, (((1,), (0,)), ((), ())), preferred_element_type=F32)


def nt(left, right):
    return lax.dot_general(left, right, (((1,), (1,)), ((), ())), preferred_element_type=F32)


def tn(left, right):
    return lax.dot_general(left, right, (((0,), (0,)), ((), ())), preferred_element_type=F32)


def normalize(values):
    center = values - jnp.mean(values, axis=-1, keepdims=True)
    spread = jnp.mean(center * center, axis=-1, keepdims=True)
    inverse = lax.rsqrt(spread + 1e-06)
    return center * inverse, inverse


def norm_back(grad, normed, inverse):
    return inverse * (
        grad
        - jnp.mean(grad, axis=-1, keepdims=True)
        - normed * jnp.mean(grad * normed, axis=-1, keepdims=True)
    )


def column_sum(values):
    return jnp.sum(values, axis=0, keepdims=True)


def head_masks(rows):
    lane = lax.broadcasted_iota(jnp.int32, (rows, PAIR), 1)
    return lane < HEAD_DIM, lane >= HEAD_DIM


def masked(values, mask):
    return jnp.where(mask, values, jnp.zeros_like(values))


def softmax_rows(queries, keys, penalty):
    scores = nt(queries, keys) + penalty
    exps = jnp.exp(scores - jnp.max(scores, axis=-1, keepdims=True))
    return exps / jnp.sum(exps, axis=-1, keepdims=True)


def fetch(pairs, sems):
    copies = []
    for index, (source, target) in enumerate(pairs):
        copy = pltpu.make_async_copy(source, target, sems.at[index])
        copy.start()
        copies.append(copy)
    return copies


def own_images(near_ref, far_ref, target_ref, first_image):
    half_len = near_ref.shape[1]
    pairs = []
    for image in range(target_ref.shape[0]):
        slot = first_image + image
        pairs.append((near_ref.at[slot], target_ref.at[image, pl.ds(0, half_len)]))
        pairs.append((far_ref.at[slot], target_ref.at[image, pl.ds(half_len, half_len)]))
    return pairs


def own_marks(mask_ref, counts_ref, core, image, image_count, half_len):
    slot = core * image_count + image
    live = jnp.where(slot < counts_ref[0], 1.0, 0.0)
    marks = mask_ref[pl.ds(slot, 1), :].astype(F32) * live
    low_marks, high_marks = marks[:, :half_len], marks[:, half_len:]
    return jnp.concatenate(
        [
            jnp.where(core == 0, low_marks, high_marks),
            jnp.where(core == 0, high_marks, low_marks),
        ],
        axis=1,
    )


def as_row(ref):
    return ref[...].astype(F32).reshape(1, ref.shape[0])


def load_kernel(
    tokens_hbm,
    tokens_far_ref,
    ids_hbm,
    counts_hbm,
    mask_hbm,
    qv_b_hbm,
    out_b_hbm,
    up_b_hbm,
    down_b_hbm,
    ada_w_hbm,
    ada_b_hbm,
    images_ref,
    penalty_ref,
    hot_ref,
    marks_ref,
    qkv_b_ref,
    out_b_ref,
    up_b_ref,
    down_b_ref,
    ada_w_ref,
    ada_b_ref,
    ids_ref,
    counts_ref,
    mask_ref,
    qv_b_ref,
    out_b_raw,
    up_b_raw,
    down_b_raw,
    ada_b_raw,
    sems,
):
    core = lax.axis_index("seq")
    image_count, length, width = images_ref.shape
    half_len = length // 2
    first_image = core * image_count
    copies = fetch(
        [
            (ids_hbm, ids_ref),
            (counts_hbm, counts_ref),
            (mask_hbm, mask_ref),
            (qv_b_hbm, qv_b_ref),
            (out_b_hbm, out_b_raw),
            (up_b_hbm, up_b_raw),
            (down_b_hbm, down_b_raw),
            (ada_b_hbm, ada_b_raw),
            (ada_w_hbm, ada_w_ref),
        ]
        + own_images(tokens_hbm, tokens_far_ref, images_ref, first_image),
        sems,
    )
    for copy in copies[:8]:
        copy.wait()
    row = lax.broadcasted_iota(jnp.int32, hot_ref.shape, 0)
    column = lax.broadcasted_iota(jnp.int32, hot_ref.shape, 1)
    lane = lax.broadcasted_iota(jnp.int32, marks_ref.shape, 1)
    hot = jnp.zeros(hot_ref.shape, F32)
    marks = jnp.zeros(marks_ref.shape, F32)
    for slot in range(2 * image_count):
        marks = jnp.where(lane == slot, ids_ref[slot].astype(F32), marks)
    marks_ref[...] = marks
    penalty_ref[...] = jnp.zeros_like(penalty_ref)
    for image in range(image_count):
        group = ids_ref[first_image + image]
        place = 8 * (group // GROUPS_PER_RANK) + group % GROUPS_PER_RANK
        hot = jnp.where((row == image) & (column == place), 1.0, hot)
        own = own_marks(mask_ref, counts_ref, core, image, image_count, half_len)
        penalty_ref[image : image + 1, :] = (own - 1.0) * 30000.0
    hot_ref[...] = hot.astype(LOW)
    qkv_b_ref[...] = jnp.concatenate(
        [qv_b_ref[0:1, :], jnp.zeros((1, width), LOW), qv_b_ref[1:2, :]], axis=1
    ).astype(F32)
    for raw, target in (
        (out_b_raw, out_b_ref),
        (up_b_raw, up_b_ref),
        (down_b_raw, down_b_ref),
        (ada_b_raw, ada_b_ref),
    ):
        target[...] = as_row(raw)
    for copy in copies[8:]:
        copy.wait()


def attention_pair(step, qkv_ref, penalty_ref, length, width):
    image, pair = divmod(step, HEADS // 2)
    rows = slice(image * length, (image + 1) * length)

    def lanes(which):
        start = which * width + pair * PAIR
        return slice(start, start + PAIR)

    queries = qkv_ref[rows, lanes(0)] * jnp.asarray(HEAD_DIM**-0.5, LOW)
    return rows, lanes, queries, qkv_ref[rows, lanes(1)], qkv_ref[rows, lanes(2)]


def image_rows(image, length):
    return slice(image * length, (image + 1) * length)


def mod_part(mod_ref, image, which, width):
    return mod_ref[image : image + 1, which * width : (which + 1) * width].astype(F32)


def wide_column(column_ref, rows, width):
    return jnp.concatenate([column_ref[rows, :]] * (width // LANES), axis=1)


def forward_kernel(
    lead_rows,
    cond_ref,
    images_ref,
    cot_far_ref,
    penalty_ref,
    hot_ref,
    qkv_b_ref,
    out_b_ref,
    up_b_ref,
    ada_w_ref,
    ada_b_ref,
    cot_hbm,
    qkv_w_hbm,
    out_w_hbm,
    up_w_hbm,
    down_w_hbm,
    qkv_ref,
    h1_ref,
    normed_ref,
    inverse_ref,
    mod_ref,
    lead_ref,
    att_ref,
    mid_ref,
    attn_ref,
    act_ref,
    gpre_ref,
    valid_ref,
    cot_ref,
    qkv_w_ref,
    out_w_ref,
    up_w_ref,
    down_w_ref,
    keep_ref,
    send_ref,
    small_ref,
    cond_rows_ref,
    turned_ref,
    h2_ref,
    gffn_ref,
    sems,
):
    core = lax.axis_index("seq")
    image_count, length, width = images_ref.shape
    half_len = length // 2
    half = width // 2
    ff_width = up_w_ref.shape[1]
    copies = fetch(
        [
            (qkv_w_hbm, qkv_w_ref),
            (out_w_hbm, out_w_ref),
            (up_w_hbm, up_w_ref),
            (down_w_hbm, down_w_ref),
        ]
        + own_images(cot_hbm, cot_far_ref, cot_ref, core * image_count),
        sems,
    )
    block_count, block_rows = cond_ref.shape[:2]
    cond_rows_ref[...] = jnp.zeros_like(cond_rows_ref)
    for block in range(block_count):
        cond_rows_ref[8 * block : 8 * block + block_rows, :] = cond_ref[block].astype(F32)
    cond = cond_rows_ref[...]
    silu = cond / (1.0 + jnp.exp(-cond))
    image_silu = nn(hot_ref[...], silu.astype(LOW)).astype(LOW)
    mod_ref[...] = (nn(image_silu, ada_w_ref[...]) + ada_b_ref[...]).astype(LOW)

    def part(image, which):
        return mod_part(mod_ref, image, which, width)

    copies[0].wait()
    for image in range(image_count):
        rows = image_rows(image, length)
        normed, inverse = normalize(images_ref[image].astype(F32))
        normed_ref[rows, :] = normed
        inverse_ref[rows, :] = jnp.broadcast_to(inverse, (length, LANES))
        marks = jnp.where(penalty_ref[image : image + 1, :] < 0.0, 0.0, 1.0)
        valid_ref[rows, :] = jnp.broadcast_to(marks, (LANES, length)).T
        h1 = (normed * (1.0 + part(image, 1)) + part(image, 0)).astype(LOW)
        h1_ref[rows, :] = h1
        qkv_ref[rows, :] = (nn(h1, qkv_w_ref[...]) + qkv_b_ref[...]).astype(LOW)

    first, second = head_masks(length)
    for step in range(image_count * (HEADS // 2)):
        rows, lanes, queries, keys, values = attention_pair(
            step, qkv_ref, penalty_ref, length, width
        )
        image = step // (HEADS // 2)
        penalty = penalty_ref[image : image + 1, :]
        total = jnp.zeros((length, PAIR), F32)
        for mask in (first, second):
            probs = softmax_rows(masked(queries, mask), keys, penalty).astype(LOW)
            total = total + nn(probs, masked(values, mask))
        att_ref[rows, lanes(0)] = total.astype(LOW)

    for copy in copies[1:]:
        copy.wait()
    if lead_rows:
        turned_ref[...] = silu.T
        start = pl.multiple_of(lax.axis_index("dp") * lead_rows, 8)
        lead_ref[...] = turned_ref[pl.ds(start, lead_rows), :].astype(LOW)
    else:
        lead_ref[...] = jnp.zeros_like(lead_ref)
    small_ref[...] = jnp.zeros_like(small_ref)
    down_bias_grad = jnp.zeros((1, width), F32)
    for image in range(image_count):
        rows = image_rows(image, length)
        valid = wide_column(valid_ref, rows, width)
        attn = nn(att_ref[rows, :], out_w_ref[...]) + out_b_ref[...]
        attn_ref[rows, :] = attn
        middle = images_ref[image].astype(F32) + valid * part(image, 2) * attn
        mid_ref[rows, :] = middle
        normed, _ = normalize(middle)
        h2_ref[rows, :] = (normed * (1.0 + part(image, 4)) + part(image, 3)).astype(LOW)
        grad_ffn = (valid * part(image, 5) * cot_ref[image].astype(F32)).astype(LOW)
        gffn_ref[rows, :] = grad_ffn
        down_bias_grad = down_bias_grad + column_sum(grad_ffn.astype(F32))
    small_ref[13:14, :] = down_bias_grad

    for chunk in range(ff_width // CHUNK):
        columns = slice(chunk * CHUNK, (chunk + 1) * CHUNK)
        up_w = up_w_ref[:, columns]
        down_w = down_w_ref[columns, :]
        bias = jnp.zeros((1, CHUNK), F32)
        for image in range(image_count):
            rows = image_rows(image, length)
            pre = nn(h2_ref[rows, :], up_w) + up_b_ref[:, columns]
            square = pre * pre
            inner = jnp.tanh(pre * (0.7978845608028654 + 0.035677408136300125 * square))
            cdf = 0.5 * inner + 0.5
            act_ref[rows, columns] = (pre * cdf).astype(LOW)
            slope = 0.5 * (pre * (0.7978845608028654 + 0.10703222440890037 * square)) * (
                1.0 - inner * inner
            ) + cdf
            grad_pre = (nt(gffn_ref[rows, :], down_w) * slope).astype(LOW)
            gpre_ref[rows, columns] = grad_pre
            bias = bias + column_sum(grad_pre.astype(F32))
        for tile in range(CHUNK // LANES):
            start = chunk * CHUNK + tile * LANES
            small_ref[9 + start // width : 10 + start // width, start % width : start % width + LANES] = (
                bias[:, tile * LANES : (tile + 1) * LANES]
            )

    first_half = gffn_ref[:, :half]
    second_half = gffn_ref[:, half:]
    gffn_keep = jnp.where(core == 0, first_half, second_half)
    gffn_send = jnp.where(core == 0, second_half, first_half)
    side_chunks = ff_width // CHUNK // 2
    for step in range(side_chunks):
        low = slice(step * CHUNK, (step + 1) * CHUNK)
        high = slice((step + side_chunks) * CHUNK, (step + side_chunks + 1) * CHUNK)
        up_low = tn(h2_ref[...], gpre_ref[:, low])
        up_high = tn(h2_ref[...], gpre_ref[:, high])
        up_keep = jnp.where(core == 0, up_low, up_high)
        up_send = jnp.where(core == 0, up_high, up_low).astype(LOW)
        for tile in range(CHUNK // LANES):
            start = step * CHUNK + tile * LANES
            rows = slice(start // width * width, (start // width + 1) * width)
            columns = slice(start % width, start % width + LANES)
            keep_ref[rows, columns] = up_keep[:, tile * LANES : (tile + 1) * LANES]
            send_ref[rows, columns] = up_send[:, tile * LANES : (tile + 1) * LANES]
        rows = slice(2 * width + step * CHUNK, 2 * width + (step + 1) * CHUNK)
        for target, side in ((keep_ref, gffn_keep), (send_ref, gffn_send)):
            target[rows, :] = jnp.concatenate(
                [tn(act_ref[:, low], side), tn(act_ref[:, high], side)], axis=1
            ).astype(target.dtype)


def finish_forward_kernel(
    mod_ref,
    att_ref,
    mid_ref,
    attn_ref,
    act_ref,
    gpre_ref,
    valid_ref,
    cot_ref,
    out_w_ref,
    up_w_ref,
    down_w_ref,
    down_b_ref,
    early_ref,
    output_ref,
    grad_att_ref,
    grad_mid_ref,
    keep_ref,
    send_ref,
    small_ref,
    gattn_ref,
):
    core = lax.axis_index("seq")
    image_count, length, width = cot_ref.shape
    half_len = length // 2
    half = width // 2
    small_ref[...] = early_ref[...]

    def part(image, which):
        return mod_part(mod_ref, image, which, width)

    out_bias_grad = jnp.zeros((1, width), F32)
    for image in range(image_count):
        rows = image_rows(image, length)
        valid = wide_column(valid_ref, rows, width)
        upstream = cot_ref[image].astype(F32)
        middle = mid_ref[rows, :]
        ffn = nn(act_ref[rows, :], down_w_ref[...]) + down_b_ref[...]
        output_ref[image] = (middle + valid * part(image, 5) * ffn).astype(LOW)
        small_ref[6 + image : 7 + image, :] = column_sum(valid * ffn * upstream)
        normed, inverse = normalize(middle)
        grad_h2 = nt(gpre_ref[rows, :], up_w_ref[...])
        small_ref[2 + image : 3 + image, :] = column_sum(grad_h2)
        small_ref[4 + image : 5 + image, :] = column_sum(grad_h2 * normed)
        grad_mid = upstream + norm_back(grad_h2 * (1.0 + part(image, 4)), normed, inverse)
        grad_mid_ref[rows, :] = grad_mid
        small_ref[image : image + 1, :] = column_sum(valid * attn_ref[rows, :] * grad_mid)
        grad_attn = (valid * part(image, 2) * grad_mid).astype(LOW)
        gattn_ref[rows, :] = grad_attn
        out_bias_grad = out_bias_grad + column_sum(grad_attn.astype(F32))
        grad_att_ref[rows, :] = nt(grad_attn, out_w_ref[...]).astype(LOW)
    small_ref[8:9, :] = out_bias_grad
    out_term = tn(att_ref[...], gattn_ref[...])
    out_first = jnp.concatenate([out_term[:half, :half], out_term[half:, :half]], axis=1)
    out_second = jnp.concatenate([out_term[:half, half:], out_term[half:, half:]], axis=1)
    keep_ref[...] = jnp.where(core == 0, out_first, out_second)
    send_ref[:half, :] = jnp.where(core == 0, out_second, out_first).astype(LOW)
    send_ref[half : half + 16, :] = small_ref[...].astype(LOW)
    for image in range(image_count):
        start = half + 16 + image * half_len
        send_ref[start : start + half_len, :] = output_ref[image, half_len:, :]


def backward_kernel(
    normed_ref,
    inverse_ref,
    penalty_ref,
    qkv_w_ref,
    qkv_ref,
    h1_ref,
    grad_att_ref,
    grad_mid_ref,
    mod_ref,
    after_ref,
    after_too_ref,
    after_all_ref,
    grad_tokens_ref,
    keep_ref,
    send_ref,
    other_ref,
    small_ref,
    gqkv_ref,
):
    core = lax.axis_index("seq")
    image_count, length, width = grad_tokens_ref.shape
    half_len = length // 2
    half = width // 2
    first, second = head_masks(length)
    for step in range(image_count * (HEADS // 2)):
        rows, lanes, queries, keys, values = attention_pair(
            step, qkv_ref, penalty_ref, length, width
        )
        image = step // (HEADS // 2)
        penalty = penalty_ref[image : image + 1, :]
        grad_att = grad_att_ref[rows, lanes(0)]
        grad_q = jnp.zeros((length, PAIR), F32)
        grad_k = jnp.zeros((length, PAIR), F32)
        grad_v = jnp.zeros((length, PAIR), F32)
        for mask in (first, second):
            own_queries = masked(queries, mask)
            own_grad = masked(grad_att, mask)
            probs = softmax_rows(own_queries, keys, penalty)
            grad_probs = nt(own_grad, values)
            dots = jnp.sum(probs * grad_probs, axis=-1, keepdims=True)
            grad_scores = (probs * (grad_probs - dots)).astype(LOW)
            grad_v = grad_v + tn(probs.astype(LOW), own_grad)
            grad_q = grad_q + nn(grad_scores, masked(keys, mask))
            grad_k = grad_k + tn(grad_scores, own_queries)
        gqkv_ref[rows, lanes(0)] = (grad_q * HEAD_DIM**-0.5).astype(LOW)
        gqkv_ref[rows, lanes(1)] = grad_k.astype(LOW)
        gqkv_ref[rows, lanes(2)] = grad_v.astype(LOW)

    def part(image, which):
        return mod_ref[image : image + 1, which * width : (which + 1) * width].astype(F32)

    small_ref[...] = jnp.zeros_like(small_ref)
    small_ref[4:5, :] = column_sum(gqkv_ref[:, :width].astype(F32))
    small_ref[5:6, :] = column_sum(gqkv_ref[:, 2 * width :].astype(F32))
    for image in range(image_count):
        rows = slice(image * length, (image + 1) * length)
        normed = normed_ref[rows, :]
        inverse = jnp.concatenate([inverse_ref[rows, :]] * (width // LANES), axis=1)
        grad_h1 = nt(gqkv_ref[rows, :], qkv_w_ref[...])
        small_ref[image : image + 1, :] = column_sum(grad_h1)
        small_ref[2 + image : 3 + image, :] = column_sum(grad_h1 * normed)
        grad_in = norm_back(grad_h1 * (1.0 + part(image, 1)), normed, inverse)
        grad_tokens_ref[image] = (grad_mid_ref[rows, :] + grad_in).astype(LOW)
    low_term = tn(h1_ref[...], gqkv_ref[:, :width])
    high_term = tn(h1_ref[...], gqkv_ref[:, 2 * width :])
    keep_ref[:width, :] = jnp.where(core == 0, low_term, high_term)
    pair = jnp.where(core == 0, high_term, low_term).astype(LOW)
    term = tn(h1_ref[...], gqkv_ref[:, width : 2 * width])
    low_unit = jnp.concatenate([term[:half, :half], term[half:, :half]], axis=1)
    high_unit = jnp.concatenate([term[:half, half:], term[half:, half:]], axis=1)
    keep_ref[width:, :] = jnp.where(core == 0, low_unit, high_unit)
    cut = send_ref.shape[0] - half_len
    send_ref[:cut, :] = pair[:cut]
    send_ref[cut:, :] = grad_tokens_ref[0, half_len:, :]
    start = width - cut
    other_ref[:start, :] = pair[cut:]
    other_ref[start : start + half, :] = jnp.where(core == 0, high_unit, low_unit).astype(LOW)
    start += half
    other_ref[start : start + 8, :] = small_ref[...].astype(LOW)
    other_ref[start + 8 :, :] = grad_tokens_ref[1, half_len:, :]


def by_core(core, near, far):
    return [jnp.where(core == 0, near, far), jnp.where(core == 0, far, near)]


def split_kernel(
    keep_ref, recv_ref, marks_ref, own_up_ref, own_down_ref, send_up_ref, send_down_ref
):
    width = keep_ref.shape[1]
    piece = width // 16
    long = 4 * piece
    block = 8 * piece
    plane = lax.axis_index("dp") & 3

    def move(target, start, size, to):
        rows = pl.ds(pl.multiple_of(start, 8), size)
        target[to : to + size, :] = (keep_ref[rows, :] + recv_ref[rows, :].astype(F32)).astype(
            target.dtype
        )

    for target, steps in ((own_up_ref, (0, 2)), (send_up_ref, (1, 3))):
        for index, step in enumerate(steps):
            who = plane ^ step
            for z in range(4):
                for side in range(2):
                    start = side * width + piece * (4 * z + who)
                    move(target, start, piece, index * block + (2 * z + side) * piece)
    for target, steps in ((own_down_ref, (0, 1)), (send_down_ref, (2, 3))):
        for index, step in enumerate(steps):
            who = plane ^ step
            for z in range(2):
                start = 2 * width + long * (4 * z + who)
                move(target, start, long, index * block + z * long)
    send_up_ref[2 * block :, :] = marks_ref[...].astype(LOW)


def cross_kernel(
    own_up_ref,
    own_down_ref,
    recv_up_ref,
    recv_down_ref,
    marks_ref,
    after_ref,
    kept_ref,
    send_up_ref,
    send_down_ref,
):
    block = own_up_ref.shape[0] // 2
    first, second = slice(0, block), slice(block, 2 * block)
    kept_ref[first, :] = own_up_ref[first, :] + recv_up_ref[first, :].astype(F32)
    kept_ref[second, :] = own_down_ref[first, :] + recv_down_ref[first, :].astype(F32)
    kept_ref[2 * block : 2 * block + 8, :] = marks_ref[...].astype(LOW).astype(F32)
    kept_ref[2 * block + 8 :, :] = recv_up_ref[2 * block :, :].astype(F32)
    send_up_ref[first, :] = (own_up_ref[second, :] + recv_up_ref[second, :].astype(F32)).astype(LOW)
    send_up_ref[block : block + 8, :] = marks_ref[...].astype(LOW)
    send_up_ref[block + 8 :, :] = recv_up_ref[2 * block :, :]
    send_down_ref[...] = (own_down_ref[second, :] + recv_down_ref[second, :].astype(F32)).astype(LOW)


def split_qkv_kernel(
    keep_ref, recv_ref, other_ref, small_ref, keep_out_ref, recv_out_ref, early_ref, *refs
):
    core = lax.axis_index("seq")
    width = keep_ref.shape[1]
    piece = width // 16
    half = width // 2
    cut = PIECE_ROWS
    start = keep_ref.shape[0] - cut
    near = small_ref[...].astype(LOW).astype(F32)
    far = other_ref[start : start + 8, :].astype(F32)
    first, second = by_core(core, near, far)
    near_early = early_ref[...].astype(LOW).astype(F32)
    far_early = recv_out_ref[half : half + 16, :].astype(F32)
    early, early_too = by_core(core, near_early, far_early)
    rows = []
    for kind in range(3):
        low_rows = [first, second] if kind < 2 else [early, early_too]
        low_start = 2 * kind if kind < 2 else 0
        low_rows = [block[low_start : low_start + 2] for block in low_rows]
        high_rows = [block[2 * kind + 2 : 2 * kind + 4] for block in (early, early_too)]
        rows.append(
            jnp.where(
                core == 0, jnp.concatenate(low_rows, axis=0), jnp.concatenate(high_rows, axis=0)
            )
        )
    rows += [early[8:14] + early_too[8:14], first[4:6] + second[4:6], jnp.zeros((4, width), F32)]
    small = jnp.concatenate(rows, axis=0).astype(LOW)
    total_ref = refs[-1]
    total_ref[:cut, :] = keep_ref[:cut, :] + recv_ref[:cut, :].astype(F32)
    total_ref[cut : width + half, :] = keep_ref[cut:, :] + other_ref[:start, :].astype(F32)
    total_ref[width + half :, :] = keep_out_ref[...] + recv_out_ref[:half, :].astype(F32)
    for step, target in enumerate(refs[-5:-1]):
        who = (lax.axis_index("dp") & 3) ^ step
        for z in range(8):
            begin = piece * (4 * z + who)
            if z >= 4:
                begin = width + (z - 4) // 2 * half + piece * (4 * (z % 2) + who)
            rows = pl.ds(pl.multiple_of(begin, 8), piece)
            target[piece * z : piece * (z + 1), :] = total_ref[rows, :].astype(target.dtype)
        target[8 * piece :, :] = small.astype(target.dtype)


def summed(sources, rows):
    return sum((source[rows, :].astype(F32) for source in sources[1:]), sources[0][rows, :])


def fold_kernel(*refs):
    kept_ref, up_ref, down_ref = refs[:3]
    rest_ref, rest_small_ref = refs[4:6]
    sends = refs[6:9]
    total_ref, group_ref = refs[9:]
    width = total_ref.shape[1]
    piece = width // 16
    long = 4 * piece
    half = width // 2
    block = 8 * piece
    total_ref[:block, :] = kept_ref[:block, :] + up_ref[:block, :].astype(F32)
    total_ref[block:, :] = kept_ref[block : 2 * block, :] + down_ref[...].astype(F32)
    plane = lax.axis_index("dp") & 3
    for index in range(2):
        start = 2 * block + 8 * index
        group_ref[plane ^ index] = kept_ref[start : start + 8, :]
        start = block + 8 * index
        group_ref[plane ^ (2 + index)] = up_ref[start : start + 8, :].astype(F32)
    ids = [group_ref[q, 0:1] for q in range(4)] + [jnp.zeros((4, width), F32)]
    small = jnp.concatenate(ids, axis=0).astype(LOW)
    rest_small_ref[...] = small
    for step, target in enumerate((rest_ref,) + tuple(sends)):
        who = (lax.axis_index("dp") >> 2) ^ step
        rows = pl.ds(pl.multiple_of(2 * piece * who, 8), 2 * piece)
        target[: 2 * piece, :] = total_ref[rows, :].astype(target.dtype)
        rows = pl.ds(pl.multiple_of(8 * piece + long * (who % 2), 8), long)
        down = total_ref[rows, :]
        down = jnp.where(who < 2, down[:, :half], down[:, half:])
        down = jnp.concatenate([down[: 2 * piece], down[2 * piece :]], axis=1)
        target[2 * piece : 4 * piece, :] = down.astype(target.dtype)
        if step:
            target[4 * piece :, :] = small


def fold_qkv_kernel(*refs):
    parts = refs[:4]
    rest_ref, rest_small_ref = refs[4:6]
    sends = refs[6:9]
    total_ref, late_ref = refs[9:]
    width = total_ref.shape[1]
    piece = width // 16
    half = width // 2
    total_ref[...] = summed(parts, slice(0, 8 * piece))
    for step, part in enumerate(parts):
        late_ref[(lax.axis_index("dp") & 3) ^ step] = part[8 * piece :, :].astype(F32)
    rows = [late_ref[q, :12] for q in range(4)]
    rows.append(late_ref[0, 12:20] + late_ref[1, 12:20] + late_ref[2, 12:20] + late_ref[3, 12:20])
    small = jnp.concatenate(rows, axis=0).astype(LOW)
    rest_small_ref[...] = small
    for step, target in enumerate((rest_ref,) + tuple(sends)):
        who = (lax.axis_index("dp") >> 2) ^ step

        def side(start):
            value = total_ref[pl.ds(pl.multiple_of(piece * (start + who % 2), 8), piece), :]
            return jnp.where(who < 2, value[:, :half], value[:, half:])

        target[:piece, :] = jnp.concatenate([side(6), side(4)], axis=1).astype(target.dtype)
        pair = total_ref[pl.ds(pl.multiple_of(piece * who, 8), piece), :]
        target[piece : 2 * piece, :] = pair.astype(target.dtype)
        if step:
            target[2 * piece :, :] = small


def one_hot(ids, lead):
    place = lax.broadcasted_iota(jnp.int32, (lead.shape[1], ids.shape[1]), 0)
    wanted = (ids // GROUPS_PER_RANK) * 8 + ids % GROUPS_PER_RANK
    return jnp.where(place == wanted, 1.0, 0.0).astype(LOW)


def group_parts(silu_rows, own_groups, kinds, kind_of):
    zeros = jnp.zeros_like(kind_of, F32)
    blocks = [masked(silu_rows, kind_of == kind) for kind in kinds]
    rows = []
    for kind in kinds:
        for one in own_groups:
            rows.append(jnp.where((kind_of == kind) & one, 1.0, zeros))
    for kind in kinds:
        rows.append(jnp.where(kind_of == kind, 1.0, zeros))
    while len(rows) % 8:
        rows.append(zeros)
    return blocks, jnp.concatenate(rows, axis=0).astype(LOW)


def split_dot(values, weight):
    high = values.astype(LOW)
    low = (values - high.astype(F32)).astype(LOW)
    return nt(high, weight) + nt(low, weight)


def finish_kernel(
    own_ref,
    own_small_ref,
    one_ref,
    two_ref,
    three_ref,
    lead_ref,
    recv_out_ref,
    recv_two_ref,
    recv_other_ref,
    output_ref,
    grad_tokens_ref,
    output_to,
    grad_tokens_to,
    up_ref,
    down_ref,
    silu_ref,
    ids_ref,
    stack_ref,
    sems,
):
    core = lax.axis_index("seq")
    width = own_ref.shape[1]
    piece = width // 16
    half = width // 2
    slots, half_len = output_to.shape[:2]
    count = slots // 2
    pairs = []
    for index in range(count):
        slot = (1 - core) * count + index
        start = recv_out_ref.shape[0] - (count - index) * half_len
        pairs.append((recv_out_ref.at[pl.ds(start, half_len)], output_to.at[slot]))
        source = (recv_two_ref, recv_other_ref)[index]
        start = source.shape[0] - half_len
        pairs.append((source.at[pl.ds(start, half_len)], grad_tokens_to.at[slot]))
        slot = core * count + index
        pairs.append((output_ref.at[index, pl.ds(0, half_len)], output_to.at[slot]))
        pairs.append((grad_tokens_ref.at[index, pl.ds(0, half_len)], grad_tokens_to.at[slot]))
    copies = fetch(pairs, sems)
    parts = (own_ref, one_ref, two_ref, three_ref)
    total = summed(parts, slice(0, 4 * piece))
    up_ref[...] = jnp.concatenate([total[:piece], total[piece : 2 * piece]], axis=1)
    down = total[2 * piece :]
    down_ref[...] = jnp.concatenate([down[:, :half], down[:, half:]], axis=0)
    line = lax.axis_index("dp") >> 2
    smalls = (own_small_ref[...],) + tuple(part[4 * piece :, :] for part in parts[1:])
    for step, small in enumerate(smalls):
        stack_ref[line ^ step] = small[:, :LANES].astype(F32)
    stack = stack_ref[...].reshape(32, LANES).astype(LOW)
    count = 192
    row = lax.broadcasted_iota(jnp.int32, (32, count), 0)
    chip = lax.broadcasted_iota(jnp.int32, (32, count), 1) // 12
    spread = tn(stack, jnp.where(row == chip + 4 * (chip // 4), 1.0, 0.0).astype(LOW))[:8]
    slot = lax.broadcasted_iota(jnp.int32, (8, count), 0)
    wanted = lax.broadcasted_iota(jnp.int32, (8, count), 1) % 4
    ids = column_sum(jnp.where(slot == wanted, spread, 0.0)).astype(jnp.int32)
    ids_ref[...] = ids
    lead = lead_ref[...]
    silu_ref[...] = nn(lead, one_hot(ids, lead)).astype(LOW)
    for copy in copies:
        copy.wait()


def late_kernel(
    own_small_ref,
    one_ref,
    two_ref,
    three_ref,
    silu_ref,
    ids_ref,
    ada_ref,
    ada_out_ref,
    own_sums_ref,
    send_ref,
    out_bias_ref,
    up_bias_ref,
    down_bias_ref,
    qv_ref,
    stack_ref,
    bias_ref,
):
    core = lax.axis_index("seq")
    width = own_small_ref.shape[1]
    piece = width // 16
    half = width // 2
    line = lax.axis_index("dp") >> 2
    smalls = (own_small_ref[...],) + tuple(
        part[2 * piece :, :] for part in (one_ref, two_ref, three_ref)
    )
    for step, small in enumerate(smalls):
        stack_ref[line ^ step] = small[:48]
        bias_ref[line ^ step] = small[48:].astype(F32)
    stack = stack_ref[...].reshape(192, width)
    ids = ids_ref[...]
    item = lax.broadcasted_iota(jnp.int32, (1, 192), 1) % 12
    base = GROUPS_PER_RANK * lax.axis_index("dp")
    own = [ids == base + index for index in range(GROUPS_PER_RANK)]
    blocks, rows = group_parts(silu_ref[...], own, range(3), item // 4)
    sums = nn(rows, stack)
    for kind in range(3):
        ada_out_ref[:, kind * width : (kind + 1) * width] = nn(blocks[kind], stack)
    weight = ada_ref[:, pl.ds(pl.multiple_of(core * 3 * width, LANES), 3 * width)]
    own_sum = jnp.concatenate(
        [
            jnp.concatenate([sums[2 * kind : 2 * kind + 2] for kind in range(3)], axis=1),
            jnp.zeros((6, 3 * width), F32),
        ],
        axis=0,
    )
    cond = split_dot(own_sum, weight)
    low_cond, high_cond = cond[:2, :half], cond[:2, half:]
    kept = jnp.where(core == 0, low_cond, high_cond)
    sent = jnp.where(core == 0, high_cond, low_cond)
    zeros = jnp.zeros((2, half), F32)
    pad = jnp.zeros((3, width), F32)
    own_sums_ref[...] = jnp.concatenate(
        [jnp.concatenate([kept, zeros], axis=1), sums[6:9], pad], axis=0
    )
    send_ref[...] = jnp.concatenate(
        [jnp.concatenate([sent, zeros], axis=1), sums[6:9], pad], axis=0
    )
    bias = bias_ref[0] + bias_ref[1] + bias_ref[2] + bias_ref[3]
    out_bias_ref[...] = bias[0:1].reshape(width)
    up_bias_ref[...] = jnp.concatenate([bias[1 + row : 2 + row] for row in range(4)], axis=1).reshape(
        4 * width
    )
    down_bias_ref[...] = bias[5:6].reshape(width)
    qv_ref[...] = bias[6:8]


def rest_kernel(own_ref, one_ref, two_ref, three_ref, after_ref, out_ref, qkv_ref):
    core = lax.axis_index("seq")
    width = own_ref.shape[1]
    piece = width // 16
    half = width // 2
    total = summed((own_ref, one_ref, two_ref, three_ref), slice(0, 2 * piece))
    out_ref[...] = total[:piece, :half]
    unit, pair = total[:piece, half:], total[piece:]
    qkv_ref[...] = jnp.where(
        core == 0,
        jnp.concatenate([pair, unit], axis=1),
        jnp.concatenate([unit, pair], axis=1),
    )


def final_kernel(own_ref, recv_ref, own_cond_ref, cond_ref, bias_ref):
    core = lax.axis_index("seq")
    width = own_ref.shape[1]
    half = width // 2
    near, far = own_ref[...], recv_ref[...]
    values = own_cond_ref[...].astype(F32)
    values = jnp.where(core == 0, values[:, :half], values[:, half:])
    gate = 1.0 / (1.0 + jnp.exp(-values))
    cond_ref[...] = (near[:2, :half] + far[:2, :half]) * (gate * (1.0 + values * (1.0 - gate)))
    rows = [block[row : row + 1] for block in by_core(core, near, far) for row in range(2, 5)]
    bias_ref[...] = jnp.concatenate(rows, axis=1).reshape(6 * width)


def silu_slope(values):
    sigmoid_val = jax.nn.sigmoid(values)
    return sigmoid_val * (1.0 + values * (1.0 - sigmoid_val))


def swap_cores(values):
    return lax.ppermute(values, "seq", CORE_SWAP)


def pick(core, first, second):
    return jnp.where(core == 0, first, second)


def to_patches(images, far, core):
    half_len = images.shape[1] // 2
    return pick(
        core,
        jnp.concatenate([images[:, :half_len], far], axis=0),
        jnp.concatenate([far, images[:, :half_len]], axis=0),
    )


def call(kernel, name, shapes, scratch, limit, spaces, *operands, aliases=None):
    chosen = {
        "s": pl.BlockSpec(memory_space=pltpu.SMEM),
        "v": pl.BlockSpec(memory_space=pltpu.VMEM),
        "V": pl.BlockSpec(memory_space=pltpu.VMEM),
        "a": pl.BlockSpec(memory_space=pl.ANY),
        "h": pl.BlockSpec(memory_space=pltpu.HBM),
    }
    pinned = {"h": pltpu.HBM, "V": pltpu.VMEM}
    into, out_of = spaces
    operands = [
        pltpu.with_memory_space_constraint(item, pinned[kind]) if kind in pinned else item
        for kind, item in zip(into, operands)
    ]
    return pl.pallas_call(
        kernel,
        out_shape=tuple(
            pinned.get(kind, jax.ShapeDtypeStruct)(shape, dtype)
            for kind, (shape, dtype) in zip(out_of, shapes)
        ),
        in_specs=[chosen[kind] for kind in into],
        out_specs=[chosen[kind] for kind in out_of],
        scratch_shapes=scratch,
        compiler_params=pltpu.CompilerParams(vmem_limit_bytes=limit << 20),
        cost_estimate=pl.CostEstimate(flops=1, bytes_accessed=1, transcendentals=0),
        input_output_aliases=aliases or {},
        name=name,
    )(*operands)


def rank_swap(values, step, count):
    return lax.ppermute(values, "dp", [(rank, rank ^ step) for rank in range(count)])


def owner_total(term, dp_count):
    blocks = term.astype(LOW).reshape(dp_count, term.shape[0] // dp_count, term.shape[1])
    return jnp.sum(lax.all_to_all(blocks, "dp", 0, 0, tiled=True).astype(F32), axis=0)


def general_tail(
    core, dp_count, dp_rank, sides, smalls, heads, cond_rows, cond, own_ids, ada_weight
):
    highest = lax.Precision.HIGHEST
    width, mod_width = ada_weight.shape
    half = width // 2
    (keep_one, send_one), (keep_out, send_out), (keep_two, send_two, send_other) = sides
    output, grad_tokens = heads
    small_one, small_two = smalls
    half_len = output.shape[1] // 2
    recv_out = swap_cores(send_out)
    first_sum = jnp.concatenate(
        [
            keep_one + swap_cores(send_one).astype(F32),
            keep_out + recv_out[:half].astype(F32),
        ],
        axis=0,
    )
    recv_two, recv_other = swap_cores(send_two), swap_cores(send_other)
    second_sum = keep_two + jnp.concatenate(
        [recv_two[:PIECE_ROWS], recv_other[: keep_two.shape[0] - PIECE_ROWS]], axis=0
    ).astype(F32)
    output_far = recv_out[half + 16 :].reshape(-1, half_len, width)
    grad_far = jnp.stack([item[-half_len:] for item in (recv_two, recv_other)])
    ff_half = first_sum.shape[0] - 2 * width - half
    up = jnp.concatenate([first_sum[:width], first_sum[width : 2 * width]], axis=1)
    down = first_sum[2 * width : 2 * width + ff_half]
    down = jnp.concatenate([down[:, :half], down[:, half:]], axis=0)
    out = first_sum[2 * width + ff_half :]
    out = jnp.concatenate([out[:, :half], out[:, half:]], axis=0)
    pair, unit = second_sum[:width], second_sum[width:]
    unit = jnp.concatenate([unit[:, :half], unit[:, half:]], axis=0)
    qkv = pick(
        core, jnp.concatenate([pair, unit], axis=1), jnp.concatenate([unit, pair], axis=1)
    )
    sums = [owner_total(term, dp_count) for term in (qkv, out, up, down)]
    image_grad = jnp.concatenate(
        [small_two[0:2], small_two[2:4], small_one[0:2], small_one[2:4], small_one[4:6], small_one[6:8]],
        axis=1,
    )
    biases = jnp.concatenate([small_two[4:6], small_one[8:14]], axis=0)
    marks = jnp.broadcast_to(own_ids.astype(F32)[:, None], (own_ids.shape[0], width))
    packed = jnp.concatenate([image_grad.reshape(-1, width), biases, marks], axis=0)
    gathered = lax.all_to_all(
        jnp.broadcast_to(packed[None], (2 * dp_count,) + packed.shape),
        ("dp", "seq"),
        0,
        0,
        tiled=True,
    )
    grad_rows = gathered[:, :12].reshape(-1, mod_width)
    bias_sums = jnp.sum(gathered[:, 12:20], axis=0)
    all_ids = gathered[:, 20:, 0].reshape(-1).astype(jnp.int32)
    group_count = cond_rows.shape[0]
    all_hot = (all_ids[:, None] == jnp.arange(group_count, dtype=jnp.int32)[None, :]).astype(F32)
    group_grad = jnp.dot(all_hot.T, grad_rows, precision=highest)
    own_rows = width // dp_count
    silu_rows = lax.reduce_precision(jax.nn.silu(cond_rows.astype(F32)), 8, 7)
    silu_part = lax.dynamic_slice_in_dim(silu_rows, dp_rank * own_rows, own_rows, 1)
    grad_half = pick(core, group_grad[:, : mod_width // 2], group_grad[:, mod_width // 2 :])
    ada_sum = jnp.dot(silu_part.T, grad_half, precision=highest)
    own_grad = lax.dynamic_slice_in_dim(
        group_grad, dp_rank * GROUPS_PER_RANK, GROUPS_PER_RANK, 0
    )
    ada_half = lax.dynamic_slice_in_dim(ada_weight, core * half, half, 0).astype(F32)
    cond_half = pick(core, cond[:, :half], cond[:, half:]).astype(F32)
    grad_cond = silu_slope(cond_half) * jnp.dot(own_grad, ada_half.T, precision=highest)
    return (
        to_patches(output, output_far, core),
        to_patches(grad_tokens, grad_far, core),
        grad_cond,
        sums[0],
        bias_sums[:2],
        sums[1],
        bias_sums[2],
        sums[2],
        bias_sums[3:7].reshape(-1),
        sums[3],
        bias_sums[7],
        ada_sum,
        jnp.sum(grad_rows, axis=0),
    )


def body(
    tokens,
    cotangent,
    cond,
    group_ids,
    image_counts,
    patch_mask,
    qkv_weight,
    qv_bias,
    out_weight,
    out_bias,
    up_weight,
    up_bias,
    down_weight,
    down_bias,
    ada_weight,
    ada_bias,
):
    slot_count, half_len, width = tokens.shape
    ff_width = up_weight.shape[1]
    mod_width = ada_weight.shape[1]
    dp_count = lax.axis_size("dp")
    core = lax.axis_index("seq").astype(jnp.int32)
    dp_rank = lax.axis_index("dp").astype(jnp.int32)
    image_count = slot_count // 2
    length = 2 * half_len
    row_count = image_count * length
    half = width // 2
    piece = width // dp_count
    fast = dp_count == 16 and not GENERAL
    cond_blocks = lax.all_to_all(
        jnp.broadcast_to(cond[None], (dp_count,) + cond.shape), "dp", 0, 0, tiled=True
    )
    tokens_far = swap_cores(tokens)
    cot_far = swap_cores(cotangent)
    image_shape = (image_count, length, width)
    half_shape = (image_count, half_len, width)
    vmem = pltpu.VMEM
    (
        images,
        penalty,
        hot,
        marks,
        qkv_b_row,
        out_b_row,
        up_b_row,
        down_b_row,
        ada_weight_near,
        ada_b_row,
    ) = call(
        load_kernel,
        "load",
        (
            (image_shape, LOW),
            ((8, length), F32),
            ((8, 8 * dp_count), LOW),
            ((8, width), F32),
            ((1, 3 * width), F32),
            ((1, width), F32),
            ((1, ff_width), F32),
            ((1, width), F32),
            (ada_weight.shape, LOW),
            ((1, mod_width), F32),
        ),
        [
            pltpu.SMEM(group_ids.shape, jnp.int32),
            pltpu.SMEM(image_counts.shape, jnp.int32),
            vmem(patch_mask.shape, jnp.int32),
            vmem(qv_bias.shape, LOW),
            vmem(out_bias.shape, LOW),
            vmem(up_bias.shape, LOW),
            vmem(down_bias.shape, LOW),
            vmem(ada_bias.shape, LOW),
            pltpu.SemaphoreType.DMA((9 + 2 * image_count,)),
        ],
        12,
        ("hVha" + "h" * 7, "V" * 10),
        tokens,
        tokens_far,
        group_ids,
        image_counts,
        patch_mask,
        qv_bias,
        out_bias,
        up_bias,
        down_bias,
        ada_weight,
        ada_bias,
    )
    (
        qkv,
        h1,
        normed,
        inverse,
        image_mod,
        lead,
        att,
        middle,
        attn,
        act,
        grad_pre,
        valid,
        cot_images,
        qkv_weight_near,
        out_weight_near,
        up_weight_near,
        down_weight_near,
        keep_one,
        send_one,
        small_early,
    ) = call(
        partial(forward_kernel, piece if fast else 0),
        "forward_and_ffn_grads",
        (
            ((row_count, 3 * width), LOW),
            ((row_count, width), LOW),
            ((row_count, width), F32),
            ((row_count, LANES), F32),
            ((8, mod_width), LOW),
            ((24, 8 * dp_count), LOW),
            ((row_count, width), LOW),
            ((row_count, width), F32),
            ((row_count, width), F32),
            ((row_count, ff_width), LOW),
            ((row_count, ff_width), LOW),
            ((row_count, LANES), F32),
            (image_shape, LOW),
            (qkv_weight.shape, LOW),
            (out_weight.shape, LOW),
            (up_weight.shape, LOW),
            (down_weight.shape, LOW),
            ((2 * width + ff_width // 2, width), F32),
            ((2 * width + ff_width // 2, width), LOW),
            ((16, width), F32),
        ),
        [
            vmem((8 * dp_count, width), F32),
            vmem((width, 8 * dp_count), F32),
            vmem((row_count, width), LOW),
            vmem((row_count, width), LOW),
            pltpu.SemaphoreType.DMA((4 + 2 * image_count,)),
        ],
        24,
        ("V" * 10 + "h" * 5, "V" * 20),
        cond_blocks,
        images,
        cot_far,
        penalty,
        hot,
        qkv_b_row,
        out_b_row,
        up_b_row,
        ada_weight_near,
        ada_b_row,
        cotangent,
        qkv_weight,
        out_weight,
        up_weight,
        down_weight,
    )
    output, grad_att, grad_mid, keep_out, send_out, small_one = call(
        finish_forward_kernel,
        "norm_back",
        (
            (image_shape, LOW),
            ((row_count, width), LOW),
            ((row_count, width), F32),
            ((half, width), F32),
            ((half + 16 + row_count // 2, width), LOW),
            ((16, width), F32),
        ),
        [vmem((row_count, width), LOW)],
        16,
        ("V" * 13, "V" * 6),
        image_mod,
        att,
        middle,
        attn,
        act,
        grad_pre,
        valid,
        cot_images,
        out_weight_near,
        up_weight_near,
        down_weight_near,
        down_b_row,
        small_early,
    )

    def attention_back(*after):
        return call(
            backward_kernel,
            "attention_back",
            (
                (image_shape, LOW),
                ((width + half, width), F32),
                ((PIECE_ROWS + half_len, width), LOW),
                ((width + half + 8 - PIECE_ROWS + half_len, width), LOW),
                ((8, width), F32),
            ),
            [vmem((row_count, 3 * width), LOW)],
            24,
            ("V" * 9 + "aaa", "VVVVV"),
            normed,
            inverse,
            penalty,
            qkv_weight_near,
            qkv,
            h1,
            grad_att,
            grad_mid,
            image_mod,
            *after,
        )

    if not fast:
        grad_tokens, keep_two, send_two, send_other, small_two = attention_back(
            small_one, keep_one, keep_out
        )
        own_ids = lax.dynamic_slice_in_dim(group_ids, core * image_count, image_count, 0)
        return general_tail(
            core,
            dp_count,
            dp_rank,
            ((keep_one, send_one), (keep_out, send_out), (keep_two, send_two, send_other)),
            (small_one, small_two),
            (output, grad_tokens),
            cond_blocks.reshape(-1, width),
            cond,
            own_ids,
            ada_weight,
        )

    recv_one = swap_cores(send_one)
    recv_out = swap_cores(send_out)
    block_rows = 8 * piece
    own_up, own_down, sent_up, sent_down = call(
        split_kernel,
        "split_plane",
        (
            ((2 * block_rows, width), F32),
            ((2 * block_rows, width), F32),
            ((2 * block_rows + 8, width), LOW),
            ((2 * block_rows, width), LOW),
        ),
        [],
        16,
        ("VVV", "VVVV"),
        keep_one,
        recv_one,
        marks,
    )
    near_up, near_down = rank_swap(sent_up, 1, 16), rank_swap(sent_down, 2, 16)
    grad_tokens, keep_two, send_two, send_other, small_two = attention_back(
        sent_up, sent_down, recv_out
    )
    kept, cross_up, cross_down = call(
        cross_kernel,
        "cross_plane",
        (
            ((2 * block_rows + 16, width), F32),
            ((block_rows + 16, width), LOW),
            ((block_rows, width), LOW),
        ),
        [],
        16,
        ("VVVVVa", "VVV"),
        own_up,
        own_down,
        near_up,
        near_down,
        marks,
        small_two,
    )
    near_up, near_down = rank_swap(cross_up, 2, 16), rank_swap(cross_down, 1, 16)
    recv_two, recv_other = swap_cores(send_two), swap_cores(send_other)
    split_rows = 8 * piece + 24
    own_qkv, *sent_qkv = call(
        split_qkv_kernel,
        "split_qkv_plane",
        (((split_rows, width), F32),) + (((split_rows, width), LOW),) * 3,
        [vmem((2 * width, width), F32)],
        16,
        ("VVVVVVVa", "VVVV"),
        keep_two,
        recv_two,
        recv_other,
        small_two,
        keep_out,
        recv_out,
        small_one,
        cross_up,
    )
    near_qkv = [rank_swap(item, step + 1, 16) for step, item in enumerate(sent_qkv)]
    line_rows = 4 * piece + 8
    rest, rest_ids, *lines = call(
        fold_kernel,
        "fold_plane",
        (((4 * piece, width), F32), ((8, width), LOW)) + (((line_rows, width), LOW),) * 3,
        [vmem((16 * piece, width), F32), vmem((4, 8, width), F32)],
        16,
        ("VVVa", "VVVVV"),
        kept,
        near_up,
        near_down,
        sent_qkv[2],
    )
    lines = [rank_swap(item, 4 * (step + 1), 16) for step, item in enumerate(lines)]
    line_rows = 2 * piece + 56
    rest_qkv, rest_small, *lines_qkv = call(
        fold_qkv_kernel,
        "fold_qkv_plane",
        (((2 * piece, width), F32), ((56, width), LOW)) + (((line_rows, width), LOW),) * 3,
        [vmem((8 * piece, width), F32), vmem((4, 24, width), F32)],
        16,
        ("VVVV", "VVVVV"),
        own_qkv,
        *near_qkv,
    )
    lines_qkv = [rank_swap(item, 4 * (step + 1), 16) for step, item in enumerate(lines_qkv)]
    output, grad_tokens, up_sum, down_sum, silu_rows, all_ids = call(
        finish_kernel,
        "finish_line",
        (
            (tokens.shape, LOW),
            (tokens.shape, LOW),
            ((piece, ff_width // 2), F32),
            ((4 * piece, half), F32),
            ((piece, 192), LOW),
            ((1, 192), jnp.int32),
        ),
        [vmem((4, 8, LANES), F32), pltpu.SemaphoreType.DMA((4 * image_count,))],
        16,
        ("V" * 11, "hhvvVV"),
        rest,
        rest_ids,
        *lines,
        lead,
        recv_out,
        recv_two,
        recv_other,
        output,
        grad_tokens,
    )
    (
        ada_sum,
        own_sums,
        send_sums,
        out_bias_sum,
        up_bias_sum,
        down_bias_sum,
        qv_sum,
    ) = call(
        late_kernel,
        "late_groups",
        (
            ((piece, mod_width // 2), F32),
            ((8, width), F32),
            ((8, width), F32),
            ((width,), F32),
            ((ff_width,), F32),
            ((width,), F32),
            ((2, width), F32),
        ),
        [vmem((4, 48, width), LOW), vmem((4, 8, width), F32)],
        16,
        ("V" * 7, "vVVvvvv"),
        rest_small,
        *lines_qkv,
        silu_rows,
        all_ids,
        ada_weight_near,
    )
    out_sum, qkv_sum = call(
        rest_kernel,
        "rest_sums",
        (((piece, half), F32), ((piece, 3 * half), F32)),
        [],
        16,
        ("VVVVa", "vv"),
        rest_qkv,
        *lines_qkv,
        send_sums,
    )
    grad_cond, ada_bias_sum = call(
        final_kernel,
        "final_groups",
        (((GROUPS_PER_RANK, half), F32), ((mod_width,), F32)),
        [],
        16,
        ("VVv", "vv"),
        own_sums,
        swap_cores(send_sums),
        cond,
    )
    return (
        output,
        grad_tokens,
        grad_cond,
        qkv_sum,
        qv_sum,
        out_sum,
        out_bias_sum,
        up_sum,
        up_bias_sum,
        down_sum,
        down_bias_sum,
        ada_sum,
        ada_bias_sum,
    )


def solution(mesh):
    placed = (
        P("dp", "seq", None),
        P("dp", "seq", None),
        P("dp", None),
        P("dp"),
        P("dp"),
        P("dp", None),
        P(),
        P(),
        P(),
        P(),
        P(),
        P(),
        P(),
        P(),
        P(),
        P(),
    )
    return jax.shard_map(
        body,
        mesh=mesh,
        in_specs=placed,
        out_specs=(
            P("dp", "seq", None),
            P("dp", "seq", None),
            P("dp", "seq"),
            P("dp", "seq"),
            P(),
            P("dp", "seq"),
            P(),
            P("dp", "seq"),
            P(),
            P("dp", "seq"),
            P(),
            P("dp", "seq"),
            P(),
        ),
        check_vma=False,
    )
```

```python
from functools import partial

import jax
import jax.numpy as jnp
from jax import lax
from jax.experimental import pallas as pl
from jax.experimental.pallas import tpu as pltpu
from jax.sharding import PartitionSpec as P

HEADS = 6
HEAD_DIM = 64
PAIR = 2 * HEAD_DIM
CORE_SWAP = ((0, 1), (1, 0))
CHUNK = 256
LANES = 128
GROUPS_PER_RANK = 2
GENERAL = False
PIECE_ROWS = 288
F32 = jnp.float32
LOW = jnp.bfloat16


def nn(left, right):
    return lax.dot_general(left, right, (((1,), (0,)), ((), ())), preferred_element_type=F32)


def nt(left, right):
    return lax.dot_general(left, right, (((1,), (1,)), ((), ())), preferred_element_type=F32)


def tn(left, right):
    return lax.dot_general(left, right, (((0,), (0,)), ((), ())), preferred_element_type=F32)


def normalize(values):
    center = values - jnp.mean(values, axis=-1, keepdims=True)
    spread = jnp.mean(center * center, axis=-1, keepdims=True)
    inverse = lax.rsqrt(spread + 1e-06)
    return center * inverse, inverse


def norm_back(grad, normed, inverse):
    return inverse * (
        grad
        - jnp.mean(grad, axis=-1, keepdims=True)
        - normed * jnp.mean(grad * normed, axis=-1, keepdims=True)
    )


def column_sum(values):
    return jnp.sum(values, axis=0, keepdims=True)


def head_masks(rows):
    lane = lax.broadcasted_iota(jnp.int32, (rows, PAIR), 1)
    return lane < HEAD_DIM, lane >= HEAD_DIM


def masked(values, mask):
    return jnp.where(mask, values, jnp.zeros_like(values))


def fetch(pairs, sems):
    copies = []
    for index, (source, target) in enumerate(pairs):
        copy = pltpu.make_async_copy(source, target, sems.at[index])
        copy.start()
        copies.append(copy)
    return copies


def own_images(near_ref, far_ref, target_ref, first_image):
    half_len = near_ref.shape[1]
    pairs = []
    for image in range(target_ref.shape[0]):
        slot = first_image + image
        pairs.append((near_ref.at[slot], target_ref.at[image, pl.ds(0, half_len)]))
        pairs.append((far_ref.at[slot], target_ref.at[image, pl.ds(half_len, half_len)]))
    return pairs


def own_marks(mask_ref, counts_ref, core, image, image_count, half_len):
    slot = core * image_count + image
    live = jnp.where(slot < counts_ref[0], 1.0, 0.0)
    marks = mask_ref[pl.ds(slot, 1), :].astype(F32) * live
    low_marks, high_marks = marks[:, :half_len], marks[:, half_len:]
    return jnp.concatenate(
        [
            jnp.where(core == 0, low_marks, high_marks),
            jnp.where(core == 0, high_marks, low_marks),
        ],
        axis=1,
    )


def as_row(ref):
    return ref[...].astype(F32).reshape(1, ref.shape[0])


def load_kernel(
    tokens_hbm,
    tokens_far_ref,
    ids_hbm,
    counts_hbm,
    mask_hbm,
    qv_b_hbm,
    out_b_hbm,
    up_b_hbm,
    down_b_hbm,
    ada_w_hbm,
    ada_b_hbm,
    images_ref,
    penalty_ref,
    hot_ref,
    marks_ref,
    qkv_b_ref,
    out_b_ref,
    up_b_ref,
    down_b_ref,
    ada_w_ref,
    ada_b_ref,
    ids_ref,
    counts_ref,
    mask_ref,
    qv_b_ref,
    out_b_raw,
    up_b_raw,
    down_b_raw,
    ada_b_raw,
    sems,
):
    core = lax.axis_index("seq")
    image_count, length, width = images_ref.shape
    half_len = length // 2
    first_image = core * image_count
    copies = fetch(
        [
            (ids_hbm, ids_ref),
            (counts_hbm, counts_ref),
            (mask_hbm, mask_ref),
            (qv_b_hbm, qv_b_ref),
            (out_b_hbm, out_b_raw),
            (up_b_hbm, up_b_raw),
            (down_b_hbm, down_b_raw),
            (ada_b_hbm, ada_b_raw),
            (ada_w_hbm, ada_w_ref),
        ]
        + own_images(tokens_hbm, tokens_far_ref, images_ref, first_image),
        sems,
    )
    for copy in copies[:8]:
        copy.wait()
    row = lax.broadcasted_iota(jnp.int32, hot_ref.shape, 0)
    column = lax.broadcasted_iota(jnp.int32, hot_ref.shape, 1)
    lane = lax.broadcasted_iota(jnp.int32, marks_ref.shape, 1)
    hot = jnp.zeros(hot_ref.shape, F32)
    marks = jnp.zeros(marks_ref.shape, F32)
    for slot in range(2 * image_count):
        marks = jnp.where(lane == slot, ids_ref[slot].astype(F32), marks)
    marks_ref[...] = marks
    penalty_ref[...] = jnp.zeros_like(penalty_ref)
    for image in range(image_count):
        group = ids_ref[first_image + image]
        place = 8 * (group // GROUPS_PER_RANK) + group % GROUPS_PER_RANK
        hot = jnp.where((row == image) & (column == place), 1.0, hot)
        own = own_marks(mask_ref, counts_ref, core, image, image_count, half_len)
        penalty_ref[image : image + 1, :] = (own - 1.0) * 30000.0
    hot_ref[...] = hot.astype(LOW)
    qkv_b_ref[...] = jnp.concatenate(
        [qv_b_ref[0:1, :], jnp.zeros((1, width), LOW), qv_b_ref[1:2, :]], axis=1
    ).astype(F32)
    for raw, target in (
        (out_b_raw, out_b_ref),
        (up_b_raw, up_b_ref),
        (down_b_raw, down_b_ref),
        (ada_b_raw, ada_b_ref),
    ):
        target[...] = as_row(raw)
    for copy in copies[8:]:
        copy.wait()


def attention_pair(step, qkv_ref, penalty_ref, length, width):
    image, pair = divmod(step, HEADS // 2)
    rows = slice(image * length, (image + 1) * length)

    def lanes(which):
        start = which * width + pair * PAIR
        return slice(start, start + PAIR)

    queries = qkv_ref[rows, lanes(0)] * jnp.asarray(HEAD_DIM**-0.5, LOW)
    return rows, lanes, queries, qkv_ref[rows, lanes(1)], qkv_ref[rows, lanes(2)]


def image_rows(image, length):
    return slice(image * length, (image + 1) * length)


def mod_part(mod_ref, image, which, width):
    return mod_ref[image : image + 1, which * width : (which + 1) * width].astype(F32)


def wide_column(column_ref, rows, width):
    return jnp.concatenate([column_ref[rows, :]] * (width // LANES), axis=1)


def forward_kernel(
    lead_rows,
    cond_ref,
    images_ref,
    cot_far_ref,
    penalty_ref,
    hot_ref,
    qkv_b_ref,
    out_b_ref,
    up_b_ref,
    ada_w_ref,
    ada_b_ref,
    cot_hbm,
    qkv_w_hbm,
    out_w_hbm,
    up_w_hbm,
    down_w_hbm,
    qkv_ref,
    h1_ref,
    normed_ref,
    inverse_ref,
    mod_ref,
    lead_ref,
    logs_ref,
    att_ref,
    mid_ref,
    attn_ref,
    act_ref,
    gpre_ref,
    valid_ref,
    cot_ref,
    qkv_w_ref,
    out_w_ref,
    up_w_ref,
    down_w_ref,
    keep_ref,
    send_ref,
    small_ref,
    cond_rows_ref,
    turned_ref,
    h2_ref,
    gffn_ref,
    sems,
):
    core = lax.axis_index("seq")
    image_count, length, width = images_ref.shape
    half_len = length // 2
    half = width // 2
    ff_width = up_w_ref.shape[1]
    copies = fetch(
        [
            (qkv_w_hbm, qkv_w_ref),
            (out_w_hbm, out_w_ref),
            (up_w_hbm, up_w_ref),
            (down_w_hbm, down_w_ref),
        ]
        + own_images(cot_hbm, cot_far_ref, cot_ref, core * image_count),
        sems,
    )
    block_count, block_rows = cond_ref.shape[:2]
    cond_rows_ref[...] = jnp.zeros_like(cond_rows_ref)
    for block in range(block_count):
        start = 8 * (block_count - 1 - block)
        cond_rows_ref[start : start + block_rows, :] = cond_ref[block].astype(F32)
    cond = cond_rows_ref[...]
    silu = cond / (1.0 + jnp.exp(-cond))
    image_silu = nn(hot_ref[...], silu.astype(LOW)).astype(LOW)
    mod_ref[...] = (nn(image_silu, ada_w_ref[...]) + ada_b_ref[...]).astype(LOW)

    def part(image, which):
        return mod_part(mod_ref, image, which, width)

    copies[0].wait()
    for image in range(image_count):
        rows = image_rows(image, length)
        normed, inverse = normalize(images_ref[image].astype(F32))
        normed_ref[rows, :] = normed
        inverse_ref[rows, :] = jnp.broadcast_to(inverse, (length, LANES))
        marks = jnp.where(penalty_ref[image : image + 1, :] < 0.0, 0.0, 1.0)
        valid_ref[rows, :] = jnp.broadcast_to(marks, (LANES, length)).T
        h1 = (normed * (1.0 + part(image, 1)) + part(image, 0)).astype(LOW)
        h1_ref[rows, :] = h1
        qkv_ref[rows, :] = (nn(h1, qkv_w_ref[...]) + qkv_b_ref[...]).astype(LOW)

    first, second = head_masks(length)
    for step in range(image_count * (HEADS // 2)):
        rows, lanes, queries, keys, values = attention_pair(
            step, qkv_ref, penalty_ref, length, width
        )
        image = step // (HEADS // 2)
        penalty = penalty_ref[image : image + 1, :]
        total = jnp.zeros((length, PAIR), F32)
        for side, mask in enumerate((first, second)):
            scores = nt(masked(queries, mask), keys) + penalty
            top = jnp.max(scores, axis=-1, keepdims=True)
            exps = jnp.exp(scores - top)
            whole = jnp.sum(exps, axis=-1, keepdims=True)
            head = 2 * (step % (HEADS // 2)) + side
            logs_ref[rows, head * LANES : (head + 1) * LANES] = jnp.broadcast_to(
                top + jnp.log(whole), (length, LANES)
            )
            total = total + nn((exps / whole).astype(LOW), masked(values, mask))
        att_ref[rows, lanes(0)] = total.astype(LOW)

    for copy in copies[1:]:
        copy.wait()
    if lead_rows:
        turned_ref[...] = silu.T
        start = pl.multiple_of(lax.axis_index("dp") * lead_rows, 8)
        lead_ref[...] = turned_ref[pl.ds(start, lead_rows), :].astype(LOW)
    else:
        lead_ref[...] = jnp.zeros_like(lead_ref)
    small_ref[...] = jnp.zeros_like(small_ref)
    down_bias_grad = jnp.zeros((1, width), F32)
    for image in range(image_count):
        rows = image_rows(image, length)
        valid = wide_column(valid_ref, rows, width)
        attn = nn(att_ref[rows, :], out_w_ref[...]) + out_b_ref[...]
        attn_ref[rows, :] = attn
        middle = images_ref[image].astype(F32) + valid * part(image, 2) * attn
        mid_ref[rows, :] = middle
        normed, _ = normalize(middle)
        h2_ref[rows, :] = (normed * (1.0 + part(image, 4)) + part(image, 3)).astype(LOW)
        grad_ffn = (valid * part(image, 5) * cot_ref[image].astype(F32)).astype(LOW)
        gffn_ref[rows, :] = grad_ffn
        down_bias_grad = down_bias_grad + column_sum(grad_ffn.astype(F32))
    small_ref[13:14, :] = down_bias_grad

    for chunk in range(ff_width // CHUNK):
        columns = slice(chunk * CHUNK, (chunk + 1) * CHUNK)
        up_w = up_w_ref[:, columns]
        down_w = down_w_ref[columns, :]
        bias = jnp.zeros((1, CHUNK), F32)
        for image in range(image_count):
            rows = image_rows(image, length)
            pre = nn(h2_ref[rows, :], up_w) + up_b_ref[:, columns]
            square = pre * pre
            inner = jnp.tanh(pre * (0.7978845608028654 + 0.035677408136300125 * square))
            cdf = 0.5 * inner + 0.5
            act_ref[rows, columns] = (pre * cdf).astype(LOW)
            slope = 0.5 * (pre * (0.7978845608028654 + 0.10703222440890037 * square)) * (
                1.0 - inner * inner
            ) + cdf
            grad_pre = (nt(gffn_ref[rows, :], down_w) * slope).astype(LOW)
            gpre_ref[rows, columns] = grad_pre
            bias = bias + column_sum(grad_pre.astype(F32))
        for tile in range(CHUNK // LANES):
            start = chunk * CHUNK + tile * LANES
            small_ref[9 + start // width : 10 + start // width, start % width : start % width + LANES] = (
                bias[:, tile * LANES : (tile + 1) * LANES]
            )

    first_half = gffn_ref[:, :half]
    second_half = gffn_ref[:, half:]
    gffn_keep = jnp.where(core == 0, first_half, second_half)
    gffn_send = jnp.where(core == 0, second_half, first_half)
    side_chunks = ff_width // CHUNK // 2
    for step in range(side_chunks):
        low = slice(step * CHUNK, (step + 1) * CHUNK)
        high = slice((step + side_chunks) * CHUNK, (step + side_chunks + 1) * CHUNK)
        up_low = tn(h2_ref[...], gpre_ref[:, low])
        up_high = tn(h2_ref[...], gpre_ref[:, high])
        up_keep = jnp.where(core == 0, up_low, up_high)
        up_send = jnp.where(core == 0, up_high, up_low).astype(LOW)
        for tile in range(CHUNK // LANES):
            start = step * CHUNK + tile * LANES
            rows = slice(start // width * width, (start // width + 1) * width)
            columns = slice(start % width, start % width + LANES)
            keep_ref[rows, columns] = up_keep[:, tile * LANES : (tile + 1) * LANES]
            send_ref[rows, columns] = up_send[:, tile * LANES : (tile + 1) * LANES]
        rows = slice(2 * width + step * CHUNK, 2 * width + (step + 1) * CHUNK)
        for target, side in ((keep_ref, gffn_keep), (send_ref, gffn_send)):
            target[rows, :] = jnp.concatenate(
                [tn(act_ref[:, low], side), tn(act_ref[:, high], side)], axis=1
            ).astype(target.dtype)


def finish_forward_kernel(
    mod_ref,
    att_ref,
    mid_ref,
    attn_ref,
    act_ref,
    gpre_ref,
    valid_ref,
    cot_ref,
    out_w_ref,
    up_w_ref,
    down_w_ref,
    down_b_ref,
    early_ref,
    output_ref,
    grad_att_ref,
    grad_mid_ref,
    keep_ref,
    send_ref,
    small_ref,
    gattn_ref,
):
    core = lax.axis_index("seq")
    image_count, length, width = cot_ref.shape
    half_len = length // 2
    half = width // 2
    small_ref[...] = early_ref[...]

    def part(image, which):
        return mod_part(mod_ref, image, which, width)

    out_bias_grad = jnp.zeros((1, width), F32)
    for image in range(image_count):
        rows = image_rows(image, length)
        valid = wide_column(valid_ref, rows, width)
        upstream = cot_ref[image].astype(F32)
        middle = mid_ref[rows, :]
        ffn = nn(act_ref[rows, :], down_w_ref[...]) + down_b_ref[...]
        output_ref[image] = (middle + valid * part(image, 5) * ffn).astype(LOW)
        small_ref[6 + image : 7 + image, :] = column_sum(valid * ffn * upstream)
        normed, inverse = normalize(middle)
        grad_h2 = nt(gpre_ref[rows, :], up_w_ref[...])
        small_ref[2 + image : 3 + image, :] = column_sum(grad_h2)
        small_ref[4 + image : 5 + image, :] = column_sum(grad_h2 * normed)
        grad_mid = upstream + norm_back(grad_h2 * (1.0 + part(image, 4)), normed, inverse)
        grad_mid_ref[rows, :] = grad_mid
        small_ref[image : image + 1, :] = column_sum(valid * attn_ref[rows, :] * grad_mid)
        grad_attn = (valid * part(image, 2) * grad_mid).astype(LOW)
        gattn_ref[rows, :] = grad_attn
        out_bias_grad = out_bias_grad + column_sum(grad_attn.astype(F32))
        grad_att_ref[rows, :] = nt(grad_attn, out_w_ref[...]).astype(LOW)
    small_ref[8:9, :] = out_bias_grad
    out_term = tn(att_ref[...], gattn_ref[...])
    out_first = jnp.concatenate([out_term[:half, :half], out_term[half:, :half]], axis=1)
    out_second = jnp.concatenate([out_term[:half, half:], out_term[half:, half:]], axis=1)
    keep_ref[...] = jnp.where(core == 0, out_first, out_second)
    send_ref[:half, :] = jnp.where(core == 0, out_second, out_first).astype(LOW)
    send_ref[half : half + 16, :] = small_ref[...].astype(LOW)
    for image in range(image_count):
        start = half + 16 + image * half_len
        send_ref[start : start + half_len, :] = output_ref[image, half_len:, :]


def backward_kernel(
    normed_ref,
    inverse_ref,
    penalty_ref,
    logs_ref,
    qkv_w_ref,
    qkv_ref,
    h1_ref,
    grad_att_ref,
    grad_mid_ref,
    mod_ref,
    after_ref,
    after_too_ref,
    after_all_ref,
    grad_tokens_ref,
    keep_ref,
    send_ref,
    other_ref,
    small_ref,
    gqkv_ref,
):
    core = lax.axis_index("seq")
    image_count, length, width = grad_tokens_ref.shape
    half_len = length // 2
    half = width // 2
    first, second = head_masks(length)
    for step in range(image_count * (HEADS // 2)):
        rows, lanes, queries, keys, values = attention_pair(
            step, qkv_ref, penalty_ref, length, width
        )
        image = step // (HEADS // 2)
        penalty = penalty_ref[image : image + 1, :]
        grad_att = grad_att_ref[rows, lanes(0)]
        grad_q = jnp.zeros((length, PAIR), F32)
        grad_k = jnp.zeros((length, PAIR), F32)
        grad_v = jnp.zeros((length, PAIR), F32)
        for side, mask in enumerate((first, second)):
            own_queries = masked(queries, mask)
            own_grad = masked(grad_att, mask)
            head = 2 * (step % (HEADS // 2)) + side
            logs = logs_ref[rows, head * LANES : (head + 1) * LANES]
            logs = jnp.concatenate([logs] * (length // LANES), axis=1)
            probs = jnp.exp(nt(own_queries, keys) + penalty - logs)
            grad_probs = nt(own_grad, values)
            dots = jnp.sum(probs * grad_probs, axis=-1, keepdims=True)
            grad_scores = (probs * (grad_probs - dots)).astype(LOW)
            grad_v = grad_v + tn(probs.astype(LOW), own_grad)
            grad_q = grad_q + nn(grad_scores, masked(keys, mask))
            grad_k = grad_k + tn(grad_scores, own_queries)
        gqkv_ref[rows, lanes(0)] = (grad_q * HEAD_DIM**-0.5).astype(LOW)
        gqkv_ref[rows, lanes(1)] = grad_k.astype(LOW)
        gqkv_ref[rows, lanes(2)] = grad_v.astype(LOW)

    def part(image, which):
        return mod_ref[image : image + 1, which * width : (which + 1) * width].astype(F32)

    small_ref[...] = jnp.zeros_like(small_ref)
    small_ref[4:5, :] = column_sum(gqkv_ref[:, :width].astype(F32))
    small_ref[5:6, :] = column_sum(gqkv_ref[:, 2 * width :].astype(F32))
    for image in range(image_count):
        rows = slice(image * length, (image + 1) * length)
        normed = normed_ref[rows, :]
        inverse = jnp.concatenate([inverse_ref[rows, :]] * (width // LANES), axis=1)
        grad_h1 = nt(gqkv_ref[rows, :], qkv_w_ref[...])
        small_ref[image : image + 1, :] = column_sum(grad_h1)
        small_ref[2 + image : 3 + image, :] = column_sum(grad_h1 * normed)
        grad_in = norm_back(grad_h1 * (1.0 + part(image, 1)), normed, inverse)
        grad_tokens_ref[image] = (grad_mid_ref[rows, :] + grad_in).astype(LOW)
    low_term = tn(h1_ref[...], gqkv_ref[:, :width])
    high_term = tn(h1_ref[...], gqkv_ref[:, 2 * width :])
    keep_ref[:width, :] = jnp.where(core == 0, low_term, high_term)
    pair = jnp.where(core == 0, high_term, low_term).astype(LOW)
    term = tn(h1_ref[...], gqkv_ref[:, width : 2 * width])
    low_unit = jnp.concatenate([term[:half, :half], term[half:, :half]], axis=1)
    high_unit = jnp.concatenate([term[:half, half:], term[half:, half:]], axis=1)
    keep_ref[width:, :] = jnp.where(core == 0, low_unit, high_unit)
    cut = send_ref.shape[0] - half_len
    send_ref[:cut, :] = pair[:cut]
    send_ref[cut:, :] = grad_tokens_ref[0, half_len:, :]
    start = width - cut
    other_ref[:start, :] = pair[cut:]
    other_ref[start : start + half, :] = jnp.where(core == 0, high_unit, low_unit).astype(LOW)
    start += half
    other_ref[start : start + 8, :] = small_ref[...].astype(LOW)
    other_ref[start + 8 :, :] = grad_tokens_ref[1, half_len:, :]


def by_core(core, near, far):
    return [jnp.where(core == 0, near, far), jnp.where(core == 0, far, near)]


def split_kernel(
    keep_ref, recv_ref, marks_ref, own_up_ref, own_down_ref, send_up_ref, send_down_ref
):
    width = keep_ref.shape[1]
    piece = width // 16
    long = 4 * piece
    block = 8 * piece
    plane = lax.axis_index("dp") & 3

    def move(target, start, size, to):
        rows = pl.ds(pl.multiple_of(start, 8), size)
        target[to : to + size, :] = (keep_ref[rows, :] + recv_ref[rows, :].astype(F32)).astype(
            target.dtype
        )

    for target, steps in ((own_up_ref, (0, 2)), (send_up_ref, (1, 3))):
        for index, step in enumerate(steps):
            who = plane ^ step
            for z in range(4):
                for side in range(2):
                    start = side * width + piece * (4 * z + who)
                    move(target, start, piece, index * block + (2 * z + side) * piece)
    for target, steps in ((own_down_ref, (0, 1)), (send_down_ref, (2, 3))):
        for index, step in enumerate(steps):
            who = plane ^ step
            for z in range(2):
                start = 2 * width + long * (4 * z + who)
                move(target, start, long, index * block + z * long)
    send_up_ref[2 * block :, :] = marks_ref[...].astype(LOW)


def cross_kernel(
    own_up_ref,
    own_down_ref,
    recv_up_ref,
    recv_down_ref,
    marks_ref,
    after_ref,
    kept_ref,
    send_up_ref,
    send_down_ref,
):
    block = own_up_ref.shape[0] // 2
    first, second = slice(0, block), slice(block, 2 * block)
    kept_ref[first, :] = own_up_ref[first, :] + recv_up_ref[first, :].astype(F32)
    kept_ref[second, :] = own_down_ref[first, :] + recv_down_ref[first, :].astype(F32)
    kept_ref[2 * block : 2 * block + 8, :] = marks_ref[...].astype(LOW).astype(F32)
    kept_ref[2 * block + 8 :, :] = recv_up_ref[2 * block :, :].astype(F32)
    send_up_ref[first, :] = (own_up_ref[second, :] + recv_up_ref[second, :].astype(F32)).astype(LOW)
    send_up_ref[block : block + 8, :] = marks_ref[...].astype(LOW)
    send_up_ref[block + 8 :, :] = recv_up_ref[2 * block :, :]
    send_down_ref[...] = (own_down_ref[second, :] + recv_down_ref[second, :].astype(F32)).astype(LOW)


def split_qkv_kernel(
    keep_ref, recv_ref, other_ref, small_ref, keep_out_ref, recv_out_ref, early_ref, *refs
):
    core = lax.axis_index("seq")
    width = keep_ref.shape[1]
    piece = width // 16
    half = width // 2
    cut = PIECE_ROWS
    start = keep_ref.shape[0] - cut
    near = small_ref[...].astype(LOW).astype(F32)
    far = other_ref[start : start + 8, :].astype(F32)
    first, second = by_core(core, near, far)
    near_early = early_ref[...].astype(LOW).astype(F32)
    far_early = recv_out_ref[half : half + 16, :].astype(F32)
    early, early_too = by_core(core, near_early, far_early)
    rows = []
    for kind in range(3):
        low_rows = [first, second] if kind < 2 else [early, early_too]
        low_start = 2 * kind if kind < 2 else 0
        low_rows = [block[low_start : low_start + 2] for block in low_rows]
        high_rows = [block[2 * kind + 2 : 2 * kind + 4] for block in (early, early_too)]
        rows.append(
            jnp.where(
                core == 0, jnp.concatenate(low_rows, axis=0), jnp.concatenate(high_rows, axis=0)
            )
        )
    rows += [early[8:14] + early_too[8:14], first[4:6] + second[4:6], jnp.zeros((4, width), F32)]
    small = jnp.concatenate(rows, axis=0).astype(LOW)
    total_ref = refs[-1]
    total_ref[:cut, :] = keep_ref[:cut, :] + recv_ref[:cut, :].astype(F32)
    total_ref[cut : width + half, :] = keep_ref[cut:, :] + other_ref[:start, :].astype(F32)
    total_ref[width + half :, :] = keep_out_ref[...] + recv_out_ref[:half, :].astype(F32)
    for step, target in enumerate(refs[-5:-1]):
        who = (lax.axis_index("dp") & 3) ^ step
        for z in range(8):
            begin = piece * (4 * z + who)
            if z >= 4:
                begin = width + (z - 4) // 2 * half + piece * (4 * (z % 2) + who)
            rows = pl.ds(pl.multiple_of(begin, 8), piece)
            target[piece * z : piece * (z + 1), :] = total_ref[rows, :].astype(target.dtype)
        target[8 * piece :, :] = small.astype(target.dtype)


def summed(sources, rows):
    return sum((source[rows, :].astype(F32) for source in sources[1:]), sources[0][rows, :])


def fold_kernel(*refs):
    kept_ref, up_ref, down_ref = refs[:3]
    rest_ref, rest_small_ref = refs[4:6]
    sends = refs[6:9]
    total_ref, group_ref = refs[9:]
    width = total_ref.shape[1]
    piece = width // 16
    long = 4 * piece
    half = width // 2
    block = 8 * piece
    total_ref[:block, :] = kept_ref[:block, :] + up_ref[:block, :].astype(F32)
    total_ref[block:, :] = kept_ref[block : 2 * block, :] + down_ref[...].astype(F32)
    plane = lax.axis_index("dp") & 3
    for index in range(2):
        start = 2 * block + 8 * index
        group_ref[plane ^ index] = kept_ref[start : start + 8, :]
        start = block + 8 * index
        group_ref[plane ^ (2 + index)] = up_ref[start : start + 8, :].astype(F32)
    ids = [group_ref[q, 0:1] for q in range(4)] + [jnp.zeros((4, width), F32)]
    small = jnp.concatenate(ids, axis=0).astype(LOW)
    rest_small_ref[...] = small
    for step, target in enumerate((rest_ref,) + tuple(sends)):
        who = (lax.axis_index("dp") >> 2) ^ step
        rows = pl.ds(pl.multiple_of(2 * piece * who, 8), 2 * piece)
        target[: 2 * piece, :] = total_ref[rows, :].astype(target.dtype)
        rows = pl.ds(pl.multiple_of(8 * piece + long * (who % 2), 8), long)
        down = total_ref[rows, :]
        down = jnp.where(who < 2, down[:, :half], down[:, half:])
        down = jnp.concatenate([down[: 2 * piece], down[2 * piece :]], axis=1)
        target[2 * piece : 4 * piece, :] = down.astype(target.dtype)
        if step:
            target[4 * piece :, :] = small


def fold_qkv_kernel(*refs):
    parts = refs[:4]
    rest_ref, rest_small_ref = refs[4:6]
    sends = refs[6:9]
    total_ref, late_ref = refs[9:]
    width = total_ref.shape[1]
    piece = width // 16
    half = width // 2
    total_ref[...] = summed(parts, slice(0, 8 * piece))
    for step, part in enumerate(parts):
        late_ref[(lax.axis_index("dp") & 3) ^ step] = part[8 * piece :, :].astype(F32)
    rows = [late_ref[q, :12] for q in range(4)]
    rows.append(late_ref[0, 12:20] + late_ref[1, 12:20] + late_ref[2, 12:20] + late_ref[3, 12:20])
    small = jnp.concatenate(rows, axis=0).astype(LOW)
    rest_small_ref[...] = small
    for step, target in enumerate((rest_ref,) + tuple(sends)):
        who = (lax.axis_index("dp") >> 2) ^ step

        def side(start):
            value = total_ref[pl.ds(pl.multiple_of(piece * (start + who % 2), 8), piece), :]
            return jnp.where(who < 2, value[:, :half], value[:, half:])

        target[:piece, :] = jnp.concatenate([side(6), side(4)], axis=1).astype(target.dtype)
        pair = total_ref[pl.ds(pl.multiple_of(piece * who, 8), piece), :]
        target[piece : 2 * piece, :] = pair.astype(target.dtype)
        if step:
            target[2 * piece :, :] = small


def one_hot(ids, lead):
    place = lax.broadcasted_iota(jnp.int32, (lead.shape[1], ids.shape[1]), 0)
    wanted = (ids // GROUPS_PER_RANK) * 8 + ids % GROUPS_PER_RANK
    return jnp.where(place == wanted, 1.0, 0.0).astype(LOW)


def group_rows(own_groups, kinds, kind_of):
    zeros = jnp.zeros_like(kind_of, F32)
    rows = []
    for kind in kinds:
        for one in own_groups:
            rows.append(jnp.where((kind_of == kind) & one, 1.0, zeros))
    for kind in kinds:
        rows.append(jnp.where(kind_of == kind, 1.0, zeros))
    while len(rows) % 8:
        rows.append(zeros)
    return jnp.concatenate(rows, axis=0).astype(LOW)


def split_dot(values, weight):
    high = values.astype(LOW)
    low = (values - high.astype(F32)).astype(LOW)
    both = nt(jnp.concatenate([high.astype(F32), low.astype(F32)], axis=0).astype(LOW), weight)
    return both[: values.shape[0]] + both[values.shape[0] :]


def finish_kernel(
    own_ref,
    own_small_ref,
    one_ref,
    two_ref,
    three_ref,
    lead_ref,
    recv_out_ref,
    recv_two_ref,
    recv_other_ref,
    output_ref,
    grad_tokens_ref,
    output_to,
    grad_tokens_to,
    up_ref,
    down_ref,
    silu_ref,
    ids_ref,
    stack_ref,
    sems,
):
    core = lax.axis_index("seq")
    width = own_ref.shape[1]
    piece = width // 16
    half = width // 2
    slots, half_len = output_to.shape[:2]
    count = slots // 2
    pairs = []
    for index in range(count):
        slot = (1 - core) * count + index
        start = recv_out_ref.shape[0] - (count - index) * half_len
        pairs.append((recv_out_ref.at[pl.ds(start, half_len)], output_to.at[slot]))
        source = (recv_two_ref, recv_other_ref)[index]
        start = source.shape[0] - half_len
        pairs.append((source.at[pl.ds(start, half_len)], grad_tokens_to.at[slot]))
        slot = core * count + index
        pairs.append((output_ref.at[index, pl.ds(0, half_len)], output_to.at[slot]))
        pairs.append((grad_tokens_ref.at[index, pl.ds(0, half_len)], grad_tokens_to.at[slot]))
    copies = fetch(pairs, sems)
    parts = (own_ref, one_ref, two_ref, three_ref)
    total = summed(parts, slice(0, 4 * piece))
    up_ref[...] = jnp.concatenate([total[:piece], total[piece : 2 * piece]], axis=1)
    down = total[2 * piece :]
    down_ref[...] = jnp.concatenate([down[:, :half], down[:, half:]], axis=0)
    line = lax.axis_index("dp") >> 2
    smalls = (own_small_ref[...],) + tuple(part[4 * piece :, :] for part in parts[1:])
    for step, small in enumerate(smalls):
        stack_ref[line ^ step] = small[:, :LANES].astype(F32)
    stack = stack_ref[...].reshape(32, LANES).astype(LOW)
    count = 192
    row = lax.broadcasted_iota(jnp.int32, (32, count), 0)
    chip = lax.broadcasted_iota(jnp.int32, (32, count), 1) // 12
    spread = tn(stack, jnp.where(row == chip + 4 * (chip // 4), 1.0, 0.0).astype(LOW))[:8]
    slot = lax.broadcasted_iota(jnp.int32, (8, count), 0)
    wanted = lax.broadcasted_iota(jnp.int32, (8, count), 1) % 4
    ids = column_sum(jnp.where(slot == wanted, spread, 0.0)).astype(jnp.int32)
    ids_ref[...] = ids
    lead = lead_ref[...]
    silu_ref[...] = nn(lead, one_hot(ids, lead)).astype(LOW)
    for copy in copies:
        copy.wait()


def late_kernel(
    own_small_ref,
    one_ref,
    two_ref,
    three_ref,
    ids_ref,
    ada_ref,
    stack_out_ref,
    own_sums_ref,
    send_ref,
    out_bias_ref,
    up_bias_ref,
    down_bias_ref,
    qv_ref,
    bias_ref,
):
    core = lax.axis_index("seq")
    width = own_small_ref.shape[1]
    piece = width // 16
    half = width // 2
    line = lax.axis_index("dp") >> 2
    smalls = (own_small_ref[...],) + tuple(
        part[2 * piece :, :] for part in (one_ref, two_ref, three_ref)
    )
    for step, small in enumerate(smalls):
        stack_out_ref[line ^ step] = small[:48]
        bias_ref[line ^ step] = small[48:].astype(F32)
    stack = stack_out_ref[...].reshape(192, width)
    ids = ids_ref[...]
    item = lax.broadcasted_iota(jnp.int32, (1, 192), 1) % 12
    base = GROUPS_PER_RANK * lax.axis_index("dp")
    own = [ids == base + index for index in range(GROUPS_PER_RANK)]
    sums = nn(group_rows(own, range(3), item // 4), stack)
    weight = ada_ref[:, pl.ds(pl.multiple_of(core * 3 * width, LANES), 3 * width)]
    own_sum = jnp.concatenate(
        [
            jnp.concatenate([sums[2 * kind : 2 * kind + 2] for kind in range(3)], axis=1),
            jnp.zeros((6, 3 * width), F32),
        ],
        axis=0,
    )
    cond = split_dot(own_sum, weight)
    low_cond, high_cond = cond[:2, :half], cond[:2, half:]
    kept = jnp.where(core == 0, low_cond, high_cond)
    sent = jnp.where(core == 0, high_cond, low_cond)
    zeros = jnp.zeros((2, half), F32)
    pad = jnp.zeros((3, width), F32)
    own_sums_ref[...] = jnp.concatenate(
        [jnp.concatenate([kept, zeros], axis=1), sums[6:9], pad], axis=0
    )
    send_ref[...] = jnp.concatenate(
        [jnp.concatenate([sent, zeros], axis=1), sums[6:9], pad], axis=0
    )
    bias = bias_ref[0] + bias_ref[1] + bias_ref[2] + bias_ref[3]
    out_bias_ref[...] = bias[0:1].reshape(width)
    up_bias_ref[...] = jnp.concatenate([bias[1 + row : 2 + row] for row in range(4)], axis=1).reshape(
        4 * width
    )
    down_bias_ref[...] = bias[5:6].reshape(width)
    qv_ref[...] = bias[6:8]


def rest_kernel(
    own_ref, one_ref, two_ref, three_ref, stack_ref, silu_ref, after_ref, out_ref, qkv_ref, ada_out_ref
):
    core = lax.axis_index("seq")
    width = own_ref.shape[1]
    piece = width // 16
    half = width // 2
    total = summed((own_ref, one_ref, two_ref, three_ref), slice(0, 2 * piece))
    out_ref[...] = total[:piece, :half]
    unit, pair = total[:piece, half:], total[piece:]
    qkv_ref[...] = jnp.where(
        core == 0,
        jnp.concatenate([pair, unit], axis=1),
        jnp.concatenate([unit, pair], axis=1),
    )
    stack = stack_ref[...].reshape(192, width)
    kind_of = lax.broadcasted_iota(jnp.int32, (1, 192), 1) % 12 // 4
    for kind in range(3):
        ada_out_ref[:, kind * width : (kind + 1) * width] = nn(
            masked(silu_ref[...], kind_of == kind), stack
        )


def final_kernel(own_ref, recv_ref, own_cond_ref, cond_ref, bias_ref):
    core = lax.axis_index("seq")
    width = own_ref.shape[1]
    half = width // 2
    near, far = own_ref[...], recv_ref[...]
    values = own_cond_ref[...].astype(F32)
    values = jnp.where(core == 0, values[:, :half], values[:, half:])
    gate = 1.0 / (1.0 + jnp.exp(-values))
    cond_ref[...] = (near[:2, :half] + far[:2, :half]) * (gate * (1.0 + values * (1.0 - gate)))
    rows = [block[row : row + 1] for block in by_core(core, near, far) for row in range(2, 5)]
    bias_ref[...] = jnp.concatenate(rows, axis=1).reshape(6 * width)


def silu_slope(values):
    sigmoid_val = jax.nn.sigmoid(values)
    return sigmoid_val * (1.0 + values * (1.0 - sigmoid_val))


def swap_cores(values):
    return lax.ppermute(values, "seq", CORE_SWAP)


def pick(core, first, second):
    return jnp.where(core == 0, first, second)


def to_patches(images, far, core):
    half_len = images.shape[1] // 2
    return pick(
        core,
        jnp.concatenate([images[:, :half_len], far], axis=0),
        jnp.concatenate([far, images[:, :half_len]], axis=0),
    )


def call(kernel, name, shapes, scratch, limit, spaces, *operands, aliases=None):
    chosen = {
        "s": pl.BlockSpec(memory_space=pltpu.SMEM),
        "v": pl.BlockSpec(memory_space=pltpu.VMEM),
        "V": pl.BlockSpec(memory_space=pltpu.VMEM),
        "a": pl.BlockSpec(memory_space=pl.ANY),
        "h": pl.BlockSpec(memory_space=pltpu.HBM),
    }
    pinned = {"h": pltpu.HBM, "V": pltpu.VMEM}
    into, out_of = spaces
    operands = [
        pltpu.with_memory_space_constraint(item, pinned[kind]) if kind in pinned else item
        for kind, item in zip(into, operands)
    ]
    return pl.pallas_call(
        kernel,
        out_shape=tuple(
            pinned.get(kind, jax.ShapeDtypeStruct)(shape, dtype)
            for kind, (shape, dtype) in zip(out_of, shapes)
        ),
        in_specs=[chosen[kind] for kind in into],
        out_specs=[chosen[kind] for kind in out_of],
        scratch_shapes=scratch,
        compiler_params=pltpu.CompilerParams(vmem_limit_bytes=limit << 20),
        cost_estimate=pl.CostEstimate(flops=1, bytes_accessed=1, transcendentals=0),
        input_output_aliases=aliases or {},
        name=name,
    )(*operands)


def rank_swap(values, step, count):
    return lax.ppermute(values, "dp", [(rank, rank ^ step) for rank in range(count)])


def owner_total(term, dp_count):
    blocks = term.astype(LOW).reshape(dp_count, term.shape[0] // dp_count, term.shape[1])
    return jnp.sum(lax.all_to_all(blocks, "dp", 0, 0, tiled=True).astype(F32), axis=0)


def general_tail(
    core, dp_count, dp_rank, sides, smalls, heads, cond_rows, cond, own_ids, ada_weight
):
    highest = lax.Precision.HIGHEST
    width, mod_width = ada_weight.shape
    half = width // 2
    (keep_one, send_one), (keep_out, send_out), (keep_two, send_two, send_other) = sides
    output, grad_tokens = heads
    small_one, small_two = smalls
    half_len = output.shape[1] // 2
    recv_out = swap_cores(send_out)
    first_sum = jnp.concatenate(
        [
            keep_one + swap_cores(send_one).astype(F32),
            keep_out + recv_out[:half].astype(F32),
        ],
        axis=0,
    )
    recv_two, recv_other = swap_cores(send_two), swap_cores(send_other)
    second_sum = keep_two + jnp.concatenate(
        [recv_two[:PIECE_ROWS], recv_other[: keep_two.shape[0] - PIECE_ROWS]], axis=0
    ).astype(F32)
    output_far = recv_out[half + 16 :].reshape(-1, half_len, width)
    grad_far = jnp.stack([item[-half_len:] for item in (recv_two, recv_other)])
    ff_half = first_sum.shape[0] - 2 * width - half
    up = jnp.concatenate([first_sum[:width], first_sum[width : 2 * width]], axis=1)
    down = first_sum[2 * width : 2 * width + ff_half]
    down = jnp.concatenate([down[:, :half], down[:, half:]], axis=0)
    out = first_sum[2 * width + ff_half :]
    out = jnp.concatenate([out[:, :half], out[:, half:]], axis=0)
    pair, unit = second_sum[:width], second_sum[width:]
    unit = jnp.concatenate([unit[:, :half], unit[:, half:]], axis=0)
    qkv = pick(
        core, jnp.concatenate([pair, unit], axis=1), jnp.concatenate([unit, pair], axis=1)
    )
    sums = [owner_total(term, dp_count) for term in (qkv, out, up, down)]
    image_grad = jnp.concatenate(
        [small_two[0:2], small_two[2:4], small_one[0:2], small_one[2:4], small_one[4:6], small_one[6:8]],
        axis=1,
    )
    biases = jnp.concatenate([small_two[4:6], small_one[8:14]], axis=0)
    marks = jnp.broadcast_to(own_ids.astype(F32)[:, None], (own_ids.shape[0], width))
    packed = jnp.concatenate([image_grad.reshape(-1, width), biases, marks], axis=0)
    gathered = lax.all_to_all(
        jnp.broadcast_to(packed[None], (2 * dp_count,) + packed.shape),
        ("dp", "seq"),
        0,
        0,
        tiled=True,
    )
    grad_rows = gathered[:, :12].reshape(-1, mod_width)
    bias_sums = jnp.sum(gathered[:, 12:20], axis=0)
    all_ids = gathered[:, 20:, 0].reshape(-1).astype(jnp.int32)
    group_count = cond_rows.shape[0]
    all_hot = (all_ids[:, None] == jnp.arange(group_count, dtype=jnp.int32)[None, :]).astype(F32)
    group_grad = jnp.dot(all_hot.T, grad_rows, precision=highest)
    own_rows = width // dp_count
    silu_rows = lax.reduce_precision(jax.nn.silu(cond_rows.astype(F32)), 8, 7)
    silu_part = lax.dynamic_slice_in_dim(silu_rows, dp_rank * own_rows, own_rows, 1)
    grad_half = pick(core, group_grad[:, : mod_width // 2], group_grad[:, mod_width // 2 :])
    ada_sum = jnp.dot(silu_part.T, grad_half, precision=highest)
    own_grad = lax.dynamic_slice_in_dim(
        group_grad, dp_rank * GROUPS_PER_RANK, GROUPS_PER_RANK, 0
    )
    ada_half = lax.dynamic_slice_in_dim(ada_weight, core * half, half, 0).astype(F32)
    cond_half = pick(core, cond[:, :half], cond[:, half:]).astype(F32)
    grad_cond = silu_slope(cond_half) * jnp.dot(own_grad, ada_half.T, precision=highest)
    return (
        to_patches(output, output_far, core),
        to_patches(grad_tokens, grad_far, core),
        grad_cond,
        sums[0],
        bias_sums[:2],
        sums[1],
        bias_sums[2],
        sums[2],
        bias_sums[3:7].reshape(-1),
        sums[3],
        bias_sums[7],
        ada_sum,
        jnp.sum(grad_rows, axis=0),
    )


def body(
    tokens,
    cotangent,
    cond,
    group_ids,
    image_counts,
    patch_mask,
    qkv_weight,
    qv_bias,
    out_weight,
    out_bias,
    up_weight,
    up_bias,
    down_weight,
    down_bias,
    ada_weight,
    ada_bias,
):
    slot_count, half_len, width = tokens.shape
    ff_width = up_weight.shape[1]
    mod_width = ada_weight.shape[1]
    dp_count = lax.axis_size("dp")
    core = lax.axis_index("seq").astype(jnp.int32)
    dp_rank = lax.axis_index("dp").astype(jnp.int32)
    image_count = slot_count // 2
    length = 2 * half_len
    row_count = image_count * length
    half = width // 2
    piece = width // dp_count
    fast = dp_count == 16 and not GENERAL
    cond_blocks = lax.all_to_all(
        jnp.broadcast_to(cond[None], (dp_count,) + cond.shape),
        "dp",
        0,
        0,
        axis_index_groups=[list(range(dp_count))[::-1]],
        tiled=True,
    )
    tokens_far = swap_cores(tokens)
    cot_far = swap_cores(cotangent)
    image_shape = (image_count, length, width)
    half_shape = (image_count, half_len, width)
    vmem = pltpu.VMEM
    (
        images,
        penalty,
        hot,
        marks,
        qkv_b_row,
        out_b_row,
        up_b_row,
        down_b_row,
        ada_weight_near,
        ada_b_row,
    ) = call(
        load_kernel,
        "load",
        (
            (image_shape, LOW),
            ((8, length), F32),
            ((8, 8 * dp_count), LOW),
            ((8, width), F32),
            ((1, 3 * width), F32),
            ((1, width), F32),
            ((1, ff_width), F32),
            ((1, width), F32),
            (ada_weight.shape, LOW),
            ((1, mod_width), F32),
        ),
        [
            pltpu.SMEM(group_ids.shape, jnp.int32),
            pltpu.SMEM(image_counts.shape, jnp.int32),
            vmem(patch_mask.shape, jnp.int32),
            vmem(qv_bias.shape, LOW),
            vmem(out_bias.shape, LOW),
            vmem(up_bias.shape, LOW),
            vmem(down_bias.shape, LOW),
            vmem(ada_bias.shape, LOW),
            pltpu.SemaphoreType.DMA((9 + 2 * image_count,)),
        ],
        12,
        ("hVha" + "h" * 7, "V" * 10),
        tokens,
        tokens_far,
        group_ids,
        image_counts,
        patch_mask,
        qv_bias,
        out_bias,
        up_bias,
        down_bias,
        ada_weight,
        ada_bias,
    )
    (
        qkv,
        h1,
        normed,
        inverse,
        image_mod,
        lead,
        logs,
        att,
        middle,
        attn,
        act,
        grad_pre,
        valid,
        cot_images,
        qkv_weight_near,
        out_weight_near,
        up_weight_near,
        down_weight_near,
        keep_one,
        send_one,
        small_early,
    ) = call(
        partial(forward_kernel, piece if fast else 0),
        "forward_and_ffn_grads",
        (
            ((row_count, 3 * width), LOW),
            ((row_count, width), LOW),
            ((row_count, width), F32),
            ((row_count, LANES), F32),
            ((8, mod_width), LOW),
            ((24, 8 * dp_count), LOW),
            ((row_count, HEADS * LANES), F32),
            ((row_count, width), LOW),
            ((row_count, width), F32),
            ((row_count, width), F32),
            ((row_count, ff_width), LOW),
            ((row_count, ff_width), LOW),
            ((row_count, LANES), F32),
            (image_shape, LOW),
            (qkv_weight.shape, LOW),
            (out_weight.shape, LOW),
            (up_weight.shape, LOW),
            (down_weight.shape, LOW),
            ((2 * width + ff_width // 2, width), F32),
            ((2 * width + ff_width // 2, width), LOW),
            ((16, width), F32),
        ),
        [
            vmem((8 * dp_count, width), F32),
            vmem((width, 8 * dp_count), F32),
            vmem((row_count, width), LOW),
            vmem((row_count, width), LOW),
            pltpu.SemaphoreType.DMA((4 + 2 * image_count,)),
        ],
        24,
        ("V" * 10 + "h" * 5, "V" * 21),
        cond_blocks,
        images,
        cot_far,
        penalty,
        hot,
        qkv_b_row,
        out_b_row,
        up_b_row,
        ada_weight_near,
        ada_b_row,
        cotangent,
        qkv_weight,
        out_weight,
        up_weight,
        down_weight,
    )
    output, grad_att, grad_mid, keep_out, send_out, small_one = call(
        finish_forward_kernel,
        "norm_back",
        (
            (image_shape, LOW),
            ((row_count, width), LOW),
            ((row_count, width), F32),
            ((half, width), F32),
            ((half + 16 + row_count // 2, width), LOW),
            ((16, width), F32),
        ),
        [vmem((row_count, width), LOW)],
        16,
        ("V" * 13, "V" * 6),
        image_mod,
        att,
        middle,
        attn,
        act,
        grad_pre,
        valid,
        cot_images,
        out_weight_near,
        up_weight_near,
        down_weight_near,
        down_b_row,
        small_early,
    )

    def attention_back(*after):
        return call(
            backward_kernel,
            "attention_back",
            (
                (image_shape, LOW),
                ((width + half, width), F32),
                ((PIECE_ROWS + half_len, width), LOW),
                ((width + half + 8 - PIECE_ROWS + half_len, width), LOW),
                ((8, width), F32),
            ),
            [vmem((row_count, 3 * width), LOW)],
            24,
            ("V" * 10 + "aaa", "VVVVV"),
            normed,
            inverse,
            penalty,
            logs,
            qkv_weight_near,
            qkv,
            h1,
            grad_att,
            grad_mid,
            image_mod,
            *after,
        )

    if not fast:
        grad_tokens, keep_two, send_two, send_other, small_two = attention_back(
            small_one, keep_one, keep_out
        )
        own_ids = lax.dynamic_slice_in_dim(group_ids, core * image_count, image_count, 0)
        return general_tail(
            core,
            dp_count,
            dp_rank,
            ((keep_one, send_one), (keep_out, send_out), (keep_two, send_two, send_other)),
            (small_one, small_two),
            (output, grad_tokens),
            cond_blocks[::-1].reshape(-1, width),
            cond,
            own_ids,
            ada_weight,
        )

    recv_one = swap_cores(send_one)
    recv_out = swap_cores(send_out)
    block_rows = 8 * piece
    own_up, own_down, sent_up, sent_down = call(
        split_kernel,
        "split_plane",
        (
            ((2 * block_rows, width), F32),
            ((2 * block_rows, width), F32),
            ((2 * block_rows + 8, width), LOW),
            ((2 * block_rows, width), LOW),
        ),
        [],
        16,
        ("VVV", "VVVV"),
        keep_one,
        recv_one,
        marks,
    )
    near_up, near_down = rank_swap(sent_up, 1, 16), rank_swap(sent_down, 2, 16)
    grad_tokens, keep_two, send_two, send_other, small_two = attention_back(
        sent_up, sent_down, recv_out
    )
    kept, cross_up, cross_down = call(
        cross_kernel,
        "cross_plane",
        (
            ((2 * block_rows + 16, width), F32),
            ((block_rows + 16, width), LOW),
            ((block_rows, width), LOW),
        ),
        [],
        16,
        ("VVVVVa", "VVV"),
        own_up,
        own_down,
        near_up,
        near_down,
        marks,
        small_two,
    )
    near_up, near_down = rank_swap(cross_up, 2, 16), rank_swap(cross_down, 1, 16)
    recv_two, recv_other = swap_cores(send_two), swap_cores(send_other)
    split_rows = 8 * piece + 24
    own_qkv, *sent_qkv = call(
        split_qkv_kernel,
        "split_qkv_plane",
        (((split_rows, width), F32),) + (((split_rows, width), LOW),) * 3,
        [vmem((2 * width, width), F32)],
        16,
        ("VVVVVVVa", "VVVV"),
        keep_two,
        recv_two,
        recv_other,
        small_two,
        keep_out,
        recv_out,
        small_one,
        cross_up,
    )
    near_qkv = [rank_swap(item, step + 1, 16) for step, item in enumerate(sent_qkv)]
    line_rows = 4 * piece + 8
    rest, rest_ids, *lines = call(
        fold_kernel,
        "fold_plane",
        (((4 * piece, width), F32), ((8, width), LOW)) + (((line_rows, width), LOW),) * 3,
        [vmem((16 * piece, width), F32), vmem((4, 8, width), F32)],
        16,
        ("VVVa", "VVVVV"),
        kept,
        near_up,
        near_down,
        sent_qkv[2],
    )
    lines = [rank_swap(item, 4 * (step + 1), 16) for step, item in enumerate(lines)]
    line_rows = 2 * piece + 56
    rest_qkv, rest_small, *lines_qkv = call(
        fold_qkv_kernel,
        "fold_qkv_plane",
        (((2 * piece, width), F32), ((56, width), LOW)) + (((line_rows, width), LOW),) * 3,
        [vmem((8 * piece, width), F32), vmem((4, 24, width), F32)],
        16,
        ("VVVV", "VVVVV"),
        own_qkv,
        *near_qkv,
    )
    lines_qkv = [rank_swap(item, 4 * (step + 1), 16) for step, item in enumerate(lines_qkv)]
    output, grad_tokens, up_sum, down_sum, silu_rows, all_ids = call(
        finish_kernel,
        "finish_line",
        (
            (tokens.shape, LOW),
            (tokens.shape, LOW),
            ((piece, ff_width // 2), F32),
            ((4 * piece, half), F32),
            ((piece, 192), LOW),
            ((1, 192), jnp.int32),
        ),
        [vmem((4, 8, LANES), F32), pltpu.SemaphoreType.DMA((4 * image_count,))],
        16,
        ("V" * 11, "hhvvVV"),
        rest,
        rest_ids,
        *lines,
        lead,
        recv_out,
        recv_two,
        recv_other,
        output,
        grad_tokens,
    )
    (
        stack,
        own_sums,
        send_sums,
        out_bias_sum,
        up_bias_sum,
        down_bias_sum,
        qv_sum,
    ) = call(
        late_kernel,
        "late_groups",
        (
            ((4, 48, width), LOW),
            ((8, width), F32),
            ((8, width), F32),
            ((width,), F32),
            ((ff_width,), F32),
            ((width,), F32),
            ((2, width), F32),
        ),
        [vmem((4, 8, width), F32)],
        16,
        ("V" * 6, "VVVvvvv"),
        rest_small,
        *lines_qkv,
        all_ids,
        ada_weight_near,
    )
    out_sum, qkv_sum, ada_sum = call(
        rest_kernel,
        "rest_sums",
        (((piece, half), F32), ((piece, 3 * half), F32), ((piece, mod_width // 2), F32)),
        [],
        16,
        ("VVVVVVa", "vvv"),
        rest_qkv,
        *lines_qkv,
        stack,
        silu_rows,
        send_sums,
    )
    grad_cond, ada_bias_sum = call(
        final_kernel,
        "final_groups",
        (((GROUPS_PER_RANK, half), F32), ((mod_width,), F32)),
        [],
        16,
        ("VVv", "vv"),
        own_sums,
        swap_cores(send_sums),
        cond,
    )
    return (
        output,
        grad_tokens,
        grad_cond,
        qkv_sum,
        qv_sum,
        out_sum,
        out_bias_sum,
        up_sum,
        up_bias_sum,
        down_sum,
        down_bias_sum,
        ada_sum,
        ada_bias_sum,
    )


def solution(mesh):
    placed = (
        P("dp", "seq", None),
        P("dp", "seq", None),
        P("dp", None),
        P("dp"),
        P("dp"),
        P("dp", None),
        P(),
        P(),
        P(),
        P(),
        P(),
        P(),
        P(),
        P(),
        P(),
        P(),
    )
    return jax.shard_map(
        body,
        mesh=mesh,
        in_specs=placed,
        out_specs=(
            P("dp", "seq", None),
            P("dp", "seq", None),
            P("dp", "seq"),
            P("dp", "seq"),
            P(),
            P("dp", "seq"),
            P(),
            P("dp", "seq"),
            P(),
            P("dp", "seq"),
            P(),
            P("dp", "seq"),
            P(),
        ),
        check_vma=False,
    )
```

```python
from functools import partial

import jax
import jax.numpy as jnp
from jax import lax
from jax.experimental import pallas as pl
from jax.experimental.pallas import tpu as pltpu
from jax.sharding import PartitionSpec as P

HEADS = 6
HEAD_DIM = 64
PAIR = 2 * HEAD_DIM
CORE_SWAP = ((0, 1), (1, 0))
CHUNK = 256
LANES = 128
GROUPS_PER_RANK = 2
GENERAL = False
PIECE_ROWS = 288
PLANE_STEPS = (3, 1, 2)
LINE_STEPS = (2, 3, 1)
F32 = jnp.float32
LOW = jnp.bfloat16


def nn(left, right):
    return lax.dot_general(left, right, (((1,), (0,)), ((), ())), preferred_element_type=F32)


def nt(left, right):
    return lax.dot_general(left, right, (((1,), (1,)), ((), ())), preferred_element_type=F32)


def tn(left, right):
    return lax.dot_general(left, right, (((0,), (0,)), ((), ())), preferred_element_type=F32)


def normalize(values):
    center = values - jnp.mean(values, axis=-1, keepdims=True)
    spread = jnp.mean(center * center, axis=-1, keepdims=True)
    inverse = lax.rsqrt(spread + 1e-06)
    return center * inverse, inverse


def norm_back(grad, normed, inverse):
    return inverse * (
        grad
        - jnp.mean(grad, axis=-1, keepdims=True)
        - normed * jnp.mean(grad * normed, axis=-1, keepdims=True)
    )


def column_sum(values):
    return jnp.sum(values, axis=0, keepdims=True)


def head_masks(rows):
    lane = lax.broadcasted_iota(jnp.int32, (rows, PAIR), 1)
    return lane < HEAD_DIM, lane >= HEAD_DIM


def masked(values, mask):
    return jnp.where(mask, values, jnp.zeros_like(values))


def fetch(pairs, sems):
    copies = []
    for index, (source, target) in enumerate(pairs):
        copy = pltpu.make_async_copy(source, target, sems.at[index])
        copy.start()
        copies.append(copy)
    return copies


def own_images(near_ref, far_ref, target_ref, first_image):
    half_len = near_ref.shape[1]
    pairs = []
    for image in range(target_ref.shape[0]):
        slot = first_image + image
        pairs.append((near_ref.at[slot], target_ref.at[image, pl.ds(0, half_len)]))
        pairs.append((far_ref.at[slot], target_ref.at[image, pl.ds(half_len, half_len)]))
    return pairs


def own_marks(mask_ref, counts_ref, core, image, image_count, half_len):
    slot = core * image_count + image
    live = jnp.where(slot < counts_ref[0], 1.0, 0.0)
    marks = mask_ref[pl.ds(slot, 1), :].astype(F32) * live
    low_marks, high_marks = marks[:, :half_len], marks[:, half_len:]
    return jnp.concatenate(
        [
            jnp.where(core == 0, low_marks, high_marks),
            jnp.where(core == 0, high_marks, low_marks),
        ],
        axis=1,
    )


def as_row(ref):
    return ref[...].astype(F32).reshape(1, ref.shape[0])


def load_kernel(
    tokens_hbm,
    tokens_far_ref,
    ids_hbm,
    counts_hbm,
    mask_hbm,
    qv_b_hbm,
    out_b_hbm,
    up_b_hbm,
    down_b_hbm,
    ada_w_hbm,
    ada_b_hbm,
    images_ref,
    penalty_ref,
    hot_ref,
    marks_ref,
    qkv_b_ref,
    out_b_ref,
    up_b_ref,
    down_b_ref,
    ada_w_ref,
    ada_b_ref,
    ids_ref,
    counts_ref,
    mask_ref,
    qv_b_ref,
    out_b_raw,
    up_b_raw,
    down_b_raw,
    ada_b_raw,
    sems,
):
    core = lax.axis_index("seq")
    image_count, length, width = images_ref.shape
    half_len = length // 2
    first_image = core * image_count
    copies = fetch(
        [
            (ids_hbm, ids_ref),
            (counts_hbm, counts_ref),
            (mask_hbm, mask_ref),
            (qv_b_hbm, qv_b_ref),
            (out_b_hbm, out_b_raw),
            (up_b_hbm, up_b_raw),
            (down_b_hbm, down_b_raw),
            (ada_b_hbm, ada_b_raw),
            (ada_w_hbm, ada_w_ref),
        ]
        + own_images(tokens_hbm, tokens_far_ref, images_ref, first_image),
        sems,
    )
    for copy in copies[:8]:
        copy.wait()
    row = lax.broadcasted_iota(jnp.int32, hot_ref.shape, 0)
    column = lax.broadcasted_iota(jnp.int32, hot_ref.shape, 1)
    lane = lax.broadcasted_iota(jnp.int32, marks_ref.shape, 1)
    hot = jnp.zeros(hot_ref.shape, F32)
    marks = jnp.zeros(marks_ref.shape, F32)
    for slot in range(2 * image_count):
        marks = jnp.where(lane == slot, ids_ref[slot].astype(F32), marks)
    marks_ref[...] = marks
    penalty_ref[...] = jnp.zeros_like(penalty_ref)
    for image in range(image_count):
        group = ids_ref[first_image + image]
        place = 8 * (group // GROUPS_PER_RANK) + group % GROUPS_PER_RANK
        hot = jnp.where((row == image) & (column == place), 1.0, hot)
        own = own_marks(mask_ref, counts_ref, core, image, image_count, half_len)
        penalty_ref[image : image + 1, :] = (own - 1.0) * 30000.0
    hot_ref[...] = hot.astype(LOW)
    qkv_b_ref[...] = jnp.concatenate(
        [qv_b_ref[0:1, :], jnp.zeros((1, width), LOW), qv_b_ref[1:2, :]], axis=1
    ).astype(F32)
    for raw, target in (
        (out_b_raw, out_b_ref),
        (up_b_raw, up_b_ref),
        (down_b_raw, down_b_ref),
        (ada_b_raw, ada_b_ref),
    ):
        target[...] = as_row(raw)
    for copy in copies[8:]:
        copy.wait()


def attention_pair(step, qkv_ref, penalty_ref, length, width):
    image, pair = divmod(step, HEADS // 2)
    rows = slice(image * length, (image + 1) * length)

    def lanes(which):
        start = which * width + pair * PAIR
        return slice(start, start + PAIR)

    queries = qkv_ref[rows, lanes(0)] * jnp.asarray(HEAD_DIM**-0.5, LOW)
    return rows, lanes, queries, qkv_ref[rows, lanes(1)], qkv_ref[rows, lanes(2)]


def image_rows(image, length):
    return slice(image * length, (image + 1) * length)


def mod_part(mod_ref, image, which, width):
    return mod_ref[image : image + 1, which * width : (which + 1) * width].astype(F32)


def wide_column(column_ref, rows, width):
    return jnp.concatenate([column_ref[rows, :]] * (width // LANES), axis=1)


def forward_kernel(
    lead_rows,
    cond_ref,
    images_ref,
    cot_far_ref,
    penalty_ref,
    hot_ref,
    qkv_b_ref,
    out_b_ref,
    up_b_ref,
    ada_w_ref,
    ada_b_ref,
    cot_hbm,
    qkv_w_hbm,
    out_w_hbm,
    up_w_hbm,
    down_w_hbm,
    qkv_ref,
    h1_ref,
    normed_ref,
    inverse_ref,
    mod_ref,
    lead_ref,
    logs_ref,
    att_ref,
    mid_ref,
    attn_ref,
    act_ref,
    gpre_ref,
    valid_ref,
    cot_ref,
    qkv_w_ref,
    out_w_ref,
    up_w_ref,
    down_w_ref,
    keep_ref,
    send_ref,
    small_ref,
    cond_rows_ref,
    turned_ref,
    h2_ref,
    gffn_ref,
    sems,
):
    core = lax.axis_index("seq")
    image_count, length, width = images_ref.shape
    half_len = length // 2
    half = width // 2
    ff_width = up_w_ref.shape[1]
    copies = fetch(
        [
            (qkv_w_hbm, qkv_w_ref),
            (out_w_hbm, out_w_ref),
            (up_w_hbm, up_w_ref),
            (down_w_hbm, down_w_ref),
        ]
        + own_images(cot_hbm, cot_far_ref, cot_ref, core * image_count),
        sems,
    )
    block_count, block_rows = cond_ref.shape[:2]
    cond_rows_ref[...] = jnp.zeros_like(cond_rows_ref)
    for block in range(block_count):
        start = 8 * (block_count - 1 - block)
        cond_rows_ref[start : start + block_rows, :] = cond_ref[block].astype(F32)
    cond = cond_rows_ref[...]
    silu = cond / (1.0 + jnp.exp(-cond))
    image_silu = nn(hot_ref[...], silu.astype(LOW)).astype(LOW)
    mod_ref[...] = (nn(image_silu, ada_w_ref[...]) + ada_b_ref[...]).astype(LOW)

    def part(image, which):
        return mod_part(mod_ref, image, which, width)

    copies[0].wait()
    for image in range(image_count):
        rows = image_rows(image, length)
        normed, inverse = normalize(images_ref[image].astype(F32))
        normed_ref[rows, :] = normed
        inverse_ref[rows, :] = jnp.broadcast_to(inverse, (length, LANES))
        marks = jnp.where(penalty_ref[image : image + 1, :] < 0.0, 0.0, 1.0)
        valid_ref[rows, :] = jnp.broadcast_to(marks, (LANES, length)).T
        h1 = (normed * (1.0 + part(image, 1)) + part(image, 0)).astype(LOW)
        h1_ref[rows, :] = h1
        qkv_ref[rows, :] = (nn(h1, qkv_w_ref[...]) + qkv_b_ref[...]).astype(LOW)

    first, second = head_masks(length)
    for step in range(image_count * (HEADS // 2)):
        rows, lanes, queries, keys, values = attention_pair(
            step, qkv_ref, penalty_ref, length, width
        )
        image = step // (HEADS // 2)
        penalty = penalty_ref[image : image + 1, :]
        total = jnp.zeros((length, PAIR), F32)
        for side, mask in enumerate((first, second)):
            scores = nt(masked(queries, mask), keys) + penalty
            top = jnp.max(scores, axis=-1, keepdims=True)
            exps = jnp.exp(scores - top)
            whole = jnp.sum(exps, axis=-1, keepdims=True)
            head = 2 * (step % (HEADS // 2)) + side
            logs_ref[rows, head * LANES : (head + 1) * LANES] = jnp.broadcast_to(
                top + jnp.log(whole), (length, LANES)
            )
            total = total + nn((exps / whole).astype(LOW), masked(values, mask))
        att_ref[rows, lanes(0)] = total.astype(LOW)

    for copy in copies[1:]:
        copy.wait()
    if lead_rows:
        turned_ref[...] = silu.T
        start = pl.multiple_of(lax.axis_index("dp") * lead_rows, 8)
        lead_ref[...] = turned_ref[pl.ds(start, lead_rows), :].astype(LOW)
    else:
        lead_ref[...] = jnp.zeros_like(lead_ref)
    small_ref[...] = jnp.zeros_like(small_ref)
    down_bias_grad = jnp.zeros((1, width), F32)
    for image in range(image_count):
        rows = image_rows(image, length)
        valid = wide_column(valid_ref, rows, width)
        attn = nn(att_ref[rows, :], out_w_ref[...]) + out_b_ref[...]
        attn_ref[rows, :] = attn
        middle = images_ref[image].astype(F32) + valid * part(image, 2) * attn
        mid_ref[rows, :] = middle
        normed, _ = normalize(middle)
        h2_ref[rows, :] = (normed * (1.0 + part(image, 4)) + part(image, 3)).astype(LOW)
        grad_ffn = (valid * part(image, 5) * cot_ref[image].astype(F32)).astype(LOW)
        gffn_ref[rows, :] = grad_ffn
        down_bias_grad = down_bias_grad + column_sum(grad_ffn.astype(F32))
    small_ref[13:14, :] = down_bias_grad

    for chunk in range(ff_width // CHUNK):
        columns = slice(chunk * CHUNK, (chunk + 1) * CHUNK)
        up_w = up_w_ref[:, columns]
        down_w = down_w_ref[columns, :]
        bias = jnp.zeros((1, CHUNK), F32)
        for image in range(image_count):
            rows = image_rows(image, length)
            pre = nn(h2_ref[rows, :], up_w) + up_b_ref[:, columns]
            square = pre * pre
            inner = jnp.tanh(pre * (0.7978845608028654 + 0.035677408136300125 * square))
            cdf = 0.5 * inner + 0.5
            act_ref[rows, columns] = (pre * cdf).astype(LOW)
            slope = 0.5 * (pre * (0.7978845608028654 + 0.10703222440890037 * square)) * (
                1.0 - inner * inner
            ) + cdf
            grad_pre = (nt(gffn_ref[rows, :], down_w) * slope).astype(LOW)
            gpre_ref[rows, columns] = grad_pre
            bias = bias + column_sum(grad_pre.astype(F32))
        for tile in range(CHUNK // LANES):
            start = chunk * CHUNK + tile * LANES
            small_ref[9 + start // width : 10 + start // width, start % width : start % width + LANES] = (
                bias[:, tile * LANES : (tile + 1) * LANES]
            )

    first_half = gffn_ref[:, :half]
    second_half = gffn_ref[:, half:]
    gffn_keep = jnp.where(core == 0, first_half, second_half)
    gffn_send = jnp.where(core == 0, second_half, first_half)
    side_chunks = ff_width // CHUNK // 2
    for step in range(side_chunks):
        low = slice(step * CHUNK, (step + 1) * CHUNK)
        high = slice((step + side_chunks) * CHUNK, (step + side_chunks + 1) * CHUNK)
        up_low = tn(h2_ref[...], gpre_ref[:, low])
        up_high = tn(h2_ref[...], gpre_ref[:, high])
        up_keep = jnp.where(core == 0, up_low, up_high)
        up_send = jnp.where(core == 0, up_high, up_low).astype(LOW)
        for tile in range(CHUNK // LANES):
            start = step * CHUNK + tile * LANES
            rows = slice(start // width * width, (start // width + 1) * width)
            columns = slice(start % width, start % width + LANES)
            keep_ref[rows, columns] = up_keep[:, tile * LANES : (tile + 1) * LANES]
            send_ref[rows, columns] = up_send[:, tile * LANES : (tile + 1) * LANES]
        rows = slice(2 * width + step * CHUNK, 2 * width + (step + 1) * CHUNK)
        for target, side in ((keep_ref, gffn_keep), (send_ref, gffn_send)):
            target[rows, :] = jnp.concatenate(
                [tn(act_ref[:, low], side), tn(act_ref[:, high], side)], axis=1
            ).astype(target.dtype)


def finish_forward_kernel(
    mod_ref,
    att_ref,
    mid_ref,
    attn_ref,
    act_ref,
    gpre_ref,
    valid_ref,
    cot_ref,
    out_w_ref,
    up_w_ref,
    down_w_ref,
    down_b_ref,
    early_ref,
    output_ref,
    grad_att_ref,
    grad_mid_ref,
    keep_ref,
    send_ref,
    small_ref,
    gattn_ref,
):
    core = lax.axis_index("seq")
    image_count, length, width = cot_ref.shape
    half_len = length // 2
    half = width // 2
    small_ref[...] = early_ref[...]

    def part(image, which):
        return mod_part(mod_ref, image, which, width)

    out_bias_grad = jnp.zeros((1, width), F32)
    for image in range(image_count):
        rows = image_rows(image, length)
        valid = wide_column(valid_ref, rows, width)
        upstream = cot_ref[image].astype(F32)
        middle = mid_ref[rows, :]
        ffn = nn(act_ref[rows, :], down_w_ref[...]) + down_b_ref[...]
        output_ref[image] = (middle + valid * part(image, 5) * ffn).astype(LOW)
        small_ref[6 + image : 7 + image, :] = column_sum(valid * ffn * upstream)
        normed, inverse = normalize(middle)
        grad_h2 = nt(gpre_ref[rows, :], up_w_ref[...])
        small_ref[2 + image : 3 + image, :] = column_sum(grad_h2)
        small_ref[4 + image : 5 + image, :] = column_sum(grad_h2 * normed)
        grad_mid = upstream + norm_back(grad_h2 * (1.0 + part(image, 4)), normed, inverse)
        grad_mid_ref[rows, :] = grad_mid
        small_ref[image : image + 1, :] = column_sum(valid * attn_ref[rows, :] * grad_mid)
        grad_attn = (valid * part(image, 2) * grad_mid).astype(LOW)
        gattn_ref[rows, :] = grad_attn
        out_bias_grad = out_bias_grad + column_sum(grad_attn.astype(F32))
        grad_att_ref[rows, :] = nt(grad_attn, out_w_ref[...]).astype(LOW)
    small_ref[8:9, :] = out_bias_grad
    out_term = tn(att_ref[...], gattn_ref[...])
    out_first = jnp.concatenate([out_term[:half, :half], out_term[half:, :half]], axis=1)
    out_second = jnp.concatenate([out_term[:half, half:], out_term[half:, half:]], axis=1)
    keep_ref[...] = jnp.where(core == 0, out_first, out_second)
    send_ref[:half, :] = jnp.where(core == 0, out_second, out_first).astype(LOW)
    send_ref[half : half + 16, :] = small_ref[...].astype(LOW)
    for image in range(image_count):
        start = half + 16 + image * half_len
        send_ref[start : start + half_len, :] = output_ref[image, half_len:, :]


def backward_kernel(
    normed_ref,
    inverse_ref,
    penalty_ref,
    logs_ref,
    qkv_w_ref,
    qkv_ref,
    h1_ref,
    grad_att_ref,
    grad_mid_ref,
    mod_ref,
    after_ref,
    after_too_ref,
    after_all_ref,
    grad_tokens_ref,
    keep_ref,
    send_ref,
    other_ref,
    small_ref,
    gqkv_ref,
):
    core = lax.axis_index("seq")
    image_count, length, width = grad_tokens_ref.shape
    half_len = length // 2
    half = width // 2
    first, second = head_masks(length)
    for step in range(image_count * (HEADS // 2)):
        rows, lanes, queries, keys, values = attention_pair(
            step, qkv_ref, penalty_ref, length, width
        )
        image = step // (HEADS // 2)
        penalty = penalty_ref[image : image + 1, :]
        grad_att = grad_att_ref[rows, lanes(0)]
        grad_q = jnp.zeros((length, PAIR), F32)
        grad_k = jnp.zeros((length, PAIR), F32)
        grad_v = jnp.zeros((length, PAIR), F32)
        for side, mask in enumerate((first, second)):
            own_queries = masked(queries, mask)
            own_grad = masked(grad_att, mask)
            head = 2 * (step % (HEADS // 2)) + side
            logs = logs_ref[rows, head * LANES : (head + 1) * LANES]
            logs = jnp.concatenate([logs] * (length // LANES), axis=1)
            probs = jnp.exp(nt(own_queries, keys) + penalty - logs)
            grad_probs = nt(own_grad, values)
            dots = jnp.sum(probs * grad_probs, axis=-1, keepdims=True)
            grad_scores = (probs * (grad_probs - dots)).astype(LOW)
            grad_v = grad_v + tn(probs.astype(LOW), own_grad)
            grad_q = grad_q + nn(grad_scores, masked(keys, mask))
            grad_k = grad_k + tn(grad_scores, own_queries)
        gqkv_ref[rows, lanes(0)] = (grad_q * HEAD_DIM**-0.5).astype(LOW)
        gqkv_ref[rows, lanes(1)] = grad_k.astype(LOW)
        gqkv_ref[rows, lanes(2)] = grad_v.astype(LOW)

    def part(image, which):
        return mod_ref[image : image + 1, which * width : (which + 1) * width].astype(F32)

    small_ref[...] = jnp.zeros_like(small_ref)
    small_ref[4:5, :] = column_sum(gqkv_ref[:, :width].astype(F32))
    small_ref[5:6, :] = column_sum(gqkv_ref[:, 2 * width :].astype(F32))
    for image in range(image_count):
        rows = slice(image * length, (image + 1) * length)
        normed = normed_ref[rows, :]
        inverse = jnp.concatenate([inverse_ref[rows, :]] * (width // LANES), axis=1)
        grad_h1 = nt(gqkv_ref[rows, :], qkv_w_ref[...])
        small_ref[image : image + 1, :] = column_sum(grad_h1)
        small_ref[2 + image : 3 + image, :] = column_sum(grad_h1 * normed)
        grad_in = norm_back(grad_h1 * (1.0 + part(image, 1)), normed, inverse)
        grad_tokens_ref[image] = (grad_mid_ref[rows, :] + grad_in).astype(LOW)
    low_term = tn(h1_ref[...], gqkv_ref[:, :width])
    high_term = tn(h1_ref[...], gqkv_ref[:, 2 * width :])
    keep_ref[:width, :] = jnp.where(core == 0, low_term, high_term)
    pair = jnp.where(core == 0, high_term, low_term).astype(LOW)
    term = tn(h1_ref[...], gqkv_ref[:, width : 2 * width])
    low_unit = jnp.concatenate([term[:half, :half], term[half:, :half]], axis=1)
    high_unit = jnp.concatenate([term[:half, half:], term[half:, half:]], axis=1)
    keep_ref[width:, :] = jnp.where(core == 0, low_unit, high_unit)
    cut = send_ref.shape[0] - half_len
    send_ref[:cut, :] = pair[:cut]
    send_ref[cut:, :] = grad_tokens_ref[0, half_len:, :]
    start = width - cut
    other_ref[:start, :] = pair[cut:]
    other_ref[start : start + half, :] = jnp.where(core == 0, high_unit, low_unit).astype(LOW)
    start += half
    other_ref[start : start + 8, :] = small_ref[...].astype(LOW)
    other_ref[start + 8 :, :] = grad_tokens_ref[1, half_len:, :]


def by_core(core, near, far):
    return [jnp.where(core == 0, near, far), jnp.where(core == 0, far, near)]


def split_kernel(
    keep_ref, recv_ref, marks_ref, own_up_ref, own_down_ref, send_up_ref, send_down_ref
):
    width = keep_ref.shape[1]
    piece = width // 16
    long = 4 * piece
    block = 8 * piece
    plane = lax.axis_index("dp") & 3

    def move(target, start, size, to):
        rows = pl.ds(pl.multiple_of(start, 8), size)
        target[to : to + size, :] = (keep_ref[rows, :] + recv_ref[rows, :].astype(F32)).astype(
            target.dtype
        )

    for target, steps in ((own_up_ref, (0, 2)), (send_up_ref, (1, 3))):
        for index, step in enumerate(steps):
            who = plane ^ step
            for z in range(4):
                for side in range(2):
                    start = side * width + piece * (4 * z + who)
                    move(target, start, piece, index * block + (2 * z + side) * piece)
    for target, steps in ((own_down_ref, (0, 1)), (send_down_ref, (2, 3))):
        for index, step in enumerate(steps):
            who = plane ^ step
            for z in range(2):
                start = 2 * width + long * (4 * z + who)
                move(target, start, long, index * block + z * long)
    send_up_ref[2 * block :, :] = marks_ref[...].astype(LOW)


def cross_kernel(
    own_up_ref,
    own_down_ref,
    recv_up_ref,
    recv_down_ref,
    marks_ref,
    after_ref,
    kept_ref,
    send_up_ref,
    send_down_ref,
):
    block = own_up_ref.shape[0] // 2
    first, second = slice(0, block), slice(block, 2 * block)
    kept_ref[first, :] = own_up_ref[first, :] + recv_up_ref[first, :].astype(F32)
    kept_ref[second, :] = own_down_ref[first, :] + recv_down_ref[first, :].astype(F32)
    kept_ref[2 * block : 2 * block + 8, :] = marks_ref[...].astype(LOW).astype(F32)
    kept_ref[2 * block + 8 :, :] = recv_up_ref[2 * block :, :].astype(F32)
    send_up_ref[first, :] = (own_up_ref[second, :] + recv_up_ref[second, :].astype(F32)).astype(LOW)
    send_up_ref[block : block + 8, :] = marks_ref[...].astype(LOW)
    send_up_ref[block + 8 :, :] = recv_up_ref[2 * block :, :]
    send_down_ref[...] = (own_down_ref[second, :] + recv_down_ref[second, :].astype(F32)).astype(LOW)


def split_qkv_kernel(
    keep_ref, recv_ref, other_ref, small_ref, keep_out_ref, recv_out_ref, early_ref, *refs
):
    core = lax.axis_index("seq")
    width = keep_ref.shape[1]
    piece = width // 16
    half = width // 2
    cut = PIECE_ROWS
    start = keep_ref.shape[0] - cut
    near = small_ref[...].astype(LOW).astype(F32)
    far = other_ref[start : start + 8, :].astype(F32)
    first, second = by_core(core, near, far)
    near_early = early_ref[...].astype(LOW).astype(F32)
    far_early = recv_out_ref[half : half + 16, :].astype(F32)
    early, early_too = by_core(core, near_early, far_early)
    rows = []
    for kind in range(3):
        low_rows = [first, second] if kind < 2 else [early, early_too]
        low_start = 2 * kind if kind < 2 else 0
        low_rows = [block[low_start : low_start + 2] for block in low_rows]
        high_rows = [block[2 * kind + 2 : 2 * kind + 4] for block in (early, early_too)]
        rows.append(
            jnp.where(
                core == 0, jnp.concatenate(low_rows, axis=0), jnp.concatenate(high_rows, axis=0)
            )
        )
    rows += [early[8:14] + early_too[8:14], first[4:6] + second[4:6], jnp.zeros((4, width), F32)]
    small = jnp.concatenate(rows, axis=0).astype(LOW)
    total_ref = refs[-1]
    total_ref[:cut, :] = keep_ref[:cut, :] + recv_ref[:cut, :].astype(F32)
    total_ref[cut : width + half, :] = keep_ref[cut:, :] + other_ref[:start, :].astype(F32)
    total_ref[width + half :, :] = keep_out_ref[...] + recv_out_ref[:half, :].astype(F32)
    for step, target in zip((0,) + PLANE_STEPS, refs[-5:-1]):
        who = (lax.axis_index("dp") & 3) ^ step
        for z in range(8):
            begin = piece * (4 * z + who)
            if z >= 4:
                begin = width + (z - 4) // 2 * half + piece * (4 * (z % 2) + who)
            rows = pl.ds(pl.multiple_of(begin, 8), piece)
            target[piece * z : piece * (z + 1), :] = total_ref[rows, :].astype(target.dtype)
        target[8 * piece :, :] = small.astype(target.dtype)


def summed(sources, rows):
    return sum((source[rows, :].astype(F32) for source in sources[1:]), sources[0][rows, :])


def fold_kernel(*refs):
    kept_ref, up_ref, down_ref = refs[:3]
    rest_ref, rest_small_ref = refs[4:6]
    sends = refs[6:9]
    total_ref, group_ref = refs[9:]
    width = total_ref.shape[1]
    piece = width // 16
    long = 4 * piece
    half = width // 2
    block = 8 * piece
    total_ref[:block, :] = kept_ref[:block, :] + up_ref[:block, :].astype(F32)
    total_ref[block:, :] = kept_ref[block : 2 * block, :] + down_ref[...].astype(F32)
    plane = lax.axis_index("dp") & 3
    for index in range(2):
        start = 2 * block + 8 * index
        group_ref[plane ^ index] = kept_ref[start : start + 8, :]
        start = block + 8 * index
        group_ref[plane ^ (2 + index)] = up_ref[start : start + 8, :].astype(F32)
    ids = [group_ref[q, 0:1] for q in range(4)] + [jnp.zeros((4, width), F32)]
    small = jnp.concatenate(ids, axis=0).astype(LOW)
    rest_small_ref[...] = small
    for step, target in zip((0,) + LINE_STEPS, (rest_ref,) + tuple(sends)):
        who = (lax.axis_index("dp") >> 2) ^ step
        rows = pl.ds(pl.multiple_of(2 * piece * who, 8), 2 * piece)
        target[: 2 * piece, :] = total_ref[rows, :].astype(target.dtype)
        rows = pl.ds(pl.multiple_of(8 * piece + long * (who % 2), 8), long)
        down = total_ref[rows, :]
        down = jnp.where(who < 2, down[:, :half], down[:, half:])
        down = jnp.concatenate([down[: 2 * piece], down[2 * piece :]], axis=1)
        target[2 * piece : 4 * piece, :] = down.astype(target.dtype)
        if step:
            target[4 * piece :, :] = small


def fold_qkv_kernel(*refs):
    parts = refs[:4]
    rest_ref, rest_small_ref = refs[4:6]
    sends = refs[6:9]
    total_ref, late_ref = refs[9:]
    width = total_ref.shape[1]
    piece = width // 16
    half = width // 2
    total_ref[...] = summed(parts, slice(0, 8 * piece))
    for step, part in zip((0,) + PLANE_STEPS, parts):
        late_ref[(lax.axis_index("dp") & 3) ^ step] = part[8 * piece :, :].astype(F32)
    rows = [late_ref[q, :12] for q in range(4)]
    rows.append(late_ref[0, 12:20] + late_ref[1, 12:20] + late_ref[2, 12:20] + late_ref[3, 12:20])
    small = jnp.concatenate(rows, axis=0).astype(LOW)
    rest_small_ref[...] = small
    for step, target in zip((0,) + LINE_STEPS, (rest_ref,) + tuple(sends)):
        who = (lax.axis_index("dp") >> 2) ^ step

        def side(start):
            value = total_ref[pl.ds(pl.multiple_of(piece * (start + who % 2), 8), piece), :]
            return jnp.where(who < 2, value[:, :half], value[:, half:])

        target[:piece, :] = jnp.concatenate([side(6), side(4)], axis=1).astype(target.dtype)
        pair = total_ref[pl.ds(pl.multiple_of(piece * who, 8), piece), :]
        target[piece : 2 * piece, :] = pair.astype(target.dtype)
        if step:
            target[2 * piece :, :] = small


def one_hot(ids, lead):
    place = lax.broadcasted_iota(jnp.int32, (lead.shape[1], ids.shape[1]), 0)
    wanted = (ids // GROUPS_PER_RANK) * 8 + ids % GROUPS_PER_RANK
    return jnp.where(place == wanted, 1.0, 0.0).astype(LOW)


def group_rows(own_groups, kinds, kind_of):
    zeros = jnp.zeros_like(kind_of, F32)
    rows = []
    for kind in kinds:
        for one in own_groups:
            rows.append(jnp.where((kind_of == kind) & one, 1.0, zeros))
    for kind in kinds:
        rows.append(jnp.where(kind_of == kind, 1.0, zeros))
    while len(rows) % 8:
        rows.append(zeros)
    return jnp.concatenate(rows, axis=0).astype(LOW)


def split_dot(values, weight):
    high = values.astype(LOW)
    low = (values - high.astype(F32)).astype(LOW)
    both = nt(jnp.concatenate([high.astype(F32), low.astype(F32)], axis=0).astype(LOW), weight)
    return both[: values.shape[0]] + both[values.shape[0] :]


def finish_kernel(
    own_ref,
    own_small_ref,
    one_ref,
    two_ref,
    three_ref,
    lead_ref,
    recv_out_ref,
    recv_two_ref,
    recv_other_ref,
    output_ref,
    grad_tokens_ref,
    output_to,
    grad_tokens_to,
    up_ref,
    down_ref,
    silu_ref,
    ids_ref,
    stack_ref,
    sems,
):
    core = lax.axis_index("seq")
    width = own_ref.shape[1]
    piece = width // 16
    half = width // 2
    slots, half_len = output_to.shape[:2]
    count = slots // 2
    pairs = []
    for index in range(count):
        slot = (1 - core) * count + index
        start = recv_out_ref.shape[0] - (count - index) * half_len
        pairs.append((recv_out_ref.at[pl.ds(start, half_len)], output_to.at[slot]))
        source = (recv_two_ref, recv_other_ref)[index]
        start = source.shape[0] - half_len
        pairs.append((source.at[pl.ds(start, half_len)], grad_tokens_to.at[slot]))
        slot = core * count + index
        pairs.append((output_ref.at[index, pl.ds(0, half_len)], output_to.at[slot]))
        pairs.append((grad_tokens_ref.at[index, pl.ds(0, half_len)], grad_tokens_to.at[slot]))
    copies = fetch(pairs, sems)
    parts = (own_ref, one_ref, two_ref, three_ref)
    total = summed(parts, slice(0, 4 * piece))
    up_ref[...] = jnp.concatenate([total[:piece], total[piece : 2 * piece]], axis=1)
    down = total[2 * piece :]
    down_ref[...] = jnp.concatenate([down[:, :half], down[:, half:]], axis=0)
    line = lax.axis_index("dp") >> 2
    smalls = (own_small_ref[...],) + tuple(part[4 * piece :, :] for part in parts[1:])
    for step, small in zip((0,) + LINE_STEPS, smalls):
        stack_ref[line ^ step] = small[:, :LANES].astype(F32)
    stack = stack_ref[...].reshape(32, LANES).astype(LOW)
    count = 192
    row = lax.broadcasted_iota(jnp.int32, (32, count), 0)
    chip = lax.broadcasted_iota(jnp.int32, (32, count), 1) // 12
    spread = tn(stack, jnp.where(row == chip + 4 * (chip // 4), 1.0, 0.0).astype(LOW))[:8]
    slot = lax.broadcasted_iota(jnp.int32, (8, count), 0)
    wanted = lax.broadcasted_iota(jnp.int32, (8, count), 1) % 4
    ids = column_sum(jnp.where(slot == wanted, spread, 0.0)).astype(jnp.int32)
    ids_ref[...] = ids
    lead = lead_ref[...]
    silu_ref[...] = nn(lead, one_hot(ids, lead)).astype(LOW)
    for copy in copies:
        copy.wait()


def late_kernel(
    own_small_ref,
    one_ref,
    two_ref,
    three_ref,
    ids_ref,
    ada_ref,
    stack_out_ref,
    own_sums_ref,
    send_ref,
    out_bias_ref,
    up_bias_ref,
    down_bias_ref,
    qv_ref,
    bias_ref,
):
    core = lax.axis_index("seq")
    width = own_small_ref.shape[1]
    piece = width // 16
    half = width // 2
    line = lax.axis_index("dp") >> 2
    smalls = (own_small_ref[...],) + tuple(
        part[2 * piece :, :] for part in (one_ref, two_ref, three_ref)
    )
    for step, small in zip((0,) + LINE_STEPS, smalls):
        stack_out_ref[line ^ step] = small[:48]
        bias_ref[line ^ step] = small[48:].astype(F32)
    stack = stack_out_ref[...].reshape(192, width)
    ids = ids_ref[...]
    item = lax.broadcasted_iota(jnp.int32, (1, 192), 1) % 12
    base = GROUPS_PER_RANK * lax.axis_index("dp")
    own = [ids == base + index for index in range(GROUPS_PER_RANK)]
    sums = nn(group_rows(own, range(3), item // 4), stack)
    weight = ada_ref[:, pl.ds(pl.multiple_of(core * 3 * width, LANES), 3 * width)]
    own_sum = jnp.concatenate(
        [
            jnp.concatenate([sums[2 * kind : 2 * kind + 2] for kind in range(3)], axis=1),
            jnp.zeros((6, 3 * width), F32),
        ],
        axis=0,
    )
    cond = split_dot(own_sum, weight)
    low_cond, high_cond = cond[:2, :half], cond[:2, half:]
    kept = jnp.where(core == 0, low_cond, high_cond)
    sent = jnp.where(core == 0, high_cond, low_cond)
    zeros = jnp.zeros((2, half), F32)
    pad = jnp.zeros((3, width), F32)
    own_sums_ref[...] = jnp.concatenate(
        [jnp.concatenate([kept, zeros], axis=1), sums[6:9], pad], axis=0
    )
    send_ref[...] = jnp.concatenate(
        [jnp.concatenate([sent, zeros], axis=1), sums[6:9], pad], axis=0
    )
    bias = bias_ref[0] + bias_ref[1] + bias_ref[2] + bias_ref[3]
    out_bias_ref[...] = bias[0:1].reshape(width)
    up_bias_ref[...] = jnp.concatenate([bias[1 + row : 2 + row] for row in range(4)], axis=1).reshape(
        4 * width
    )
    down_bias_ref[...] = bias[5:6].reshape(width)
    qv_ref[...] = bias[6:8]


def rest_kernel(
    own_ref, one_ref, two_ref, three_ref, stack_ref, silu_ref, after_ref, out_ref, qkv_ref, ada_out_ref
):
    core = lax.axis_index("seq")
    width = own_ref.shape[1]
    piece = width // 16
    half = width // 2
    total = summed((own_ref, one_ref, two_ref, three_ref), slice(0, 2 * piece))
    out_ref[...] = total[:piece, :half]
    unit, pair = total[:piece, half:], total[piece:]
    qkv_ref[...] = jnp.where(
        core == 0,
        jnp.concatenate([pair, unit], axis=1),
        jnp.concatenate([unit, pair], axis=1),
    )
    stack = stack_ref[...].reshape(192, width)
    kind_of = lax.broadcasted_iota(jnp.int32, (1, 192), 1) % 12 // 4
    for kind in range(3):
        ada_out_ref[:, kind * width : (kind + 1) * width] = nn(
            masked(silu_ref[...], kind_of == kind), stack
        )


def final_kernel(own_ref, recv_ref, own_cond_ref, cond_ref, bias_ref):
    core = lax.axis_index("seq")
    width = own_ref.shape[1]
    half = width // 2
    near, far = own_ref[...], recv_ref[...]
    values = own_cond_ref[...].astype(F32)
    values = jnp.where(core == 0, values[:, :half], values[:, half:])
    gate = 1.0 / (1.0 + jnp.exp(-values))
    cond_ref[...] = (near[:2, :half] + far[:2, :half]) * (gate * (1.0 + values * (1.0 - gate)))
    rows = [block[row : row + 1] for block in by_core(core, near, far) for row in range(2, 5)]
    bias_ref[...] = jnp.concatenate(rows, axis=1).reshape(6 * width)


def silu_slope(values):
    sigmoid_val = jax.nn.sigmoid(values)
    return sigmoid_val * (1.0 + values * (1.0 - sigmoid_val))


def swap_cores(values):
    return lax.ppermute(values, "seq", CORE_SWAP)


def pick(core, first, second):
    return jnp.where(core == 0, first, second)


def to_patches(images, far, core):
    half_len = images.shape[1] // 2
    return pick(
        core,
        jnp.concatenate([images[:, :half_len], far], axis=0),
        jnp.concatenate([far, images[:, :half_len]], axis=0),
    )


def call(kernel, name, shapes, scratch, limit, spaces, *operands, aliases=None):
    chosen = {
        "s": pl.BlockSpec(memory_space=pltpu.SMEM),
        "v": pl.BlockSpec(memory_space=pltpu.VMEM),
        "V": pl.BlockSpec(memory_space=pltpu.VMEM),
        "a": pl.BlockSpec(memory_space=pl.ANY),
        "h": pl.BlockSpec(memory_space=pltpu.HBM),
    }
    pinned = {"h": pltpu.HBM, "V": pltpu.VMEM}
    into, out_of = spaces
    operands = [
        pltpu.with_memory_space_constraint(item, pinned[kind]) if kind in pinned else item
        for kind, item in zip(into, operands)
    ]
    return pl.pallas_call(
        kernel,
        out_shape=tuple(
            pinned.get(kind, jax.ShapeDtypeStruct)(shape, dtype)
            for kind, (shape, dtype) in zip(out_of, shapes)
        ),
        in_specs=[chosen[kind] for kind in into],
        out_specs=[chosen[kind] for kind in out_of],
        scratch_shapes=scratch,
        compiler_params=pltpu.CompilerParams(vmem_limit_bytes=limit << 20),
        cost_estimate=pl.CostEstimate(flops=1, bytes_accessed=1, transcendentals=0),
        input_output_aliases=aliases or {},
        name=name,
    )(*operands)


def rank_swap(values, step, count):
    return lax.ppermute(values, "dp", [(rank, rank ^ step) for rank in range(count)])


def owner_total(term, dp_count):
    blocks = term.astype(LOW).reshape(dp_count, term.shape[0] // dp_count, term.shape[1])
    return jnp.sum(lax.all_to_all(blocks, "dp", 0, 0, tiled=True).astype(F32), axis=0)


def general_tail(
    core, dp_count, dp_rank, sides, smalls, heads, cond_rows, cond, own_ids, ada_weight
):
    highest = lax.Precision.HIGHEST
    width, mod_width = ada_weight.shape
    half = width // 2
    (keep_one, send_one), (keep_out, send_out), (keep_two, send_two, send_other) = sides
    output, grad_tokens = heads
    small_one, small_two = smalls
    half_len = output.shape[1] // 2
    recv_out = swap_cores(send_out)
    first_sum = jnp.concatenate(
        [
            keep_one + swap_cores(send_one).astype(F32),
            keep_out + recv_out[:half].astype(F32),
        ],
        axis=0,
    )
    recv_two, recv_other = swap_cores(send_two), swap_cores(send_other)
    second_sum = keep_two + jnp.concatenate(
        [recv_two[:PIECE_ROWS], recv_other[: keep_two.shape[0] - PIECE_ROWS]], axis=0
    ).astype(F32)
    output_far = recv_out[half + 16 :].reshape(-1, half_len, width)
    grad_far = jnp.stack([item[-half_len:] for item in (recv_two, recv_other)])
    ff_half = first_sum.shape[0] - 2 * width - half
    up = jnp.concatenate([first_sum[:width], first_sum[width : 2 * width]], axis=1)
    down = first_sum[2 * width : 2 * width + ff_half]
    down = jnp.concatenate([down[:, :half], down[:, half:]], axis=0)
    out = first_sum[2 * width + ff_half :]
    out = jnp.concatenate([out[:, :half], out[:, half:]], axis=0)
    pair, unit = second_sum[:width], second_sum[width:]
    unit = jnp.concatenate([unit[:, :half], unit[:, half:]], axis=0)
    qkv = pick(
        core, jnp.concatenate([pair, unit], axis=1), jnp.concatenate([unit, pair], axis=1)
    )
    sums = [owner_total(term, dp_count) for term in (qkv, out, up, down)]
    image_grad = jnp.concatenate(
        [small_two[0:2], small_two[2:4], small_one[0:2], small_one[2:4], small_one[4:6], small_one[6:8]],
        axis=1,
    )
    biases = jnp.concatenate([small_two[4:6], small_one[8:14]], axis=0)
    marks = jnp.broadcast_to(own_ids.astype(F32)[:, None], (own_ids.shape[0], width))
    packed = jnp.concatenate([image_grad.reshape(-1, width), biases, marks], axis=0)
    gathered = lax.all_to_all(
        jnp.broadcast_to(packed[None], (2 * dp_count,) + packed.shape),
        ("dp", "seq"),
        0,
        0,
        tiled=True,
    )
    grad_rows = gathered[:, :12].reshape(-1, mod_width)
    bias_sums = jnp.sum(gathered[:, 12:20], axis=0)
    all_ids = gathered[:, 20:, 0].reshape(-1).astype(jnp.int32)
    group_count = cond_rows.shape[0]
    all_hot = (all_ids[:, None] == jnp.arange(group_count, dtype=jnp.int32)[None, :]).astype(F32)
    group_grad = jnp.dot(all_hot.T, grad_rows, precision=highest)
    own_rows = width // dp_count
    silu_rows = lax.reduce_precision(jax.nn.silu(cond_rows.astype(F32)), 8, 7)
    silu_part = lax.dynamic_slice_in_dim(silu_rows, dp_rank * own_rows, own_rows, 1)
    grad_half = pick(core, group_grad[:, : mod_width // 2], group_grad[:, mod_width // 2 :])
    ada_sum = jnp.dot(silu_part.T, grad_half, precision=highest)
    own_grad = lax.dynamic_slice_in_dim(
        group_grad, dp_rank * GROUPS_PER_RANK, GROUPS_PER_RANK, 0
    )
    ada_half = lax.dynamic_slice_in_dim(ada_weight, core * half, half, 0).astype(F32)
    cond_half = pick(core, cond[:, :half], cond[:, half:]).astype(F32)
    grad_cond = silu_slope(cond_half) * jnp.dot(own_grad, ada_half.T, precision=highest)
    return (
        to_patches(output, output_far, core),
        to_patches(grad_tokens, grad_far, core),
        grad_cond,
        sums[0],
        bias_sums[:2],
        sums[1],
        bias_sums[2],
        sums[2],
        bias_sums[3:7].reshape(-1),
        sums[3],
        bias_sums[7],
        ada_sum,
        jnp.sum(grad_rows, axis=0),
    )


def body(
    tokens,
    cotangent,
    cond,
    group_ids,
    image_counts,
    patch_mask,
    qkv_weight,
    qv_bias,
    out_weight,
    out_bias,
    up_weight,
    up_bias,
    down_weight,
    down_bias,
    ada_weight,
    ada_bias,
):
    slot_count, half_len, width = tokens.shape
    ff_width = up_weight.shape[1]
    mod_width = ada_weight.shape[1]
    dp_count = lax.axis_size("dp")
    core = lax.axis_index("seq").astype(jnp.int32)
    dp_rank = lax.axis_index("dp").astype(jnp.int32)
    image_count = slot_count // 2
    length = 2 * half_len
    row_count = image_count * length
    half = width // 2
    piece = width // dp_count
    fast = dp_count == 16 and not GENERAL
    cond_blocks = lax.all_to_all(
        jnp.broadcast_to(cond[None], (dp_count,) + cond.shape),
        "dp",
        0,
        0,
        axis_index_groups=[list(range(dp_count))[::-1]],
        tiled=True,
    )
    tokens_far = swap_cores(tokens)
    cot_far = swap_cores(cotangent)
    image_shape = (image_count, length, width)
    half_shape = (image_count, half_len, width)
    vmem = pltpu.VMEM
    (
        images,
        penalty,
        hot,
        marks,
        qkv_b_row,
        out_b_row,
        up_b_row,
        down_b_row,
        ada_weight_near,
        ada_b_row,
    ) = call(
        load_kernel,
        "load",
        (
            (image_shape, LOW),
            ((8, length), F32),
            ((8, 8 * dp_count), LOW),
            ((8, width), F32),
            ((1, 3 * width), F32),
            ((1, width), F32),
            ((1, ff_width), F32),
            ((1, width), F32),
            (ada_weight.shape, LOW),
            ((1, mod_width), F32),
        ),
        [
            pltpu.SMEM(group_ids.shape, jnp.int32),
            pltpu.SMEM(image_counts.shape, jnp.int32),
            vmem(patch_mask.shape, jnp.int32),
            vmem(qv_bias.shape, LOW),
            vmem(out_bias.shape, LOW),
            vmem(up_bias.shape, LOW),
            vmem(down_bias.shape, LOW),
            vmem(ada_bias.shape, LOW),
            pltpu.SemaphoreType.DMA((9 + 2 * image_count,)),
        ],
        12,
        ("hVha" + "h" * 7, "V" * 10),
        tokens,
        tokens_far,
        group_ids,
        image_counts,
        patch_mask,
        qv_bias,
        out_bias,
        up_bias,
        down_bias,
        ada_weight,
        ada_bias,
    )
    (
        qkv,
        h1,
        normed,
        inverse,
        image_mod,
        lead,
        logs,
        att,
        middle,
        attn,
        act,
        grad_pre,
        valid,
        cot_images,
        qkv_weight_near,
        out_weight_near,
        up_weight_near,
        down_weight_near,
        keep_one,
        send_one,
        small_early,
    ) = call(
        partial(forward_kernel, piece if fast else 0),
        "forward_and_ffn_grads",
        (
            ((row_count, 3 * width), LOW),
            ((row_count, width), LOW),
            ((row_count, width), F32),
            ((row_count, LANES), F32),
            ((8, mod_width), LOW),
            ((24, 8 * dp_count), LOW),
            ((row_count, HEADS * LANES), F32),
            ((row_count, width), LOW),
            ((row_count, width), F32),
            ((row_count, width), F32),
            ((row_count, ff_width), LOW),
            ((row_count, ff_width), LOW),
            ((row_count, LANES), F32),
            (image_shape, LOW),
            (qkv_weight.shape, LOW),
            (out_weight.shape, LOW),
            (up_weight.shape, LOW),
            (down_weight.shape, LOW),
            ((2 * width + ff_width // 2, width), F32),
            ((2 * width + ff_width // 2, width), LOW),
            ((16, width), F32),
        ),
        [
            vmem((8 * dp_count, width), F32),
            vmem((width, 8 * dp_count), F32),
            vmem((row_count, width), LOW),
            vmem((row_count, width), LOW),
            pltpu.SemaphoreType.DMA((4 + 2 * image_count,)),
        ],
        24,
        ("V" * 10 + "h" * 5, "V" * 21),
        cond_blocks,
        images,
        cot_far,
        penalty,
        hot,
        qkv_b_row,
        out_b_row,
        up_b_row,
        ada_weight_near,
        ada_b_row,
        cotangent,
        qkv_weight,
        out_weight,
        up_weight,
        down_weight,
    )
    output, grad_att, grad_mid, keep_out, send_out, small_one = call(
        finish_forward_kernel,
        "norm_back",
        (
            (image_shape, LOW),
            ((row_count, width), LOW),
            ((row_count, width), F32),
            ((half, width), F32),
            ((half + 16 + row_count // 2, width), LOW),
            ((16, width), F32),
        ),
        [vmem((row_count, width), LOW)],
        16,
        ("V" * 13, "V" * 6),
        image_mod,
        att,
        middle,
        attn,
        act,
        grad_pre,
        valid,
        cot_images,
        out_weight_near,
        up_weight_near,
        down_weight_near,
        down_b_row,
        small_early,
    )

    def attention_back(*after):
        return call(
            backward_kernel,
            "attention_back",
            (
                (image_shape, LOW),
                ((width + half, width), F32),
                ((PIECE_ROWS + half_len, width), LOW),
                ((width + half + 8 - PIECE_ROWS + half_len, width), LOW),
                ((8, width), F32),
            ),
            [vmem((row_count, 3 * width), LOW)],
            24,
            ("V" * 10 + "aaa", "VVVVV"),
            normed,
            inverse,
            penalty,
            logs,
            qkv_weight_near,
            qkv,
            h1,
            grad_att,
            grad_mid,
            image_mod,
            *after,
        )

    if not fast:
        grad_tokens, keep_two, send_two, send_other, small_two = attention_back(
            small_one, keep_one, keep_out
        )
        own_ids = lax.dynamic_slice_in_dim(group_ids, core * image_count, image_count, 0)
        return general_tail(
            core,
            dp_count,
            dp_rank,
            ((keep_one, send_one), (keep_out, send_out), (keep_two, send_two, send_other)),
            (small_one, small_two),
            (output, grad_tokens),
            cond_blocks[::-1].reshape(-1, width),
            cond,
            own_ids,
            ada_weight,
        )

    recv_one = swap_cores(send_one)
    recv_out = swap_cores(send_out)
    block_rows = 8 * piece
    own_up, own_down, sent_up, sent_down = call(
        split_kernel,
        "split_plane",
        (
            ((2 * block_rows, width), F32),
            ((2 * block_rows, width), F32),
            ((2 * block_rows + 8, width), LOW),
            ((2 * block_rows, width), LOW),
        ),
        [],
        16,
        ("VVV", "VVVV"),
        keep_one,
        recv_one,
        marks,
    )
    near_up, near_down = rank_swap(sent_up, 1, 16), rank_swap(sent_down, 2, 16)
    grad_tokens, keep_two, send_two, send_other, small_two = attention_back(
        sent_up, sent_down, recv_out
    )
    kept, cross_up, cross_down = call(
        cross_kernel,
        "cross_plane",
        (
            ((2 * block_rows + 16, width), F32),
            ((block_rows + 16, width), LOW),
            ((block_rows, width), LOW),
        ),
        [],
        16,
        ("VVVVVa", "VVV"),
        own_up,
        own_down,
        near_up,
        near_down,
        marks,
        small_two,
    )
    near_up, near_down = rank_swap(cross_up, 2, 16), rank_swap(cross_down, 1, 16)
    recv_two, recv_other = swap_cores(send_two), swap_cores(send_other)
    split_rows = 8 * piece + 24
    own_qkv, *sent_qkv = call(
        split_qkv_kernel,
        "split_qkv_plane",
        (((split_rows, width), F32),) + (((split_rows, width), LOW),) * 3,
        [vmem((2 * width, width), F32)],
        16,
        ("VVVVVVVa", "VVVV"),
        keep_two,
        recv_two,
        recv_other,
        small_two,
        keep_out,
        recv_out,
        small_one,
        cross_up,
    )
    near_qkv = [rank_swap(item, step, 16) for step, item in zip(PLANE_STEPS, sent_qkv)]
    line_rows = 4 * piece + 8
    rest, rest_ids, *lines = call(
        fold_kernel,
        "fold_plane",
        (((4 * piece, width), F32), ((8, width), LOW)) + (((line_rows, width), LOW),) * 3,
        [vmem((16 * piece, width), F32), vmem((4, 8, width), F32)],
        16,
        ("VVVa", "VVVVV"),
        kept,
        near_up,
        near_down,
        sent_qkv[2],
    )
    lines = [rank_swap(item, 4 * step, 16) for step, item in zip(LINE_STEPS, lines)]
    line_rows = 2 * piece + 56
    rest_qkv, rest_small, *lines_qkv = call(
        fold_qkv_kernel,
        "fold_qkv_plane",
        (((2 * piece, width), F32), ((56, width), LOW)) + (((line_rows, width), LOW),) * 3,
        [vmem((8 * piece, width), F32), vmem((4, 24, width), F32)],
        16,
        ("VVVV", "VVVVV"),
        own_qkv,
        *near_qkv,
    )
    lines_qkv = [rank_swap(item, 4 * step, 16) for step, item in zip(LINE_STEPS, lines_qkv)]
    output, grad_tokens, up_sum, down_sum, silu_rows, all_ids = call(
        finish_kernel,
        "finish_line",
        (
            (tokens.shape, LOW),
            (tokens.shape, LOW),
            ((piece, ff_width // 2), F32),
            ((4 * piece, half), F32),
            ((piece, 192), LOW),
            ((1, 192), jnp.int32),
        ),
        [vmem((4, 8, LANES), F32), pltpu.SemaphoreType.DMA((4 * image_count,))],
        16,
        ("V" * 11, "hhvvVV"),
        rest,
        rest_ids,
        *lines,
        lead,
        recv_out,
        recv_two,
        recv_other,
        output,
        grad_tokens,
    )
    (
        stack,
        own_sums,
        send_sums,
        out_bias_sum,
        up_bias_sum,
        down_bias_sum,
        qv_sum,
    ) = call(
        late_kernel,
        "late_groups",
        (
            ((4, 48, width), LOW),
            ((8, width), F32),
            ((8, width), F32),
            ((width,), F32),
            ((ff_width,), F32),
            ((width,), F32),
            ((2, width), F32),
        ),
        [vmem((4, 8, width), F32)],
        16,
        ("V" * 6, "VVVvvvv"),
        rest_small,
        *lines_qkv,
        all_ids,
        ada_weight_near,
    )
    out_sum, qkv_sum, ada_sum = call(
        rest_kernel,
        "rest_sums",
        (((piece, half), F32), ((piece, 3 * half), F32), ((piece, mod_width // 2), F32)),
        [],
        16,
        ("VVVVVVa", "vvv"),
        rest_qkv,
        *lines_qkv,
        stack,
        silu_rows,
        send_sums,
    )
    grad_cond, ada_bias_sum = call(
        final_kernel,
        "final_groups",
        (((GROUPS_PER_RANK, half), F32), ((mod_width,), F32)),
        [],
        16,
        ("VVv", "vv"),
        own_sums,
        swap_cores(send_sums),
        cond,
    )
    return (
        output,
        grad_tokens,
        grad_cond,
        qkv_sum,
        qv_sum,
        out_sum,
        out_bias_sum,
        up_sum,
        up_bias_sum,
        down_sum,
        down_bias_sum,
        ada_sum,
        ada_bias_sum,
    )


def solution(mesh):
    placed = (
        P("dp", "seq", None),
        P("dp", "seq", None),
        P("dp", None),
        P("dp"),
        P("dp"),
        P("dp", None),
        P(),
        P(),
        P(),
        P(),
        P(),
        P(),
        P(),
        P(),
        P(),
        P(),
    )
    return jax.shard_map(
        body,
        mesh=mesh,
        in_specs=placed,
        out_specs=(
            P("dp", "seq", None),
            P("dp", "seq", None),
            P("dp", "seq"),
            P("dp", "seq"),
            P(),
            P("dp", "seq"),
            P(),
            P("dp", "seq"),
            P(),
            P("dp", "seq"),
            P(),
            P("dp", "seq"),
            P(),
        ),
        check_vma=False,
    )
```

```python
from functools import partial

import jax
import jax.numpy as jnp
from jax import lax
from jax.experimental import pallas as pl
from jax.experimental.pallas import tpu as pltpu
from jax.sharding import PartitionSpec as P

HEADS = 6
HEAD_DIM = 64
PAIR = 2 * HEAD_DIM
CORE_SWAP = ((0, 1), (1, 0))
CHUNK = 256
LANES = 128
GROUPS_PER_RANK = 2
GENERAL = False
PIECE_ROWS = 288
PLANE_STEPS = (3, 1, 2)
LINE_STEPS = (2, 3, 1)
F32 = jnp.float32
LOW = jnp.bfloat16


def nn(left, right):
    return lax.dot_general(left, right, (((1,), (0,)), ((), ())), preferred_element_type=F32)


def nt(left, right):
    return lax.dot_general(left, right, (((1,), (1,)), ((), ())), preferred_element_type=F32)


def tn(left, right):
    return lax.dot_general(left, right, (((0,), (0,)), ((), ())), preferred_element_type=F32)


def normalize(values):
    center = values - jnp.mean(values, axis=-1, keepdims=True)
    spread = jnp.mean(center * center, axis=-1, keepdims=True)
    inverse = lax.rsqrt(spread + 1e-06)
    return center * inverse, inverse


def norm_back(grad, normed, inverse):
    return inverse * (
        grad
        - jnp.mean(grad, axis=-1, keepdims=True)
        - normed * jnp.mean(grad * normed, axis=-1, keepdims=True)
    )


def column_sum(values):
    return jnp.sum(values, axis=0, keepdims=True)


def head_masks(rows):
    lane = lax.broadcasted_iota(jnp.int32, (rows, PAIR), 1)
    return lane < HEAD_DIM, lane >= HEAD_DIM


def masked(values, mask):
    return jnp.where(mask, values, jnp.zeros_like(values))


def fetch(pairs, sems):
    copies = []
    for index, (source, target) in enumerate(pairs):
        copy = pltpu.make_async_copy(source, target, sems.at[index])
        copy.start()
        copies.append(copy)
    return copies


def own_images(near_ref, far_ref, target_ref, first_image):
    half_len = near_ref.shape[1]
    pairs = []
    for image in range(target_ref.shape[0]):
        slot = first_image + image
        pairs.append((near_ref.at[slot], target_ref.at[image, pl.ds(0, half_len)]))
        pairs.append((far_ref.at[slot], target_ref.at[image, pl.ds(half_len, half_len)]))
    return pairs


def own_marks(mask_ref, counts_ref, core, image, image_count, half_len):
    slot = core * image_count + image
    live = jnp.where(slot < counts_ref[0], 1.0, 0.0)
    marks = mask_ref[pl.ds(slot, 1), :].astype(F32) * live
    low_marks, high_marks = marks[:, :half_len], marks[:, half_len:]
    return jnp.concatenate(
        [
            jnp.where(core == 0, low_marks, high_marks),
            jnp.where(core == 0, high_marks, low_marks),
        ],
        axis=1,
    )


def as_row(ref):
    return ref[...].astype(F32).reshape(1, ref.shape[0])


def load_kernel(
    tokens_hbm,
    tokens_far_ref,
    ids_hbm,
    counts_hbm,
    mask_hbm,
    qv_b_hbm,
    out_b_hbm,
    up_b_hbm,
    down_b_hbm,
    ada_w_hbm,
    ada_b_hbm,
    images_ref,
    penalty_ref,
    hot_ref,
    marks_ref,
    qkv_b_ref,
    out_b_ref,
    up_b_ref,
    down_b_ref,
    ada_w_ref,
    ada_b_ref,
    ids_ref,
    counts_ref,
    mask_ref,
    qv_b_ref,
    out_b_raw,
    up_b_raw,
    down_b_raw,
    ada_b_raw,
    sems,
):
    core = lax.axis_index("seq")
    image_count, length, width = images_ref.shape
    half_len = length // 2
    first_image = core * image_count
    copies = fetch(
        [
            (ids_hbm, ids_ref),
            (counts_hbm, counts_ref),
            (mask_hbm, mask_ref),
            (qv_b_hbm, qv_b_ref),
            (out_b_hbm, out_b_raw),
            (up_b_hbm, up_b_raw),
            (down_b_hbm, down_b_raw),
            (ada_b_hbm, ada_b_raw),
            (ada_w_hbm, ada_w_ref),
        ]
        + own_images(tokens_hbm, tokens_far_ref, images_ref, first_image),
        sems,
    )
    for copy in copies[:8]:
        copy.wait()
    row = lax.broadcasted_iota(jnp.int32, hot_ref.shape, 0)
    column = lax.broadcasted_iota(jnp.int32, hot_ref.shape, 1)
    lane = lax.broadcasted_iota(jnp.int32, marks_ref.shape, 1)
    hot = jnp.zeros(hot_ref.shape, F32)
    marks = jnp.zeros(marks_ref.shape, F32)
    for slot in range(2 * image_count):
        marks = jnp.where(lane == slot, ids_ref[slot].astype(F32), marks)
    marks_ref[...] = marks
    penalty_ref[...] = jnp.zeros_like(penalty_ref)
    for image in range(image_count):
        group = ids_ref[first_image + image]
        place = 8 * (group // GROUPS_PER_RANK) + group % GROUPS_PER_RANK
        hot = jnp.where((row == image) & (column == place), 1.0, hot)
        own = own_marks(mask_ref, counts_ref, core, image, image_count, half_len)
        penalty_ref[image : image + 1, :] = (own - 1.0) * 30000.0
    hot_ref[...] = hot.astype(LOW)
    qkv_b_ref[...] = jnp.concatenate(
        [qv_b_ref[0:1, :], jnp.zeros((1, width), LOW), qv_b_ref[1:2, :]], axis=1
    ).astype(F32)
    for raw, target in (
        (out_b_raw, out_b_ref),
        (up_b_raw, up_b_ref),
        (down_b_raw, down_b_ref),
        (ada_b_raw, ada_b_ref),
    ):
        target[...] = as_row(raw)
    for copy in copies[8:]:
        copy.wait()


def attention_pair(step, qkv_ref, penalty_ref, length, width):
    image, pair = divmod(step, HEADS // 2)
    rows = slice(image * length, (image + 1) * length)

    def lanes(which):
        start = which * width + pair * PAIR
        return slice(start, start + PAIR)

    queries = qkv_ref[rows, lanes(0)] * jnp.asarray(HEAD_DIM**-0.5, LOW)
    return rows, lanes, queries, qkv_ref[rows, lanes(1)], qkv_ref[rows, lanes(2)]


def image_rows(image, length):
    return slice(image * length, (image + 1) * length)


def mod_part(mod_ref, image, which, width):
    return mod_ref[image : image + 1, which * width : (which + 1) * width].astype(F32)


def wide_column(column_ref, rows, width):
    return jnp.concatenate([column_ref[rows, :]] * (width // LANES), axis=1)


def forward_kernel(
    lead_rows,
    cond_ref,
    images_ref,
    cot_far_ref,
    penalty_ref,
    hot_ref,
    qkv_b_ref,
    out_b_ref,
    up_b_ref,
    ada_w_ref,
    ada_b_ref,
    cot_hbm,
    qkv_w_hbm,
    out_w_hbm,
    up_w_hbm,
    down_w_hbm,
    qkv_ref,
    h1_ref,
    normed_ref,
    inverse_ref,
    mod_ref,
    lead_ref,
    logs_ref,
    att_ref,
    mid_ref,
    attn_ref,
    act_ref,
    gpre_ref,
    valid_ref,
    cot_ref,
    qkv_w_ref,
    out_w_ref,
    up_w_ref,
    down_w_ref,
    keep_ref,
    send_ref,
    small_ref,
    cond_rows_ref,
    turned_ref,
    h2_ref,
    gffn_ref,
    sems,
):
    core = lax.axis_index("seq")
    image_count, length, width = images_ref.shape
    half_len = length // 2
    half = width // 2
    ff_width = up_w_ref.shape[1]
    copies = fetch(
        [
            (qkv_w_hbm, qkv_w_ref),
            (out_w_hbm, out_w_ref),
            (up_w_hbm, up_w_ref),
            (down_w_hbm, down_w_ref),
        ]
        + own_images(cot_hbm, cot_far_ref, cot_ref, core * image_count),
        sems,
    )
    block_count, block_rows = cond_ref.shape[:2]
    cond_rows_ref[...] = jnp.zeros_like(cond_rows_ref)
    for block in range(block_count):
        start = 8 * (block_count - 1 - block)
        cond_rows_ref[start : start + block_rows, :] = cond_ref[block].astype(F32)
    cond = cond_rows_ref[...]
    silu = cond / (1.0 + jnp.exp(-cond))
    image_silu = nn(hot_ref[...], silu.astype(LOW)).astype(LOW)
    mod_ref[...] = (nn(image_silu, ada_w_ref[...]) + ada_b_ref[...]).astype(LOW)

    def part(image, which):
        return mod_part(mod_ref, image, which, width)

    copies[0].wait()
    for image in range(image_count):
        rows = image_rows(image, length)
        normed, inverse = normalize(images_ref[image].astype(F32))
        normed_ref[rows, :] = normed
        inverse_ref[rows, :] = jnp.broadcast_to(inverse, (length, LANES))
        marks = jnp.where(penalty_ref[image : image + 1, :] < 0.0, 0.0, 1.0)
        valid_ref[rows, :] = jnp.broadcast_to(marks, (LANES, length)).T
        h1 = (normed * (1.0 + part(image, 1)) + part(image, 0)).astype(LOW)
        h1_ref[rows, :] = h1
        qkv_ref[rows, :] = (nn(h1, qkv_w_ref[...]) + qkv_b_ref[...]).astype(LOW)

    first, second = head_masks(length)
    for step in range(image_count * (HEADS // 2)):
        rows, lanes, queries, keys, values = attention_pair(
            step, qkv_ref, penalty_ref, length, width
        )
        image = step // (HEADS // 2)
        penalty = penalty_ref[image : image + 1, :]
        total = jnp.zeros((length, PAIR), F32)
        for side, mask in enumerate((first, second)):
            scores = nt(masked(queries, mask), keys) + penalty
            top = jnp.max(scores, axis=-1, keepdims=True)
            exps = jnp.exp(scores - top)
            whole = jnp.sum(exps, axis=-1, keepdims=True)
            head = 2 * (step % (HEADS // 2)) + side
            logs_ref[rows, head * LANES : (head + 1) * LANES] = jnp.broadcast_to(
                top + jnp.log(whole), (length, LANES)
            )
            total = total + nn((exps / whole).astype(LOW), masked(values, mask))
        att_ref[rows, lanes(0)] = total.astype(LOW)

    for copy in copies[1:]:
        copy.wait()
    if lead_rows:
        turned_ref[...] = silu.T
        start = pl.multiple_of(lax.axis_index("dp") * lead_rows, 8)
        lead_ref[...] = turned_ref[pl.ds(start, lead_rows), :].astype(LOW)
    else:
        lead_ref[...] = jnp.zeros_like(lead_ref)
    small_ref[...] = jnp.zeros_like(small_ref)
    down_bias_grad = jnp.zeros((1, width), F32)
    for image in range(image_count):
        rows = image_rows(image, length)
        valid = wide_column(valid_ref, rows, width)
        attn = nn(att_ref[rows, :], out_w_ref[...]) + out_b_ref[...]
        attn_ref[rows, :] = attn
        middle = images_ref[image].astype(F32) + valid * part(image, 2) * attn
        mid_ref[rows, :] = middle
        normed, _ = normalize(middle)
        h2_ref[rows, :] = (normed * (1.0 + part(image, 4)) + part(image, 3)).astype(LOW)
        grad_ffn = (valid * part(image, 5) * cot_ref[image].astype(F32)).astype(LOW)
        gffn_ref[rows, :] = grad_ffn
        down_bias_grad = down_bias_grad + column_sum(grad_ffn.astype(F32))
    small_ref[13:14, :] = down_bias_grad

    for chunk in range(ff_width // CHUNK):
        columns = slice(chunk * CHUNK, (chunk + 1) * CHUNK)
        up_w = up_w_ref[:, columns]
        down_w = down_w_ref[columns, :]
        bias = jnp.zeros((1, CHUNK), F32)
        for image in range(image_count):
            rows = image_rows(image, length)
            pre = nn(h2_ref[rows, :], up_w) + up_b_ref[:, columns]
            square = pre * pre
            inner = jnp.tanh(pre * (0.7978845608028654 + 0.035677408136300125 * square))
            cdf = 0.5 * inner + 0.5
            act_ref[rows, columns] = (pre * cdf).astype(LOW)
            slope = 0.5 * (pre * (0.7978845608028654 + 0.10703222440890037 * square)) * (
                1.0 - inner * inner
            ) + cdf
            grad_pre = (nt(gffn_ref[rows, :], down_w) * slope).astype(LOW)
            gpre_ref[rows, columns] = grad_pre
            bias = bias + column_sum(grad_pre.astype(F32))
        for tile in range(CHUNK // LANES):
            start = chunk * CHUNK + tile * LANES
            small_ref[9 + start // width : 10 + start // width, start % width : start % width + LANES] = (
                bias[:, tile * LANES : (tile + 1) * LANES]
            )

    first_half = gffn_ref[:, :half]
    second_half = gffn_ref[:, half:]
    gffn_keep = jnp.where(core == 0, first_half, second_half)
    gffn_send = jnp.where(core == 0, second_half, first_half)
    side_chunks = ff_width // CHUNK // 2
    for step in range(side_chunks):
        low = slice(step * CHUNK, (step + 1) * CHUNK)
        high = slice((step + side_chunks) * CHUNK, (step + side_chunks + 1) * CHUNK)
        up_low = tn(h2_ref[...], gpre_ref[:, low])
        up_high = tn(h2_ref[...], gpre_ref[:, high])
        up_keep = jnp.where(core == 0, up_low, up_high)
        up_send = jnp.where(core == 0, up_high, up_low).astype(LOW)
        for tile in range(CHUNK // LANES):
            start = step * CHUNK + tile * LANES
            rows = slice(start // width * width, (start // width + 1) * width)
            columns = slice(start % width, start % width + LANES)
            keep_ref[rows, columns] = up_keep[:, tile * LANES : (tile + 1) * LANES]
            send_ref[rows, columns] = up_send[:, tile * LANES : (tile + 1) * LANES]
        rows = slice(2 * width + step * CHUNK, 2 * width + (step + 1) * CHUNK)
        for target, side in ((keep_ref, gffn_keep), (send_ref, gffn_send)):
            target[rows, :] = jnp.concatenate(
                [tn(act_ref[:, low], side), tn(act_ref[:, high], side)], axis=1
            ).astype(target.dtype)


def finish_forward_kernel(
    mod_ref,
    att_ref,
    mid_ref,
    attn_ref,
    act_ref,
    gpre_ref,
    valid_ref,
    cot_ref,
    out_w_ref,
    up_w_ref,
    down_w_ref,
    down_b_ref,
    early_ref,
    output_ref,
    grad_att_ref,
    grad_mid_ref,
    keep_ref,
    send_ref,
    small_ref,
    far_ref,
    gattn_ref,
):
    core = lax.axis_index("seq")
    image_count, length, width = cot_ref.shape
    half_len = length // 2
    half = width // 2
    small_ref[...] = early_ref[...]

    def part(image, which):
        return mod_part(mod_ref, image, which, width)

    out_bias_grad = jnp.zeros((1, width), F32)
    for image in range(image_count):
        rows = image_rows(image, length)
        valid = wide_column(valid_ref, rows, width)
        upstream = cot_ref[image].astype(F32)
        middle = mid_ref[rows, :]
        ffn = nn(act_ref[rows, :], down_w_ref[...]) + down_b_ref[...]
        output_ref[image] = (middle + valid * part(image, 5) * ffn).astype(LOW)
        small_ref[6 + image : 7 + image, :] = column_sum(valid * ffn * upstream)
        normed, inverse = normalize(middle)
        grad_h2 = nt(gpre_ref[rows, :], up_w_ref[...])
        small_ref[2 + image : 3 + image, :] = column_sum(grad_h2)
        small_ref[4 + image : 5 + image, :] = column_sum(grad_h2 * normed)
        grad_mid = upstream + norm_back(grad_h2 * (1.0 + part(image, 4)), normed, inverse)
        grad_mid_ref[rows, :] = grad_mid
        small_ref[image : image + 1, :] = column_sum(valid * attn_ref[rows, :] * grad_mid)
        grad_attn = (valid * part(image, 2) * grad_mid).astype(LOW)
        gattn_ref[rows, :] = grad_attn
        out_bias_grad = out_bias_grad + column_sum(grad_attn.astype(F32))
        grad_att_ref[rows, :] = nt(grad_attn, out_w_ref[...]).astype(LOW)
    small_ref[8:9, :] = out_bias_grad
    out_term = tn(att_ref[...], gattn_ref[...])
    out_first = jnp.concatenate([out_term[:half, :half], out_term[half:, :half]], axis=1)
    out_second = jnp.concatenate([out_term[:half, half:], out_term[half:, half:]], axis=1)
    keep_ref[...] = jnp.where(core == 0, out_first, out_second)
    send_ref[:half, :] = jnp.where(core == 0, out_second, out_first).astype(LOW)
    send_ref[half:, :] = small_ref[...].astype(LOW)
    for image in range(image_count):
        far_ref[image] = output_ref[image, half_len:, :]


def backward_kernel(
    normed_ref,
    inverse_ref,
    penalty_ref,
    logs_ref,
    qkv_w_ref,
    qkv_ref,
    h1_ref,
    grad_att_ref,
    grad_mid_ref,
    mod_ref,
    after_ref,
    after_too_ref,
    after_all_ref,
    grad_tokens_ref,
    keep_ref,
    send_ref,
    other_ref,
    small_ref,
    gqkv_ref,
):
    core = lax.axis_index("seq")
    image_count, length, width = grad_tokens_ref.shape
    half_len = length // 2
    half = width // 2
    first, second = head_masks(length)
    for step in range(image_count * (HEADS // 2)):
        rows, lanes, queries, keys, values = attention_pair(
            step, qkv_ref, penalty_ref, length, width
        )
        image = step // (HEADS // 2)
        penalty = penalty_ref[image : image + 1, :]
        grad_att = grad_att_ref[rows, lanes(0)]
        grad_q = jnp.zeros((length, PAIR), F32)
        grad_k = jnp.zeros((length, PAIR), F32)
        grad_v = jnp.zeros((length, PAIR), F32)
        for side, mask in enumerate((first, second)):
            own_queries = masked(queries, mask)
            own_grad = masked(grad_att, mask)
            head = 2 * (step % (HEADS // 2)) + side
            logs = logs_ref[rows, head * LANES : (head + 1) * LANES]
            logs = jnp.concatenate([logs] * (length // LANES), axis=1)
            probs = jnp.exp(nt(own_queries, keys) + penalty - logs)
            grad_probs = nt(own_grad, values)
            dots = jnp.sum(probs * grad_probs, axis=-1, keepdims=True)
            grad_scores = (probs * (grad_probs - dots)).astype(LOW)
            grad_v = grad_v + tn(probs.astype(LOW), own_grad)
            grad_q = grad_q + nn(grad_scores, masked(keys, mask))
            grad_k = grad_k + tn(grad_scores, own_queries)
        gqkv_ref[rows, lanes(0)] = (grad_q * HEAD_DIM**-0.5).astype(LOW)
        gqkv_ref[rows, lanes(1)] = grad_k.astype(LOW)
        gqkv_ref[rows, lanes(2)] = grad_v.astype(LOW)

    def part(image, which):
        return mod_ref[image : image + 1, which * width : (which + 1) * width].astype(F32)

    small_ref[...] = jnp.zeros_like(small_ref)
    small_ref[4:5, :] = column_sum(gqkv_ref[:, :width].astype(F32))
    small_ref[5:6, :] = column_sum(gqkv_ref[:, 2 * width :].astype(F32))
    for image in range(image_count):
        rows = slice(image * length, (image + 1) * length)
        normed = normed_ref[rows, :]
        inverse = jnp.concatenate([inverse_ref[rows, :]] * (width // LANES), axis=1)
        grad_h1 = nt(gqkv_ref[rows, :], qkv_w_ref[...])
        small_ref[image : image + 1, :] = column_sum(grad_h1)
        small_ref[2 + image : 3 + image, :] = column_sum(grad_h1 * normed)
        grad_in = norm_back(grad_h1 * (1.0 + part(image, 1)), normed, inverse)
        grad_tokens_ref[image] = (grad_mid_ref[rows, :] + grad_in).astype(LOW)
    low_term = tn(h1_ref[...], gqkv_ref[:, :width])
    high_term = tn(h1_ref[...], gqkv_ref[:, 2 * width :])
    keep_ref[:width, :] = jnp.where(core == 0, low_term, high_term)
    pair = jnp.where(core == 0, high_term, low_term).astype(LOW)
    term = tn(h1_ref[...], gqkv_ref[:, width : 2 * width])
    low_unit = jnp.concatenate([term[:half, :half], term[half:, :half]], axis=1)
    high_unit = jnp.concatenate([term[:half, half:], term[half:, half:]], axis=1)
    keep_ref[width:, :] = jnp.where(core == 0, low_unit, high_unit)
    cut = send_ref.shape[0] - half_len
    send_ref[:cut, :] = pair[:cut]
    start = width - cut
    other_ref[:start, :] = pair[cut:]
    other_ref[start : start + half, :] = jnp.where(core == 0, high_unit, low_unit).astype(LOW)
    start += half
    other_ref[start : start + 8, :] = small_ref[...].astype(LOW)
    for index, (target, start) in enumerate(((send_ref, cut), (other_ref, start + 8))):
        target[start:, :] = grad_tokens_ref[index, half_len:, :]


def by_core(core, near, far):
    return [jnp.where(core == 0, near, far), jnp.where(core == 0, far, near)]


def split_kernel(
    keep_ref,
    recv_ref,
    marks_ref,
    out_ref,
    own_up_ref,
    own_down_ref,
    send_up_ref,
    send_down_ref,
    send_out_ref,
):
    send_out_ref[...] = out_ref[...]
    width = keep_ref.shape[1]
    piece = width // 16
    long = 4 * piece
    block = 8 * piece
    plane = lax.axis_index("dp") & 3

    def move(target, start, size, to):
        rows = pl.ds(pl.multiple_of(start, 8), size)
        target[to : to + size, :] = (keep_ref[rows, :] + recv_ref[rows, :].astype(F32)).astype(
            target.dtype
        )

    for target, steps in ((own_up_ref, (0, 2)), (send_up_ref, (1, 3))):
        for index, step in enumerate(steps):
            who = plane ^ step
            for z in range(4):
                for side in range(2):
                    start = side * width + piece * (4 * z + who)
                    move(target, start, piece, index * block + (2 * z + side) * piece)
    for target, steps in ((own_down_ref, (0, 1)), (send_down_ref, (2, 3))):
        for index, step in enumerate(steps):
            who = plane ^ step
            for z in range(2):
                start = 2 * width + long * (4 * z + who)
                move(target, start, long, index * block + z * long)
    send_up_ref[2 * block :, :] = marks_ref[...].astype(LOW)


def cross_kernel(
    own_up_ref,
    own_down_ref,
    recv_up_ref,
    recv_down_ref,
    marks_ref,
    after_ref,
    kept_ref,
    send_up_ref,
    send_down_ref,
):
    block = own_up_ref.shape[0] // 2
    first, second = slice(0, block), slice(block, 2 * block)
    kept_ref[first, :] = own_up_ref[first, :] + recv_up_ref[first, :].astype(F32)
    kept_ref[second, :] = own_down_ref[first, :] + recv_down_ref[first, :].astype(F32)
    kept_ref[2 * block : 2 * block + 8, :] = marks_ref[...].astype(LOW).astype(F32)
    kept_ref[2 * block + 8 :, :] = recv_up_ref[2 * block :, :].astype(F32)
    send_up_ref[first, :] = (own_up_ref[second, :] + recv_up_ref[second, :].astype(F32)).astype(LOW)
    send_up_ref[block : block + 8, :] = marks_ref[...].astype(LOW)
    send_up_ref[block + 8 :, :] = recv_up_ref[2 * block :, :]
    send_down_ref[...] = (own_down_ref[second, :] + recv_down_ref[second, :].astype(F32)).astype(LOW)


def split_qkv_kernel(
    keep_ref, recv_ref, other_ref, small_ref, keep_out_ref, recv_out_ref, early_ref, *refs
):
    core = lax.axis_index("seq")
    width = keep_ref.shape[1]
    piece = width // 16
    half = width // 2
    cut = PIECE_ROWS
    start = keep_ref.shape[0] - cut
    near = small_ref[...].astype(LOW).astype(F32)
    far = other_ref[start : start + 8, :].astype(F32)
    first, second = by_core(core, near, far)
    near_early = early_ref[...].astype(LOW).astype(F32)
    far_early = recv_out_ref[half : half + 16, :].astype(F32)
    early, early_too = by_core(core, near_early, far_early)
    rows = []
    for kind in range(3):
        low_rows = [first, second] if kind < 2 else [early, early_too]
        low_start = 2 * kind if kind < 2 else 0
        low_rows = [block[low_start : low_start + 2] for block in low_rows]
        high_rows = [block[2 * kind + 2 : 2 * kind + 4] for block in (early, early_too)]
        rows.append(
            jnp.where(
                core == 0, jnp.concatenate(low_rows, axis=0), jnp.concatenate(high_rows, axis=0)
            )
        )
    rows += [early[8:14] + early_too[8:14], first[4:6] + second[4:6], jnp.zeros((4, width), F32)]
    small = jnp.concatenate(rows, axis=0).astype(LOW)
    total_ref = refs[-1]
    total_ref[:cut, :] = keep_ref[:cut, :] + recv_ref[:cut, :].astype(F32)
    total_ref[cut : width + half, :] = keep_ref[cut:, :] + other_ref[:start, :].astype(F32)
    total_ref[width + half :, :] = keep_out_ref[...] + recv_out_ref[:half, :].astype(F32)
    for step, target in zip((0,) + PLANE_STEPS, refs[-5:-1]):
        who = (lax.axis_index("dp") & 3) ^ step
        for z in range(8):
            begin = piece * (4 * z + who)
            if z >= 4:
                begin = width + (z - 4) // 2 * half + piece * (4 * (z % 2) + who)
            rows = pl.ds(pl.multiple_of(begin, 8), piece)
            target[piece * z : piece * (z + 1), :] = total_ref[rows, :].astype(target.dtype)
        target[8 * piece :, :] = small.astype(target.dtype)


def summed(sources, rows):
    return sum((source[rows, :].astype(F32) for source in sources[1:]), sources[0][rows, :])


def fold_kernel(*refs):
    kept_ref, up_ref, down_ref = refs[:3]
    rest_ref, rest_small_ref = refs[4:6]
    sends = refs[6:9]
    total_ref, group_ref = refs[9:]
    width = total_ref.shape[1]
    piece = width // 16
    long = 4 * piece
    half = width // 2
    block = 8 * piece
    total_ref[:block, :] = kept_ref[:block, :] + up_ref[:block, :].astype(F32)
    total_ref[block:, :] = kept_ref[block : 2 * block, :] + down_ref[...].astype(F32)
    plane = lax.axis_index("dp") & 3
    for index in range(2):
        start = 2 * block + 8 * index
        group_ref[plane ^ index] = kept_ref[start : start + 8, :]
        start = block + 8 * index
        group_ref[plane ^ (2 + index)] = up_ref[start : start + 8, :].astype(F32)
    ids = [group_ref[q, 0:1] for q in range(4)] + [jnp.zeros((4, width), F32)]
    small = jnp.concatenate(ids, axis=0).astype(LOW)
    rest_small_ref[...] = small
    for step, target in zip((0,) + LINE_STEPS, (rest_ref,) + tuple(sends)):
        who = (lax.axis_index("dp") >> 2) ^ step
        rows = pl.ds(pl.multiple_of(2 * piece * who, 8), 2 * piece)
        target[: 2 * piece, :] = total_ref[rows, :].astype(target.dtype)
        rows = pl.ds(pl.multiple_of(8 * piece + long * (who % 2), 8), long)
        down = total_ref[rows, :]
        down = jnp.where(who < 2, down[:, :half], down[:, half:])
        down = jnp.concatenate([down[: 2 * piece], down[2 * piece :]], axis=1)
        target[2 * piece : 4 * piece, :] = down.astype(target.dtype)
        if step:
            target[4 * piece :, :] = small


def fold_qkv_kernel(*refs):
    parts = refs[:4]
    rest_ref, rest_small_ref = refs[4:6]
    sends = refs[6:9]
    total_ref, late_ref = refs[9:]
    width = total_ref.shape[1]
    piece = width // 16
    half = width // 2
    total_ref[...] = summed(parts, slice(0, 8 * piece))
    for step, part in zip((0,) + PLANE_STEPS, parts):
        late_ref[(lax.axis_index("dp") & 3) ^ step] = part[8 * piece :, :].astype(F32)
    rows = [late_ref[q, :12] for q in range(4)]
    rows.append(late_ref[0, 12:20] + late_ref[1, 12:20] + late_ref[2, 12:20] + late_ref[3, 12:20])
    small = jnp.concatenate(rows, axis=0).astype(LOW)
    rest_small_ref[...] = small
    for step, target in zip((0,) + LINE_STEPS, (rest_ref,) + tuple(sends)):
        who = (lax.axis_index("dp") >> 2) ^ step

        def side(start):
            value = total_ref[pl.ds(pl.multiple_of(piece * (start + who % 2), 8), piece), :]
            return jnp.where(who < 2, value[:, :half], value[:, half:])

        target[:piece, :] = jnp.concatenate([side(6), side(4)], axis=1).astype(target.dtype)
        pair = total_ref[pl.ds(pl.multiple_of(piece * who, 8), piece), :]
        target[piece : 2 * piece, :] = pair.astype(target.dtype)
        if step:
            target[2 * piece :, :] = small


def one_hot(ids, lead):
    place = lax.broadcasted_iota(jnp.int32, (lead.shape[1], ids.shape[1]), 0)
    wanted = (ids // GROUPS_PER_RANK) * 8 + ids % GROUPS_PER_RANK
    return jnp.where(place == wanted, 1.0, 0.0).astype(LOW)


def group_rows(own_groups, kinds, kind_of):
    zeros = jnp.zeros_like(kind_of, F32)
    rows = []
    for kind in kinds:
        for one in own_groups:
            rows.append(jnp.where((kind_of == kind) & one, 1.0, zeros))
    for kind in kinds:
        rows.append(jnp.where(kind_of == kind, 1.0, zeros))
    while len(rows) % 8:
        rows.append(zeros)
    return jnp.concatenate(rows, axis=0).astype(LOW)


def split_dot(values, weight):
    high = values.astype(LOW)
    low = (values - high.astype(F32)).astype(LOW)
    both = nt(jnp.concatenate([high.astype(F32), low.astype(F32)], axis=0).astype(LOW), weight)
    return both[: values.shape[0]] + both[values.shape[0] :]


def finish_kernel(
    own_ref,
    own_small_ref,
    one_ref,
    two_ref,
    three_ref,
    lead_ref,
    recv_far_ref,
    recv_two_ref,
    recv_other_ref,
    output_ref,
    grad_tokens_ref,
    output_to,
    grad_tokens_to,
    up_ref,
    down_ref,
    silu_ref,
    ids_ref,
    stack_ref,
    sems,
):
    core = lax.axis_index("seq")
    width = own_ref.shape[1]
    piece = width // 16
    half = width // 2
    slots, half_len = output_to.shape[:2]
    count = slots // 2
    pairs = []
    for index in range(count):
        slot = (1 - core) * count + index
        source = (recv_two_ref, recv_other_ref)[index]
        pairs.append((recv_far_ref.at[index], output_to.at[slot]))
        start = source.shape[0] - half_len
        pairs.append((source.at[pl.ds(start, half_len)], grad_tokens_to.at[slot]))
        slot = core * count + index
        pairs.append((output_ref.at[index, pl.ds(0, half_len)], output_to.at[slot]))
        pairs.append((grad_tokens_ref.at[index, pl.ds(0, half_len)], grad_tokens_to.at[slot]))
    copies = fetch(pairs, sems)
    parts = (own_ref, one_ref, two_ref, three_ref)
    total = summed(parts, slice(0, 4 * piece))
    up_ref[...] = jnp.concatenate([total[:piece], total[piece : 2 * piece]], axis=1)
    down = total[2 * piece :]
    down_ref[...] = jnp.concatenate([down[:, :half], down[:, half:]], axis=0)
    line = lax.axis_index("dp") >> 2
    smalls = (own_small_ref[...],) + tuple(part[4 * piece :, :] for part in parts[1:])
    for step, small in zip((0,) + LINE_STEPS, smalls):
        stack_ref[line ^ step] = small[:, :LANES].astype(F32)
    stack = stack_ref[...].reshape(32, LANES).astype(LOW)
    count = 192
    row = lax.broadcasted_iota(jnp.int32, (32, count), 0)
    chip = lax.broadcasted_iota(jnp.int32, (32, count), 1) // 12
    spread = tn(stack, jnp.where(row == chip + 4 * (chip // 4), 1.0, 0.0).astype(LOW))[:8]
    slot = lax.broadcasted_iota(jnp.int32, (8, count), 0)
    wanted = lax.broadcasted_iota(jnp.int32, (8, count), 1) % 4
    ids = column_sum(jnp.where(slot == wanted, spread, 0.0)).astype(jnp.int32)
    ids_ref[...] = ids
    lead = lead_ref[...]
    silu_ref[...] = nn(lead, one_hot(ids, lead)).astype(LOW)
    for copy in copies:
        copy.wait()


def late_kernel(
    own_small_ref,
    one_ref,
    two_ref,
    three_ref,
    ids_ref,
    ada_ref,
    stack_out_ref,
    own_sums_ref,
    send_ref,
    out_bias_ref,
    up_bias_ref,
    down_bias_ref,
    qv_ref,
    bias_ref,
):
    core = lax.axis_index("seq")
    width = own_small_ref.shape[1]
    piece = width // 16
    half = width // 2
    line = lax.axis_index("dp") >> 2
    smalls = (own_small_ref[...],) + tuple(
        part[2 * piece :, :] for part in (one_ref, two_ref, three_ref)
    )
    for step, small in zip((0,) + LINE_STEPS, smalls):
        stack_out_ref[line ^ step] = small[:48]
        bias_ref[line ^ step] = small[48:].astype(F32)
    stack = stack_out_ref[...].reshape(192, width)
    ids = ids_ref[...]
    item = lax.broadcasted_iota(jnp.int32, (1, 192), 1) % 12
    base = GROUPS_PER_RANK * lax.axis_index("dp")
    own = [ids == base + index for index in range(GROUPS_PER_RANK)]
    sums = nn(group_rows(own, range(3), item // 4), stack)
    weight = ada_ref[:, pl.ds(pl.multiple_of(core * 3 * width, LANES), 3 * width)]
    own_sum = jnp.concatenate(
        [
            jnp.concatenate([sums[2 * kind : 2 * kind + 2] for kind in range(3)], axis=1),
            jnp.zeros((6, 3 * width), F32),
        ],
        axis=0,
    )
    cond = split_dot(own_sum, weight)
    low_cond, high_cond = cond[:2, :half], cond[:2, half:]
    kept = jnp.where(core == 0, low_cond, high_cond)
    sent = jnp.where(core == 0, high_cond, low_cond)
    zeros = jnp.zeros((2, half), F32)
    pad = jnp.zeros((3, width), F32)
    own_sums_ref[...] = jnp.concatenate(
        [jnp.concatenate([kept, zeros], axis=1), sums[6:9], pad], axis=0
    )
    send_ref[...] = jnp.concatenate(
        [jnp.concatenate([sent, zeros], axis=1), sums[6:9], pad], axis=0
    )
    bias = bias_ref[0] + bias_ref[1] + bias_ref[2] + bias_ref[3]
    out_bias_ref[...] = bias[0:1].reshape(width)
    up_bias_ref[...] = jnp.concatenate([bias[1 + row : 2 + row] for row in range(4)], axis=1).reshape(
        4 * width
    )
    down_bias_ref[...] = bias[5:6].reshape(width)
    qv_ref[...] = bias[6:8]


def rest_kernel(
    own_ref, one_ref, two_ref, three_ref, stack_ref, silu_ref, after_ref, out_ref, qkv_ref, ada_out_ref
):
    core = lax.axis_index("seq")
    width = own_ref.shape[1]
    piece = width // 16
    half = width // 2
    total = summed((own_ref, one_ref, two_ref, three_ref), slice(0, 2 * piece))
    out_ref[...] = total[:piece, :half]
    unit, pair = total[:piece, half:], total[piece:]
    qkv_ref[...] = jnp.where(
        core == 0,
        jnp.concatenate([pair, unit], axis=1),
        jnp.concatenate([unit, pair], axis=1),
    )
    stack = stack_ref[...].reshape(192, width)
    kind_of = lax.broadcasted_iota(jnp.int32, (1, 192), 1) % 12 // 4
    for kind in range(3):
        ada_out_ref[:, kind * width : (kind + 1) * width] = nn(
            masked(silu_ref[...], kind_of == kind), stack
        )


def final_kernel(own_ref, recv_ref, own_cond_ref, cond_ref, bias_ref):
    core = lax.axis_index("seq")
    width = own_ref.shape[1]
    half = width // 2
    near, far = own_ref[...], recv_ref[...]
    values = own_cond_ref[...].astype(F32)
    values = jnp.where(core == 0, values[:, :half], values[:, half:])
    gate = 1.0 / (1.0 + jnp.exp(-values))
    cond_ref[...] = (near[:2, :half] + far[:2, :half]) * (gate * (1.0 + values * (1.0 - gate)))
    rows = [block[row : row + 1] for block in by_core(core, near, far) for row in range(2, 5)]
    bias_ref[...] = jnp.concatenate(rows, axis=1).reshape(6 * width)


def silu_slope(values):
    sigmoid_val = jax.nn.sigmoid(values)
    return sigmoid_val * (1.0 + values * (1.0 - sigmoid_val))


def swap_cores(values):
    return lax.ppermute(values, "seq", CORE_SWAP)


def pick(core, first, second):
    return jnp.where(core == 0, first, second)


def to_patches(images, far, core):
    half_len = images.shape[1] // 2
    return pick(
        core,
        jnp.concatenate([images[:, :half_len], far], axis=0),
        jnp.concatenate([far, images[:, :half_len]], axis=0),
    )


def call(kernel, name, shapes, scratch, limit, spaces, *operands, aliases=None):
    chosen = {
        "s": pl.BlockSpec(memory_space=pltpu.SMEM),
        "v": pl.BlockSpec(memory_space=pltpu.VMEM),
        "V": pl.BlockSpec(memory_space=pltpu.VMEM),
        "a": pl.BlockSpec(memory_space=pl.ANY),
        "h": pl.BlockSpec(memory_space=pltpu.HBM),
    }
    pinned = {"h": pltpu.HBM, "V": pltpu.VMEM}
    into, out_of = spaces
    operands = [
        pltpu.with_memory_space_constraint(item, pinned[kind]) if kind in pinned else item
        for kind, item in zip(into, operands)
    ]
    return pl.pallas_call(
        kernel,
        out_shape=tuple(
            pinned.get(kind, jax.ShapeDtypeStruct)(shape, dtype)
            for kind, (shape, dtype) in zip(out_of, shapes)
        ),
        in_specs=[chosen[kind] for kind in into],
        out_specs=[chosen[kind] for kind in out_of],
        scratch_shapes=scratch,
        compiler_params=pltpu.CompilerParams(vmem_limit_bytes=limit << 20),
        cost_estimate=pl.CostEstimate(flops=1, bytes_accessed=1, transcendentals=0),
        input_output_aliases=aliases or {},
        name=name,
    )(*operands)


def rank_swap(values, step, count):
    return lax.ppermute(values, "dp", [(rank, rank ^ step) for rank in range(count)])


def owner_total(term, dp_count):
    blocks = term.astype(LOW).reshape(dp_count, term.shape[0] // dp_count, term.shape[1])
    return jnp.sum(lax.all_to_all(blocks, "dp", 0, 0, tiled=True).astype(F32), axis=0)


def general_tail(
    core, dp_count, dp_rank, sides, smalls, heads, cond_rows, cond, own_ids, ada_weight
):
    highest = lax.Precision.HIGHEST
    width, mod_width = ada_weight.shape
    half = width // 2
    (keep_one, send_one), (keep_out, send_out), (keep_two, send_two, send_other) = sides
    output, output_far, grad_tokens = heads
    output_far = swap_cores(output_far)
    small_one, small_two = smalls
    half_len = output.shape[1] // 2
    recv_out = swap_cores(send_out)
    first_sum = jnp.concatenate(
        [
            keep_one + swap_cores(send_one).astype(F32),
            keep_out + recv_out[:half].astype(F32),
        ],
        axis=0,
    )
    recv_two, recv_other = swap_cores(send_two), swap_cores(send_other)
    second_sum = keep_two + jnp.concatenate(
        [recv_two[:PIECE_ROWS], recv_other[: keep_two.shape[0] - PIECE_ROWS]], axis=0
    ).astype(F32)
    grad_far = jnp.stack([item[-half_len:] for item in (recv_two, recv_other)])
    ff_half = first_sum.shape[0] - 2 * width - half
    up = jnp.concatenate([first_sum[:width], first_sum[width : 2 * width]], axis=1)
    down = first_sum[2 * width : 2 * width + ff_half]
    down = jnp.concatenate([down[:, :half], down[:, half:]], axis=0)
    out = first_sum[2 * width + ff_half :]
    out = jnp.concatenate([out[:, :half], out[:, half:]], axis=0)
    pair, unit = second_sum[:width], second_sum[width:]
    unit = jnp.concatenate([unit[:, :half], unit[:, half:]], axis=0)
    qkv = pick(
        core, jnp.concatenate([pair, unit], axis=1), jnp.concatenate([unit, pair], axis=1)
    )
    sums = [owner_total(term, dp_count) for term in (qkv, out, up, down)]
    image_grad = jnp.concatenate(
        [small_two[0:2], small_two[2:4], small_one[0:2], small_one[2:4], small_one[4:6], small_one[6:8]],
        axis=1,
    )
    biases = jnp.concatenate([small_two[4:6], small_one[8:14]], axis=0)
    marks = jnp.broadcast_to(own_ids.astype(F32)[:, None], (own_ids.shape[0], width))
    packed = jnp.concatenate([image_grad.reshape(-1, width), biases, marks], axis=0)
    gathered = lax.all_to_all(
        jnp.broadcast_to(packed[None], (2 * dp_count,) + packed.shape),
        ("dp", "seq"),
        0,
        0,
        tiled=True,
    )
    grad_rows = gathered[:, :12].reshape(-1, mod_width)
    bias_sums = jnp.sum(gathered[:, 12:20], axis=0)
    all_ids = gathered[:, 20:, 0].reshape(-1).astype(jnp.int32)
    group_count = cond_rows.shape[0]
    all_hot = (all_ids[:, None] == jnp.arange(group_count, dtype=jnp.int32)[None, :]).astype(F32)
    group_grad = jnp.dot(all_hot.T, grad_rows, precision=highest)
    own_rows = width // dp_count
    silu_rows = lax.reduce_precision(jax.nn.silu(cond_rows.astype(F32)), 8, 7)
    silu_part = lax.dynamic_slice_in_dim(silu_rows, dp_rank * own_rows, own_rows, 1)
    grad_half = pick(core, group_grad[:, : mod_width // 2], group_grad[:, mod_width // 2 :])
    ada_sum = jnp.dot(silu_part.T, grad_half, precision=highest)
    own_grad = lax.dynamic_slice_in_dim(
        group_grad, dp_rank * GROUPS_PER_RANK, GROUPS_PER_RANK, 0
    )
    ada_half = lax.dynamic_slice_in_dim(ada_weight, core * half, half, 0).astype(F32)
    cond_half = pick(core, cond[:, :half], cond[:, half:]).astype(F32)
    grad_cond = silu_slope(cond_half) * jnp.dot(own_grad, ada_half.T, precision=highest)
    return (
        to_patches(output, output_far, core),
        to_patches(grad_tokens, grad_far, core),
        grad_cond,
        sums[0],
        bias_sums[:2],
        sums[1],
        bias_sums[2],
        sums[2],
        bias_sums[3:7].reshape(-1),
        sums[3],
        bias_sums[7],
        ada_sum,
        jnp.sum(grad_rows, axis=0),
    )


def body(
    tokens,
    cotangent,
    cond,
    group_ids,
    image_counts,
    patch_mask,
    qkv_weight,
    qv_bias,
    out_weight,
    out_bias,
    up_weight,
    up_bias,
    down_weight,
    down_bias,
    ada_weight,
    ada_bias,
):
    slot_count, half_len, width = tokens.shape
    ff_width = up_weight.shape[1]
    mod_width = ada_weight.shape[1]
    dp_count = lax.axis_size("dp")
    core = lax.axis_index("seq").astype(jnp.int32)
    dp_rank = lax.axis_index("dp").astype(jnp.int32)
    image_count = slot_count // 2
    length = 2 * half_len
    row_count = image_count * length
    half = width // 2
    piece = width // dp_count
    fast = dp_count == 16 and not GENERAL
    cond_blocks = lax.all_to_all(
        jnp.broadcast_to(cond[None], (dp_count,) + cond.shape),
        "dp",
        0,
        0,
        axis_index_groups=[list(range(dp_count))[::-1]],
        tiled=True,
    )
    tokens_far = swap_cores(tokens)
    cot_far = swap_cores(cotangent)
    image_shape = (image_count, length, width)
    half_shape = (image_count, half_len, width)
    vmem = pltpu.VMEM
    (
        images,
        penalty,
        hot,
        marks,
        qkv_b_row,
        out_b_row,
        up_b_row,
        down_b_row,
        ada_weight_near,
        ada_b_row,
    ) = call(
        load_kernel,
        "load",
        (
            (image_shape, LOW),
            ((8, length), F32),
            ((8, 8 * dp_count), LOW),
            ((8, width), F32),
            ((1, 3 * width), F32),
            ((1, width), F32),
            ((1, ff_width), F32),
            ((1, width), F32),
            (ada_weight.shape, LOW),
            ((1, mod_width), F32),
        ),
        [
            pltpu.SMEM(group_ids.shape, jnp.int32),
            pltpu.SMEM(image_counts.shape, jnp.int32),
            vmem(patch_mask.shape, jnp.int32),
            vmem(qv_bias.shape, LOW),
            vmem(out_bias.shape, LOW),
            vmem(up_bias.shape, LOW),
            vmem(down_bias.shape, LOW),
            vmem(ada_bias.shape, LOW),
            pltpu.SemaphoreType.DMA((9 + 2 * image_count,)),
        ],
        12,
        ("hVha" + "h" * 7, "V" * 10),
        tokens,
        tokens_far,
        group_ids,
        image_counts,
        patch_mask,
        qv_bias,
        out_bias,
        up_bias,
        down_bias,
        ada_weight,
        ada_bias,
    )
    (
        qkv,
        h1,
        normed,
        inverse,
        image_mod,
        lead,
        logs,
        att,
        middle,
        attn,
        act,
        grad_pre,
        valid,
        cot_images,
        qkv_weight_near,
        out_weight_near,
        up_weight_near,
        down_weight_near,
        keep_one,
        send_one,
        small_early,
    ) = call(
        partial(forward_kernel, piece if fast else 0),
        "forward_and_ffn_grads",
        (
            ((row_count, 3 * width), LOW),
            ((row_count, width), LOW),
            ((row_count, width), F32),
            ((row_count, LANES), F32),
            ((8, mod_width), LOW),
            ((24, 8 * dp_count), LOW),
            ((row_count, HEADS * LANES), F32),
            ((row_count, width), LOW),
            ((row_count, width), F32),
            ((row_count, width), F32),
            ((row_count, ff_width), LOW),
            ((row_count, ff_width), LOW),
            ((row_count, LANES), F32),
            (image_shape, LOW),
            (qkv_weight.shape, LOW),
            (out_weight.shape, LOW),
            (up_weight.shape, LOW),
            (down_weight.shape, LOW),
            ((2 * width + ff_width // 2, width), F32),
            ((2 * width + ff_width // 2, width), LOW),
            ((16, width), F32),
        ),
        [
            vmem((8 * dp_count, width), F32),
            vmem((width, 8 * dp_count), F32),
            vmem((row_count, width), LOW),
            vmem((row_count, width), LOW),
            pltpu.SemaphoreType.DMA((4 + 2 * image_count,)),
        ],
        24,
        ("V" * 10 + "h" * 5, "V" * 21),
        cond_blocks,
        images,
        cot_far,
        penalty,
        hot,
        qkv_b_row,
        out_b_row,
        up_b_row,
        ada_weight_near,
        ada_b_row,
        cotangent,
        qkv_weight,
        out_weight,
        up_weight,
        down_weight,
    )
    output, grad_att, grad_mid, keep_out, send_out, small_one, output_far = call(
        finish_forward_kernel,
        "norm_back",
        (
            (image_shape, LOW),
            ((row_count, width), LOW),
            ((row_count, width), F32),
            ((half, width), F32),
            ((half + 16, width), LOW),
            ((16, width), F32),
            (half_shape, LOW),
        ),
        [vmem((row_count, width), LOW)],
        16,
        ("V" * 13, "V" * 7),
        image_mod,
        att,
        middle,
        attn,
        act,
        grad_pre,
        valid,
        cot_images,
        out_weight_near,
        up_weight_near,
        down_weight_near,
        down_b_row,
        small_early,
    )

    def attention_back(*after):
        return call(
            backward_kernel,
            "attention_back",
            (
                (image_shape, LOW),
                ((width + half, width), F32),
                ((PIECE_ROWS + half_len, width), LOW),
                ((width + half + 8 - PIECE_ROWS + half_len, width), LOW),
                ((8, width), F32),
            ),
            [vmem((row_count, 3 * width), LOW)],
            24,
            ("V" * 10 + "aaa", "VVVVV"),
            normed,
            inverse,
            penalty,
            logs,
            qkv_weight_near,
            qkv,
            h1,
            grad_att,
            grad_mid,
            image_mod,
            *after,
        )

    if not fast:
        grad_tokens, keep_two, send_two, send_other, small_two = attention_back(
            small_one, keep_one, keep_out
        )
        own_ids = lax.dynamic_slice_in_dim(group_ids, core * image_count, image_count, 0)
        return general_tail(
            core,
            dp_count,
            dp_rank,
            ((keep_one, send_one), (keep_out, send_out), (keep_two, send_two, send_other)),
            (small_one, small_two),
            (output, output_far, grad_tokens),
            cond_blocks[::-1].reshape(-1, width),
            cond,
            own_ids,
            ada_weight,
        )

    recv_one = swap_cores(send_one)
    block_rows = 8 * piece
    own_up, own_down, sent_up, sent_down, sent_out = call(
        split_kernel,
        "split_plane",
        (
            ((2 * block_rows, width), F32),
            ((2 * block_rows, width), F32),
            ((2 * block_rows + 8, width), LOW),
            ((2 * block_rows, width), LOW),
            ((half + 16, width), LOW),
        ),
        [],
        16,
        ("VVVV", "VVVVV"),
        keep_one,
        recv_one,
        marks,
        send_out,
    )
    recv_out = swap_cores(sent_out)
    near_up, near_down = rank_swap(sent_up, 1, 16), rank_swap(sent_down, 2, 16)
    grad_tokens, keep_two, send_two, send_other, small_two = attention_back(
        sent_up, sent_down, recv_out
    )
    kept, cross_up, cross_down = call(
        cross_kernel,
        "cross_plane",
        (
            ((2 * block_rows + 16, width), F32),
            ((block_rows + 16, width), LOW),
            ((block_rows, width), LOW),
        ),
        [],
        16,
        ("VVVVVa", "VVV"),
        own_up,
        own_down,
        near_up,
        near_down,
        marks,
        small_two,
    )
    near_up, near_down = rank_swap(cross_up, 2, 16), rank_swap(cross_down, 1, 16)
    recv_two, recv_other = swap_cores(send_two), swap_cores(send_other)
    recv_far = swap_cores(output_far)
    split_rows = 8 * piece + 24
    own_qkv, *sent_qkv = call(
        split_qkv_kernel,
        "split_qkv_plane",
        (((split_rows, width), F32),) + (((split_rows, width), LOW),) * 3,
        [vmem((2 * width, width), F32)],
        16,
        ("VVVVVVVaa", "VVVV"),
        keep_two,
        recv_two,
        recv_other,
        small_two,
        keep_out,
        recv_out,
        small_one,
        cross_up,
        recv_far,
    )
    near_qkv = [rank_swap(item, step, 16) for step, item in zip(PLANE_STEPS, sent_qkv)]
    line_rows = 4 * piece + 8
    rest, rest_ids, *lines = call(
        fold_kernel,
        "fold_plane",
        (((4 * piece, width), F32), ((8, width), LOW)) + (((line_rows, width), LOW),) * 3,
        [vmem((16 * piece, width), F32), vmem((4, 8, width), F32)],
        16,
        ("VVVa", "VVVVV"),
        kept,
        near_up,
        near_down,
        sent_qkv[2],
    )
    lines = [rank_swap(item, 4 * step, 16) for step, item in zip(LINE_STEPS, lines)]
    line_rows = 2 * piece + 56
    rest_qkv, rest_small, *lines_qkv = call(
        fold_qkv_kernel,
        "fold_qkv_plane",
        (((2 * piece, width), F32), ((56, width), LOW)) + (((line_rows, width), LOW),) * 3,
        [vmem((8 * piece, width), F32), vmem((4, 24, width), F32)],
        16,
        ("VVVV", "VVVVV"),
        own_qkv,
        *near_qkv,
    )
    lines_qkv = [rank_swap(item, 4 * step, 16) for step, item in zip(LINE_STEPS, lines_qkv)]
    output, grad_tokens, up_sum, down_sum, silu_rows, all_ids = call(
        finish_kernel,
        "finish_line",
        (
            (tokens.shape, LOW),
            (tokens.shape, LOW),
            ((piece, ff_width // 2), F32),
            ((4 * piece, half), F32),
            ((piece, 192), LOW),
            ((1, 192), jnp.int32),
        ),
        [vmem((4, 8, LANES), F32), pltpu.SemaphoreType.DMA((4 * image_count,))],
        16,
        ("V" * 11, "hhvvVV"),
        rest,
        rest_ids,
        *lines,
        lead,
        recv_far,
        recv_two,
        recv_other,
        output,
        grad_tokens,
    )
    (
        stack,
        own_sums,
        send_sums,
        out_bias_sum,
        up_bias_sum,
        down_bias_sum,
        qv_sum,
    ) = call(
        late_kernel,
        "late_groups",
        (
            ((4, 48, width), LOW),
            ((8, width), F32),
            ((8, width), F32),
            ((width,), F32),
            ((ff_width,), F32),
            ((width,), F32),
            ((2, width), F32),
        ),
        [vmem((4, 8, width), F32)],
        16,
        ("V" * 6, "VVVvvvv"),
        rest_small,
        *lines_qkv,
        all_ids,
        ada_weight_near,
    )
    out_sum, qkv_sum, ada_sum = call(
        rest_kernel,
        "rest_sums",
        (((piece, half), F32), ((piece, 3 * half), F32), ((piece, mod_width // 2), F32)),
        [],
        16,
        ("VVVVVVa", "vvv"),
        rest_qkv,
        *lines_qkv,
        stack,
        silu_rows,
        send_sums,
    )
    grad_cond, ada_bias_sum = call(
        final_kernel,
        "final_groups",
        (((GROUPS_PER_RANK, half), F32), ((mod_width,), F32)),
        [],
        16,
        ("VVv", "vv"),
        own_sums,
        swap_cores(send_sums),
        cond,
    )
    return (
        output,
        grad_tokens,
        grad_cond,
        qkv_sum,
        qv_sum,
        out_sum,
        out_bias_sum,
        up_sum,
        up_bias_sum,
        down_sum,
        down_bias_sum,
        ada_sum,
        ada_bias_sum,
    )


def solution(mesh):
    placed = (
        P("dp", "seq", None),
        P("dp", "seq", None),
        P("dp", None),
        P("dp"),
        P("dp"),
        P("dp", None),
        P(),
        P(),
        P(),
        P(),
        P(),
        P(),
        P(),
        P(),
        P(),
        P(),
    )
    return jax.shard_map(
        body,
        mesh=mesh,
        in_specs=placed,
        out_specs=(
            P("dp", "seq", None),
            P("dp", "seq", None),
            P("dp", "seq"),
            P("dp", "seq"),
            P(),
            P("dp", "seq"),
            P(),
            P("dp", "seq"),
            P(),
            P("dp", "seq"),
            P(),
            P("dp", "seq"),
            P(),
        ),
        check_vma=False,
    )
```
